32 devices in a mesh: ctx: 2 (over y), uly: 4 (over x, core), tp: 4 (over z).
Axes of the slice: x: 2, y: 2, z: 4, core: 2. Of those that a mesh axis runs over, the one named last changes fastest.
Arguments:
- inputs: bfloat16 [2, 4096, 2048], P(None, ('ctx', 'uly', 'tp')), may hold values from -6 to 6
- doc_ids: int32 [2, 4096], replicated, may hold values from -1 to 3, as said below
- attn_norm: float32 [2048], replicated, may hold values from 0.5 to 1.5
- w_query: bfloat16 [2048, 2048], P(None, 'tp'), may hold values from -0.125 to 0.125
- w_key: bfloat16 [2048, 1024], P(None, 'tp'), may hold values from -0.125 to 0.125
- w_value: bfloat16 [2048, 1024], P(None, 'tp'), may hold values from -0.125 to 0.125
- w_headgate: bfloat16 [2048, 16], P(None, 'tp'), may hold values from -0.125 to 0.125
- query_norm: float32 [128], replicated, may hold values from 0.5 to 1.5
- key_norm: float32 [128], replicated, may hold values from 0.5 to 1.5
- w_output: bfloat16 [2048, 2048], P('tp'), may hold values from -0.5 to 0.5
- mlp_norm: float32 [2048], replicated, may hold values from 0.5 to 1.5
- w_gate: bfloat16 [2048, 6144], P(None, 'tp'), may hold values from -0.125 to 0.125
- w_up: bfloat16 [2048, 6144], P(None, 'tp'), may hold values from -0.125 to 0.125
- w_down: bfloat16 [6144, 2048], P('tp'), may hold values from -0.15625 to 0.15625
- cotangent: bfloat16 [2, 4096, 2048], P(None, ('ctx', 'uly', 'tp')), may hold values from -6 to 6
Outputs:
- outputs: bfloat16 [2, 4096, 2048], P(None, ('ctx', 'uly', 'tp'))
- grad_inputs: float32 [2, 4096, 2048], P(None, ('ctx', 'uly', 'tp'))
- grad_attn_norm: float32 [2048], replicated
- grad_query: float32 [2048, 2048], P(('ctx', 'uly'), 'tp')
- grad_key: float32 [2048, 1024], P(('ctx', 'uly'), 'tp')
- grad_value: float32 [2048, 1024], P(('ctx', 'uly'), 'tp')
- grad_headgate: float32 [2048, 16], P(('ctx', 'uly'), 'tp')
- grad_query_norm: float32 [128], replicated
- grad_key_norm: float32 [128], replicated
- grad_output: float32 [2048, 2048], P('tp', ('ctx', 'uly'))
- grad_mlp_norm: float32 [2048], replicated
- grad_gate: float32 [2048, 6144], P(('ctx', 'uly'), 'tp')
- grad_up: float32 [2048, 6144], P(('ctx', 'uly'), 'tp')
- grad_down: float32 [6144, 2048], P('tp', ('ctx', 'uly'))
The draws below stay inside these ranges and needn't reach their ends.
Inputs may be any that keep to these rules, and one draw needn't show every extreme that they name: `doc_ids`: along a row the ids never fall before the padding; document 0 of every row covers at least the first 2560 positions; the row ends in at least 128 padding tokens of id -1, and id 4 - 1 appears in every row.
All inputs are finite; a program needn't handle non-finite values.
Results may differ from the reference program's by a relative error of at most 0.03.
Values may be sent and summed in bfloat16 or wider, within the bound.
A program may use at most 384 MiB of HBM per device.

```python
import jax
import jax.numpy as jnp
from jax import lax

D = 2048
FF = 6144
HEADS = 16
KV_HEADS = 8
HEAD_DIM = 128
SEQ_LEN = 4096
DOCS = 4
SEQS = 2
QDIM = 2048
KVDIM = 1024


def draw_doc_ids(key, part):
    pad_key = jax.random.fold_in(key, 11)
    first_key = jax.random.fold_in(key, 23)
    rest_key = jax.random.fold_in(key, 37)
    padding = jax.random.randint(pad_key, (SEQS, 1), SEQ_LEN // 32, SEQ_LEN // 8)
    first_cut = jax.random.randint(first_key, (SEQS, 1), 5 * SEQ_LEN // 8, 3 * SEQ_LEN // 4)
    other_cuts = jax.random.randint(rest_key, (SEQS, DOCS - 2), 3 * SEQ_LEN // 4, SEQ_LEN - SEQ_LEN // 8)
    cuts = jnp.concatenate([first_cut, other_cuts], axis=1)
    places = jnp.arange(SEQ_LEN, dtype=jnp.int32)
    ident = jnp.sum((cuts[:, None, :] <= places[None, :, None]).astype(jnp.int32), axis=-1)
    return jnp.where(places[None, :] >= SEQ_LEN - padding, -1, ident).astype(jnp.int32)


def spiked(array, stream_key, source, target, blocks, factor):
    owner, partner = [(jnp.arange(array.shape[dim]) // (array.shape[dim] // blocks)).reshape([-1 if axis == dim else 1 for axis in range(array.ndim)]) for dim in (source, target)]
    chosen = jax.random.permutation(stream_key, blocks)[partner]
    strong = (owner == chosen) | (owner == (partner + blocks // 2) % blocks)
    return jnp.where(strong, factor * array, array)


def levels(own_key, dims, pieces, least, high):
    factor_of, own = 1.0, jax.random.fold_in(own_key, 6)
    for axis_at, blocks in pieces:
        heights = jnp.exp(jax.random.uniform(jax.random.fold_in(own, axis_at), (blocks,), jnp.float32, least / len(pieces), high / len(pieces)))
        factor_of = factor_of * jnp.repeat(heights, dims[axis_at] // blocks).reshape([-1 if axis == axis_at else 1 for axis in range(len(dims))])
    return factor_of


def noise(rng, shape, scale, limit, split=(), kind=jnp.bfloat16):
    level = levels(rng, shape, split, -0.22, 0.18) if split else 1.0
    drawn = jax.random.normal(rng, shape, jnp.float32) * scale * level
    return jnp.minimum(jnp.maximum(drawn, -limit), limit).astype(kind)


def noise_with(key, shape, scale, reach, shards, heavy, held_as=jnp.bfloat16):
    array = scale * jax.random.normal(key, shape, jnp.float32)
    if shards:
        array = array * levels(key, shape, shards, -0.22, 0.18)
    return jnp.clip(spiked(array, jax.random.fold_in(key, 3), *heavy), -reach, reach).astype(held_as)


def setup_inputs(seed: int = 0) -> dict:
    key_of = jax.random.split(jax.random.key(seed), 16)
    inputs = noise(key_of[0], (SEQS, SEQ_LEN, D), 1.0, 6.0, ((1, 32),))
    doc_ids = draw_doc_ids(jax.random.fold_in(key_of[15], 71), 0)
    attn_norm = jnp.clip(1.0 + 0.1 * jax.random.normal(key_of[2], (D,), jnp.float32), 0.5, 1.5)
    w_query = noise(key_of[3], (D, QDIM), D ** -0.5, 0.125, ((1, 4),))
    w_key = noise(key_of[4], (D, KVDIM), D ** -0.5, 0.125, ((1, 4),))
    w_value = noise(key_of[5], (D, KVDIM), D ** -0.5, 0.125, ((1, 4),))
    w_headgate = noise(key_of[6], (D, HEADS), D ** -0.5, 0.125, ((1, 4),))
    query_norm = jnp.clip(1.0 + 0.1 * jax.random.normal(key_of[7], (HEAD_DIM,), jnp.float32), 0.5, 1.5)
    key_norm = jnp.clip(1.0 + 0.1 * jax.random.normal(key_of[8], (HEAD_DIM,), jnp.float32), 0.5, 1.5)
    w_output = noise(key_of[9], (QDIM, D), (QDIM // 16) ** -0.5, 0.5, ((0, 4),))
    mlp_norm = jnp.clip(1.0 + 0.1 * jax.random.normal(key_of[10], (D,), jnp.float32), 0.5, 1.5)
    w_gate = noise(key_of[11], (D, FF), D ** -0.5, 0.125, ((1, 4),))
    w_up = noise(key_of[12], (D, FF), D ** -0.5, 0.125, ((1, 4),))
    w_down = noise(key_of[13], (FF, D), (FF // 4) ** -0.5, 0.15625, ((0, 4),))
    cotangent = noise_with(key_of[14], (SEQS, SEQ_LEN, D), 1.0, 6.0, ((1, 32),), (1, 2, 32, 2.75))
    return dict(inputs=inputs, doc_ids=doc_ids, attn_norm=attn_norm, w_query=w_query, w_key=w_key, w_value=w_value, w_headgate=w_headgate, query_norm=query_norm, key_norm=key_norm, w_output=w_output, mlp_norm=mlp_norm, w_gate=w_gate, w_up=w_up, w_down=w_down, cotangent=cotangent)


epsilon = 1e-06
rope_base = 1000000.0
masked_score = -1e+30

@jax.custom_vjp
def low(v):
    return lax.optimization_barrier(v.astype(jnp.bfloat16)).astype(jnp.float32)

@jax.custom_vjp
def low_back(v):
    return v

def low_keep(v):
    return (low(v), None)

def low_pass(kept, grad):
    return (grad,)

def back_keep(v):
    return (v, None)

def back_low(kept, grad):
    return (low(grad),)
low.defvjp(low_keep, low_pass)
low_back.defvjp(back_keep, back_low)

def matmul(left, right):
    return jnp.dot(left, right, precision=lax.Precision.HIGHEST, preferred_element_type=jnp.float32)

def rms_scale(values, gain):
    return values * lax.rsqrt(lax.optimization_barrier(jnp.mean(values * values, axis=-1, keepdims=True)) + epsilon) * gain

def rotate(values, positions):
    half_dim = values.shape[-1] // 2
    frequency = rope_base ** (-(jnp.arange(half_dim, dtype=jnp.float32) * 2.0 / values.shape[-1]))
    angles = positions.astype(jnp.float32)[:, None] * frequency[None, :]
    cosine = jnp.cos(angles)[None, :, None, :]
    sine_part = jnp.sin(angles)[None, :, None, :]
    lead_part = values[..., :half_dim]
    tail_part = values[..., half_dim:]
    return jnp.concatenate([lead_part * cosine - tail_part * sine_part, tail_part * cosine + lead_part * sine_part], axis=-1)

def head_attention(query_head, key_head, value_head, allowed):
    scale = query_head.shape[-1] ** (-0.5)
    scores = low_back(matmul(query_head, key_head.T) * scale)
    scores = jnp.where(allowed, scores, masked_score)
    peak = lax.optimization_barrier(jnp.max(scores, axis=-1, keepdims=True))
    expo = jnp.exp(scores - peak)
    soft = expo / lax.optimization_barrier(jnp.sum(expo, axis=-1, keepdims=True))
    return low_back(matmul(low(soft), value_head))

def sequence_attention(items):
    queries, keys_all, values_all, ident = items
    length = queries.shape[0]
    places = jnp.arange(length, dtype=jnp.int32)
    earlier = places[None, :] <= places[:, None]
    same_doc = (ident[:, None] == ident[None, :]) & (ident[None, :] >= 0)
    allowed = earlier & same_doc | (places[None, :] == places[:, None])

    def one_head(triple):
        return head_attention(triple[0], triple[1], triple[2], allowed)
    result = lax.map(jax.checkpoint(one_head), (queries.transpose(1, 0, 2), keys_all.transpose(1, 0, 2), values_all.transpose(1, 0, 2)))
    return result.transpose(1, 0, 2)

def reference(inputs, doc_ids, attn_norm, w_query, w_key, w_value, w_headgate, query_norm, key_norm, w_output, mlp_norm, w_gate, w_up, w_down, cotangent):
    group_size = HEADS // KV_HEADS

    def forward(xin, norm_one, wq_in, wk_in, wv_in, wg_in, qn_in, kn_in, wo_in, norm_two, wgate_in, wup_in, wdown_in):
        batch, length, width = xin.shape
        first_in = low(rms_scale(xin, norm_one))
        q_raw = low_back(matmul(first_in, wq_in)).reshape(batch, length, HEADS, HEAD_DIM)
        k_raw = low_back(matmul(first_in, wk_in)).reshape(batch, length, KV_HEADS, HEAD_DIM)
        v_raw = matmul(first_in, wv_in).reshape(batch, length, KV_HEADS, HEAD_DIM)
        gate_logit = low_back(low(matmul(first_in, wg_in)))
        positions = jnp.arange(length, dtype=jnp.int32)
        q_rot = low_back(low(rotate(rms_scale(q_raw, qn_in), positions)))
        k_rot = jnp.repeat(low_back(low(rotate(rms_scale(k_raw, kn_in), positions))), group_size, axis=2)
        v_rot = jnp.repeat(low_back(low(v_raw)), group_size, axis=2)
        attended = lax.map(sequence_attention, (q_rot, k_rot, v_rot, doc_ids))
        gated = low_back(low(attended * jax.nn.sigmoid(gate_logit)[..., None])).reshape(batch, length, HEADS * HEAD_DIM)
        middle = xin + low_back(matmul(gated, wo_in))
        second_in = low(rms_scale(middle, norm_two))
        gate = low_back(matmul(second_in, wgate_in))
        up_part = low_back(matmul(second_in, wup_in))
        hidden = low(jax.nn.silu(gate) * up_part)
        return middle + low_back(matmul(hidden, wdown_in))
    params = tuple((item.astype(jnp.float32) for item in (inputs, attn_norm, w_query, w_key, w_value, w_headgate, query_norm, key_norm, w_output, mlp_norm, w_gate, w_up, w_down)))
    result, pullback = jax.vjp(forward, *params)
    grads = pullback(cotangent.astype(jnp.float32))
    return (result.astype(jnp.bfloat16), grads[0], grads[1], grads[2], grads[3], grads[4], grads[5], grads[6], grads[7], grads[8], grads[9], grads[10], grads[11], grads[12])
```

```python
import functools
import math

import jax
import jax.numpy as jnp
from jax import lax
from jax.experimental import pallas as pl
from jax.experimental.pallas import tpu as pltpu
from jax.sharding import PartitionSpec as P

epsilon = 1e-06
rope_base = 1000000.0
log2e = 1.0 / math.log(2.0)
bf16 = jnp.bfloat16
f32 = jnp.float32
vmem_bytes = 48 * 1024 * 1024

MESH = pl.DeviceIdType.MESH
NT = (((1,), (1,)), ((), ()))
NN = (((1,), (0,)), ((), ()))
TN = (((0,), (0,)), ((), ()))


def mm(left, right, dims=NN):
    return lax.dot_general(left, right, dims, preferred_element_type=f32)


def params(**more):
    return pltpu.CompilerParams(vmem_limit_bytes=vmem_bytes, **more)


def cost(flops, moved, trans=0):
    return pl.CostEstimate(flops=int(flops), bytes_accessed=int(moved), transcendentals=int(trans))


def full(shape):
    return pl.BlockSpec(shape, lambda *_: (0,) * len(shape))


def rms_inverse(values):
    return lax.rsqrt(jnp.mean(values * values, axis=-1, keepdims=True) + epsilon)


def rope_tables(positions, head_dim):
    half = head_dim // 2
    frequency = rope_base ** (-(jnp.arange(half, dtype=f32) * 2.0 / head_dim))
    angles = positions.astype(f32)[:, None] * frequency[None, :]
    cosine, sine = jnp.cos(angles), jnp.sin(angles)
    return jnp.concatenate([cosine, cosine], 1), jnp.concatenate([-sine, sine], 1)


def project_kernel(heads, kv_heads, dim, scale, x_ref, w_ref, cos_ref, sin_ref, qg_ref, kg_ref,
                   q_ref, kv_ref, nq_ref, nk_ref, rq_ref, rk_ref, logit_ref):
    cosine, sine = cos_ref[...], sin_ref[...]
    raw = mm(x_ref[...], w_ref[...])

    def rope(unit, gain):
        scaled = unit * gain
        return scaled * cosine + pltpu.roll(scaled, dim // 2, 1) * sine

    for h in range(heads + kv_heads):
        values = raw[:, h * dim:(h + 1) * dim]
        inverse = rms_inverse(values)
        unit = values * inverse
        if h < heads:
            at = slice(h * dim, (h + 1) * dim)
            q_ref[:, at] = (rope(unit, qg_ref[...]) * (scale * log2e)).astype(bf16)
            nq_ref[:, at] = unit.astype(bf16)
            rq_ref[:, h:h + 1] = inverse
        else:
            g = h - heads
            at = slice(g * dim, (g + 1) * dim)
            kv_ref[:, at] = rope(unit, kg_ref[...]).astype(bf16)
            nk_ref[:, at] = unit.astype(bf16)
            rk_ref[:, g:g + 1] = inverse
    first = (heads + kv_heads) * dim
    kv_ref[:, kv_heads * dim:] = raw[:, first:first + kv_heads * dim].astype(bf16)
    first += kv_heads * dim
    logit_ref[...] = raw[:, first:first + heads].astype(bf16).astype(f32)


def project(x, w, tables, query_norm, key_norm, heads, kv_heads, scale, block=256):
    rows, width = x.shape
    dim = query_norm.shape[0]
    cosine, sine = tables
    block = min(block, cosine.shape[0])
    around = cosine.shape[0] // block
    kernel = functools.partial(project_kernel, heads, kv_heads, dim, scale)

    def by_row(cols):
        return pl.BlockSpec((block, cols), lambda i: (i, 0))

    table = pl.BlockSpec((block, dim), lambda i: (i % around, 0))
    shapes = [
        (heads * dim, bf16), (2 * kv_heads * dim, bf16), (heads * dim, bf16), (kv_heads * dim, bf16),
        (heads, f32), (kv_heads, f32), (heads, f32),
    ]
    return pl.pallas_call(
        kernel,
        grid=(rows // block,),
        in_specs=[by_row(width), full(w.shape), table, table, full((1, dim)), full((1, dim))],
        out_specs=[by_row(c) for c, _ in shapes],
        out_shape=[jax.ShapeDtypeStruct((rows, c), t) for c, t in shapes],
        compiler_params=params(),
        cost_estimate=cost(2 * rows * width * w.shape[1], 2 * (rows * width + w.size) + rows * 4096),
        name="project",
    )(x, w, cosine, sine, query_norm[None], key_norm[None])


def bounds_loop(bounds_ref, row, body):
    lo, full_lo, full_hi, hi = (bounds_ref[row, i] for i in range(4))
    lax.fori_loop(lo, full_lo, lambda j, c: body(j, True), None)
    lax.fori_loop(full_lo, full_hi, lambda j, c: body(j, False), None)
    lax.fori_loop(full_hi, hi, lambda j, c: body(j, True), None)


def attend_kernel(heads, kv_heads, dim, block, bounds_ref, q_ref, kv_ref, start_ref, pos_ref, logit_ref,
                  att_ref, gated_ref, lse_ref, q2_ref, acc_ref, sum_ref):
    row = pl.program_id(0)
    group = q_ref.shape[1]
    repeat = heads // kv_heads
    for h in range(kv_heads):
        for g in range(repeat):
            at = slice((h * repeat + g) * dim, (h * repeat + g + 1) * dim)
            q2_ref[g * group:(g + 1) * group, :] = q_ref[0, :, at]
        acc_ref[...] = jnp.zeros_like(acc_ref)
        sum_ref[...] = jnp.zeros_like(sum_ref)

        def body(j, masked):
            at = pl.ds(pl.multiple_of(j * block, block), block)
            keys = kv_ref[0, at, h * dim:(h + 1) * dim]
            values = kv_ref[0, at, (kv_heads + h) * dim:(kv_heads + h + 1) * dim]
            if masked:
                spot = j * block + lax.broadcasted_iota(jnp.int32, (group, block), 1)
                allowed = (spot >= start_ref[0]) & (spot <= pos_ref[...])
            for g in range(repeat):
                part = slice(g * group, (g + 1) * group)
                weight = jnp.exp2(mm(q2_ref[part, :], keys, NT))
                if masked:
                    weight = jnp.where(allowed, weight, 0.0)
                total = weight[:, :dim]
                for i in range(1, block // dim):
                    total = total + weight[:, i * dim:(i + 1) * dim]
                sum_ref[part, :] += total
                acc_ref[part, :] += mm(weight.astype(bf16), values)

        bounds_loop(bounds_ref, row, body)
        for g in range(repeat):
            part = slice(g * group, (g + 1) * group)
            n = h * repeat + g
            at = slice(n * dim, (n + 1) * dim)
            total = jnp.sum(sum_ref[part, :], axis=1, keepdims=True)
            attended = acc_ref[part, :] / total
            att_ref[0, :, at] = attended.astype(bf16)
            gated_ref[0, :, at] = (attended * jax.nn.sigmoid(logit_ref[0, :, n:n + 1])).astype(bf16)
            lse_ref[0, n:n + 1, :] = jnp.log2(jnp.sum(sum_ref[part, :].T, axis=0, keepdims=True))


def attend(q, kv, bounds, start_col, pos_col, logits, heads, kv_heads, dim, block):
    rows, group, width = q.shape
    total = kv.shape[1]
    repeat = heads // kv_heads

    def by_row(*shape):
        return pl.BlockSpec((1, *shape), lambda r, *_: (r, 0, 0))

    return pl.pallas_call(
        functools.partial(attend_kernel, heads, kv_heads, dim, block),
        grid_spec=pltpu.PrefetchScalarGridSpec(
            num_scalar_prefetch=1,
            grid=(rows,),
            in_specs=[
                by_row(group, width), by_row(total, kv.shape[2]), by_row(group, 1), full((group, 1)),
                by_row(group, heads),
            ],
            out_specs=[by_row(group, width), by_row(group, width), by_row(heads, group)],
            scratch_shapes=[
                pltpu.VMEM((repeat * group, dim), bf16),
                pltpu.VMEM((repeat * group, dim), f32),
                pltpu.VMEM((repeat * group, dim), f32),
            ],
        ),
        out_shape=[
            jax.ShapeDtypeStruct((rows, group, width), bf16),
            jax.ShapeDtypeStruct((rows, group, width), bf16),
            jax.ShapeDtypeStruct((rows, heads, group), f32),
        ],
        compiler_params=params(),
        cost_estimate=cost(
            2 * rows * heads * group * total * dim, 2 * kv.size + 6 * q.size, rows * heads * group * total // 2
        ),
        name="attend",
    )(bounds, q, kv, start_col, pos_col, logits)


def attend_back_kernel(heads, kv_heads, dim, block, scale, bounds_ref, q_ref, kv_ref, dgated_ref, att_ref,
                       logit_ref, logit_row_ref, lse_ref, start_ref, pos_ref, nq_ref, rq_ref, cos_ref, sin_ref,
                       gain_ref, dq_ref, dlogit_ref, dkv_ref, dgain_ref,
                       q2_ref, da2_ref, delta_ref, lse2_ref, dq2_ref):
    row = pl.program_id(0)
    group = q_ref.shape[1]
    repeat = heads // kv_heads
    cosine, sine, gain = cos_ref[...], sin_ref[...], gain_ref[...]

    @pl.when(row == 0)
    def _():
        dgain_ref[...] = jnp.zeros_like(dgain_ref)

    dkv_ref[...] = jnp.zeros_like(dkv_ref)
    for h in range(kv_heads):
        for g in range(repeat):
            n = h * repeat + g
            at = slice(n * dim, (n + 1) * dim)
            part = slice(g * group, (g + 1) * group)
            q2_ref[part, :] = q_ref[0, :, at]
            grad = dgated_ref[0, :, at].astype(f32)
            sigma = jax.nn.sigmoid(logit_ref[0, :, n:n + 1])
            da2_ref[part, :] = (grad * sigma).astype(bf16)
            dot = jnp.sum((grad * att_ref[0, :, at].astype(f32)).T, axis=0, keepdims=True)
            sigma_row = jax.nn.sigmoid(logit_row_ref[0, n:n + 1, :])
            dlogit_ref[0, n:n + 1, :] = dot * sigma_row * (1.0 - sigma_row)
            delta_ref[:, part] = dot * sigma_row
            lse2_ref[:, part] = lse_ref[0, n:n + 1, :]
        dq2_ref[...] = jnp.zeros_like(dq2_ref)

        def body(j, masked):
            at = pl.ds(pl.multiple_of(j * block, block), block)
            keys = kv_ref[0, at, h * dim:(h + 1) * dim]
            values = kv_ref[0, at, (kv_heads + h) * dim:(kv_heads + h + 1) * dim]
            if masked:
                spot = j * block + lax.broadcasted_iota(jnp.int32, (block, group), 0)
                allowed = (spot >= start_ref[0]) & (spot <= pos_ref[...])
            dk = jnp.zeros((block, dim), f32)
            dv = jnp.zeros((block, dim), f32)
            for g in range(repeat):
                part = slice(g * group, (g + 1) * group)
                weight = jnp.exp2(mm(keys, q2_ref[part, :], NT) - lse2_ref[:, part])
                if masked:
                    weight = jnp.where(allowed, weight, 0.0)
                dv += mm(weight.astype(bf16), da2_ref[part, :])
                dprob = mm(values, da2_ref[part, :], NT)
                dscore = (weight * (dprob - delta_ref[:, part])).astype(bf16)
                dk += mm(dscore, q2_ref[part, :])
                dq2_ref[part, :] += mm(dscore, keys, TN)
            dkv_ref[0, at, h * dim:(h + 1) * dim] = (dk * (1.0 / log2e)).astype(bf16)
            dkv_ref[0, at, (kv_heads + h) * dim:(kv_heads + h + 1) * dim] = dv.astype(bf16)

        bounds_loop(bounds_ref, row, body)
        for g in range(repeat):
            n = h * repeat + g
            at = slice(n * dim, (n + 1) * dim)
            part = slice(g * group, (g + 1) * group)
            turned = (dq2_ref[part, :] * scale).astype(bf16).astype(f32)
            back = turned * cosine - pltpu.roll(turned, dim // 2, 1) * sine
            unit = nq_ref[0, :, at].astype(f32)
            dgain_ref[...] += jnp.sum(back * unit, axis=0, keepdims=True)
            inner = back * gain
            mean = jnp.mean(inner * unit, axis=1, keepdims=True)
            dq_ref[0, :, at] = (rq_ref[0, :, n:n + 1] * (inner - unit * mean)).astype(bf16)


def attend_back(q, kv, dgated, att, logits, logit_rows, lse, bounds, start_row, pos_row, nq, rq, tables, gain,
                heads, kv_heads, dim, block, scale):
    rows, group, width = q.shape
    total = kv.shape[1]
    repeat = heads // kv_heads
    cosine, sine = tables

    def by_row(*shape):
        return pl.BlockSpec((1, *shape), lambda r, *_: (r, 0, 0))

    wide = by_row(group, width)
    return pl.pallas_call(
        functools.partial(attend_back_kernel, heads, kv_heads, dim, block, scale),
        grid_spec=pltpu.PrefetchScalarGridSpec(
            num_scalar_prefetch=1,
            grid=(rows,),
            in_specs=[
                wide, by_row(total, kv.shape[2]), wide, wide, by_row(group, heads), by_row(heads, group),
                by_row(heads, group), by_row(1, group), full((1, group)), wide, by_row(group, heads),
                full((group, dim)), full((group, dim)), full((1, dim)),
            ],
            out_specs=[wide, by_row(heads, group), by_row(total, kv.shape[2]), full((1, dim))],
            scratch_shapes=[
                pltpu.VMEM((repeat * group, dim), bf16),
                pltpu.VMEM((repeat * group, dim), bf16),
                pltpu.VMEM((1, repeat * group), f32),
                pltpu.VMEM((1, repeat * group), f32),
                pltpu.VMEM((repeat * group, dim), f32),
            ],
        ),
        out_shape=[
            jax.ShapeDtypeStruct((rows, group, width), bf16),
            jax.ShapeDtypeStruct((rows, heads, group), f32),
            jax.ShapeDtypeStruct(kv.shape, bf16),
            jax.ShapeDtypeStruct((1, dim), f32),
        ],
        compiler_params=params(),
        cost_estimate=cost(
            5 * rows * heads * group * total * dim, 4 * kv.size + 10 * q.size, rows * heads * group * total // 2
        ),
        name="attend_back",
    )(bounds, q, kv, dgated, att, logits, logit_rows, lse, start_row, pos_row, nq, rq, cosine, sine, gain[None])


def key_back_kernel(kv_heads, dim, dkv_ref, nk_ref, rk_ref, cos_ref, sin_ref, gain_ref, dk_ref, dgain_ref):
    @pl.when(pl.program_id(0) == 0)
    def _():
        dgain_ref[...] = jnp.zeros_like(dgain_ref)

    for h in range(kv_heads):
        at = slice(h * dim, (h + 1) * dim)
        turned = dkv_ref[0, :, at].astype(f32)
        back = turned * cos_ref[...] - pltpu.roll(turned, dim // 2, 1) * sin_ref[...]
        unit = nk_ref[0, :, at].astype(f32)
        dgain_ref[...] += jnp.sum(back * unit, axis=0, keepdims=True)
        inner = back * gain_ref[...]
        mean = jnp.mean(inner * unit, axis=1, keepdims=True)
        dk_ref[0, :, at] = (rk_ref[0, :, h:h + 1] * (inner - unit * mean)).astype(bf16)
    dk_ref[0, :, kv_heads * dim:] = dkv_ref[0, :, kv_heads * dim:]


def key_back(dkv, nk, rk, tables, gain, kv_heads, dim):
    rows, group, width = dkv.shape

    def by_row(*shape):
        return pl.BlockSpec((1, *shape), lambda r: (r, 0, 0))

    return pl.pallas_call(
        functools.partial(key_back_kernel, kv_heads, dim),
        grid=(rows,),
        in_specs=[
            by_row(group, width), by_row(group, kv_heads * dim), by_row(group, kv_heads), full((group, dim)),
            full((group, dim)), full((1, dim)),
        ],
        out_specs=[by_row(group, width), full((1, dim))],
        out_shape=[jax.ShapeDtypeStruct((rows, group, width), bf16), jax.ShapeDtypeStruct((1, dim), f32)],
        compiler_params=params(),
        cost_estimate=cost(20 * dkv.size, 6 * dkv.size),
        name="key_back",
    )(dkv, nk, rk, *tables, gain[None])


def line_barrier(n, me):
    barrier = pltpu.get_barrier_semaphore()
    for way in (1, -1):
        @pl.when((me + way >= 0) & (me + way < n))
        def _():
            pl.semaphore_signal(barrier, inc=1, device_id={"tp": jnp.clip(me + way, 0, n - 1)}, device_id_type=MESH)
    edge = (me == 0) | (me == n - 1)

    @pl.when(edge)
    def _():
        pl.semaphore_wait(barrier, 1)

    @pl.when(jnp.logical_not(edge))
    def _():
        pl.semaphore_wait(barrier, 2)


def line_all_sum(n, seqs, rows, piece, finish, part_ref, out_ref, land_ref, stage_ref, sems):
    rs_send, rs_recv, ag_send, ag_recv = sems
    me = lax.axis_index("tp")
    line_barrier(n, me)
    cuts = [(q, c) for q in range(seqs) for c in range(rows // piece)]

    def inside(place):
        return (place >= 0) & (place < n)

    def at(ref, owner, s):
        q, c = cuts[s]
        return ref.at[q, pl.ds(pl.multiple_of(owner * rows + c * piece, piece), piece)]

    def reduce_copy(way, k, s, source):
        d = 0 if way == 1 else 1
        return pltpu.make_async_remote_copy(
            src_ref=source, dst_ref=land_ref.at[d, k - 1, s], send_sem=rs_send.at[d, k - 1, s],
            recv_sem=rs_recv.at[d, k - 1, s], device_id={"tp": jnp.clip(me + way, 0, n - 1)}, device_id_type=MESH)

    def spread_copy(way, k, s, owner):
        d = 0 if way == 1 else 1
        rows_ref = at(out_ref, owner, s)
        return pltpu.make_async_remote_copy(
            src_ref=rows_ref, dst_ref=rows_ref, send_sem=ag_send.at[d, k - 1, s],
            recv_sem=ag_recv.at[d, k - 1, s], device_id={"tp": jnp.clip(me + way, 0, n - 1)}, device_id_type=MESH)

    def reduce_step(k, s):
        for way in (1, -1):
            d = 0 if way == 1 else 1
            dest = me + way * (n - k)
            sends = inside(me + way) & inside(dest)
            safe = jnp.clip(dest, 0, n - 1)
            if k == 1:
                @pl.when(sends)
                def _():
                    reduce_copy(way, k, s, at(part_ref, safe, s)).start()
            else:
                got = sends & inside(me - way)

                @pl.when(got)
                def _():
                    reduce_copy(way, k - 1, s, stage_ref.at[d, 0, s]).wait_recv()
                    stage_ref[d, k - 2, s] = (
                        at(part_ref, safe, s)[...].astype(f32) + land_ref[d, k - 2, s].astype(f32)).astype(bf16)
                    reduce_copy(way, k, s, stage_ref.at[d, k - 2, s]).start()

                @pl.when(sends & jnp.logical_not(inside(me - way)))
                def _():
                    reduce_copy(way, k, s, at(part_ref, safe, s)).start()

    def own_step(s):
        q, c = cuts[s]
        for way in (1, -1):
            d = 0 if way == 1 else 1

            @pl.when(inside(me - way))
            def _():
                reduce_copy(way, n - 1, s, stage_ref.at[d, 0, s]).wait_recv()

            @pl.when(jnp.logical_not(inside(me - way)))
            def _():
                land_ref[d, n - 2, s] = jnp.zeros_like(land_ref[d, n - 2, s])
        total = (at(part_ref, me, s)[...].astype(f32) + land_ref[0, n - 2, s].astype(f32)
                 + land_ref[1, n - 2, s].astype(f32))
        at(out_ref, me, s)[...] = finish(q, c, total)

    def spread_step(k, s):
        for way in (1, -1):
            owner = me - way * (k - 1)
            if k > 1:
                @pl.when(inside(owner))
                def _():
                    spread_copy(way, k - 1, s, jnp.clip(owner, 0, n - 1)).wait_recv()
            if k < n:
                @pl.when(inside(owner) & inside(me + way))
                def _():
                    spread_copy(way, k, s, jnp.clip(owner, 0, n - 1)).start()

    stages = []
    for k in range(1, n):
        stages.append(functools.partial(reduce_step, k))

    def turn(s):
        own_step(s)
        spread_step(1, s)

    stages.append(turn)
    for k in range(2, n + 1):
        stages.append(functools.partial(spread_step, k))
    for step in range(len(cuts) + len(stages) - 1):
        for s in range(len(cuts)):
            if 0 <= step - s < len(stages):
                stages[step - s](s)
    for s in range(len(cuts)):
        for way in (1, -1):
            d = 0 if way == 1 else 1
            for k in range(1, n):
                dest = me + way * (n - k)

                @pl.when(inside(me + way) & inside(dest))
                def _():
                    reduce_copy(way, k, s, land_ref.at[d, 0, s]).wait_send()
                owner = me - way * (k - 1)

                @pl.when(inside(owner) & inside(me + way))
                def _():
                    spread_copy(way, k, s, jnp.clip(owner, 0, n - 1)).wait_send()


def line_scratch(n, seqs, rows, piece, width):
    count = seqs * (rows // piece)
    return [
        pltpu.VMEM((2, n - 1, count, piece, width), bf16),
        pltpu.VMEM((2, max(n - 2, 1), count, piece, width), bf16),
        pltpu.SemaphoreType.DMA((2, n - 1, count)), pltpu.SemaphoreType.DMA((2, n - 1, count)),
        pltpu.SemaphoreType.DMA((2, n - 1, count)), pltpu.SemaphoreType.DMA((2, n - 1, count)),
    ]


def norm_forward_kernel(n, seqs, rows, piece, part_ref, x_ref, gain_ref, out_ref, mid_ref, land_ref, stage_ref, *sems):
    def finish(q, c, total):
        at = slice(c * piece, (c + 1) * piece)
        mid = x_ref[q, at].astype(f32) + total
        mid_ref[q, at] = mid
        return (mid * rms_inverse(mid) * gain_ref[...]).astype(bf16)

    line_all_sum(n, seqs, rows, piece, finish, part_ref, out_ref, land_ref, stage_ref, sems)


def norm_back_kernel(n, seqs, rows, piece, part_ref, cot_ref, mid_ref, gain_ref, out_ref, dmid_ref, dgain_ref,
                     land_ref, stage_ref, *sems):
    dgain_ref[...] = jnp.zeros_like(dgain_ref)

    def finish(q, c, total):
        at = slice(c * piece, (c + 1) * piece)
        mid = mid_ref[q, at]
        inverse = rms_inverse(mid)
        unit = mid * inverse
        dgain_ref[...] += jnp.sum(total * unit, axis=0, keepdims=True)
        inner = total * gain_ref[...]
        mean = jnp.mean(inner * unit, axis=-1, keepdims=True)
        d_mid = cot_ref[q, at].astype(f32) + inverse * (inner - unit * mean)
        dmid_ref[q, at] = d_mid
        return d_mid.astype(bf16)

    line_all_sum(n, seqs, rows, piece, finish, part_ref, out_ref, land_ref, stage_ref, sems)


def line_call(kernel, n, local, part, others, extra, collective_id, name):
    seqs, rows, width = local
    piece = min(64, rows)
    vm = pl.BlockSpec(memory_space=pltpu.VMEM)
    shapes = [jax.ShapeDtypeStruct(part.shape, bf16), jax.ShapeDtypeStruct(local, f32), *extra]
    return pl.pallas_call(
        functools.partial(kernel, n, seqs, rows, piece),
        in_specs=[vm] * (1 + len(others)),
        out_specs=[vm] * len(shapes),
        out_shape=shapes,
        scratch_shapes=line_scratch(n, seqs, rows, piece, width),
        compiler_params=params(collective_id=collective_id, has_side_effects=True),
        cost_estimate=cost(20 * part.size, 100_000_000),
        name=name,
    )(part, *others)


def plane_place(n_uly):
    return lax.axis_index("ctx") * n_uly + lax.axis_index("uly")


def plane_device(place, n_uly):
    return {"ctx": place // n_uly, "uly": lax.rem(place, n_uly)}


def plane_barrier(bits, me, n_uly):
    barrier = pltpu.get_barrier_semaphore()
    for b in range(bits):
        pl.semaphore_signal(barrier, inc=1, device_id=plane_device(me ^ (1 << b), n_uly), device_id_type=MESH)
    pl.semaphore_wait(barrier, bits)


def ways(bits):
    upper = list(range(1, bits))
    return upper, upper[::-1]


def span(order):
    out = [0]
    for b in order:
        out += [e | (1 << b) for e in out]
    return out


def plane_gather_kernel(bits, n_uly, own_ref, out_ref, copy_sem, send_sem, recv_sem):
    me = plane_place(n_uly)
    rows, half = own_ref.shape[1], own_ref.shape[2] // 2
    plane_barrier(bits, me, n_uly)
    orders = [w + [0] for w in ways(bits)]

    def block(place, d):
        return out_ref.at[:, pl.ds(pl.multiple_of(place * rows, rows), rows), pl.ds(d * half, half)]

    def copy(d, level, e):
        bit = orders[d][level]
        source = own_ref.at[:, :, pl.ds(d * half, half)] if e == 0 else block(me ^ e, d)
        return pltpu.make_async_remote_copy(
            src_ref=source, dst_ref=block(me ^ e, d), send_sem=send_sem.at[d, e | (1 << bit)],
            recv_sem=recv_sem.at[d, e | (1 << bit)], device_id=plane_device(me ^ (1 << bit), n_uly),
            device_id_type=MESH)

    own = [pltpu.make_async_copy(own_ref.at[:, :, pl.ds(d * half, half)], block(me, d), copy_sem.at[d]) for d in range(2)]
    for c in own:
        c.start()
    for level in range(bits):
        for d in range(2):
            for e in span(orders[d][:level]):
                if level > 0 and e >> orders[d][level - 1] & 1:
                    continue
                copy(d, level, e).start()
        for d in range(2):
            for e in span(orders[d][:level]):
                copy(d, level, e).wait_recv()
                if level + 1 < bits:
                    copy(d, level + 1, e | (1 << orders[d][level])).start()
    for d in range(2):
        own[d].wait()
        for level in range(bits):
            for e in span(orders[d][:level]):
                copy(d, level, e).wait_send()


def plane_gather(own, sizes, collective_id):
    n_ctx, n_uly = sizes
    count = n_ctx * n_uly
    bits = count.bit_length() - 1
    seqs, rows, width = own.shape
    if own.size * count * 2 > 12 << 20 or count != 1 << bits or bits < 2:
        return lax.all_gather(own, ("ctx", "uly"), axis=1, tiled=True)
    vm = pl.BlockSpec(memory_space=pltpu.VMEM)
    return pl.pallas_call(
        functools.partial(plane_gather_kernel, bits, n_uly),
        in_specs=[vm], out_specs=vm,
        out_shape=jax.ShapeDtypeStruct((seqs, rows * count, width), own.dtype),
        scratch_shapes=[pltpu.SemaphoreType.DMA((2,)), pltpu.SemaphoreType.DMA((2, count)), pltpu.SemaphoreType.DMA((2, count))],
        compiler_params=params(collective_id=collective_id, has_side_effects=True),
        cost_estimate=cost(0, 100_000_000),
        name="plane_gather",
    )(own)


class PlaneSum:
    def __init__(self, bits, n_uly, make, store, buf_ref, land_ref, send, recv):
        self.bits, self.n_uly, self.make, self.store = bits, n_uly, make, store
        self.buf, self.land, self.send, self.recv = buf_ref, land_ref, send, recv
        self.me = plane_place(n_uly)
        width = buf_ref.shape[-1]
        half = max(width // 256, 1) * 128
        self.parts = [(0, half), (half, width - half)]
        self.orders = ways(bits)

    @staticmethod
    def scratch(bits, rows, width):
        n = 1 << bits
        return [
            pltpu.VMEM((n, rows, width), bf16), pltpu.VMEM((n - 1, rows, width), bf16),
            pltpu.SemaphoreType.DMA((3, n)), pltpu.SemaphoreType.DMA((3, n)),
        ]

    def first_copy(self, e):
        return pltpu.make_async_remote_copy(
            src_ref=self.buf.at[e], dst_ref=self.land.at[e - 1], send_sem=self.send.at[2, e],
            recv_sem=self.recv.at[2, e], device_id=plane_device(self.me ^ 1, self.n_uly), device_id_type=MESH)

    def copy(self, d, level, e):
        at = pl.ds(*self.parts[d])
        return pltpu.make_async_remote_copy(
            src_ref=self.buf.at[e, :, at], dst_ref=self.land.at[e - 1, :, at], send_sem=self.send.at[d, e],
            recv_sem=self.recv.at[d, e],
            device_id=plane_device(self.me ^ (1 << self.orders[d][level]), self.n_uly), device_id_type=MESH)

    def sent(self, d, level):
        return [(1 << self.orders[d][level]) | e for e in span(self.orders[d][level + 1:])]

    def compute(self):
        n = 1 << self.bits
        for e in range(1, n, 2):
            self.buf[e] = self.make(self.me ^ e).astype(bf16)
            self.first_copy(e).start()
        for e in range(0, n, 2):
            self.buf[e] = self.make(self.me ^ e).astype(bf16)

    def pair(self):
        for e in range(1, 1 << self.bits, 2):
            self.first_copy(e).wait_recv()
            self.buf[e - 1] = (self.buf[e - 1].astype(f32) + self.land[e - 1].astype(f32)).astype(bf16)

    def push(self, level):
        for d in range(2):
            for e in self.sent(d, level):
                self.copy(d, level, e).start()

    def pull(self, level):
        for d in range(2):
            at = pl.ds(*self.parts[d])
            for e in self.sent(d, level):
                kept = e ^ (1 << self.orders[d][level])
                self.copy(d, level, e).wait_recv()
                total = self.buf[kept, :, at].astype(f32) + self.land[e - 1, :, at].astype(f32)
                if level == self.bits - 2:
                    self.store(at, total)
                else:
                    self.buf[kept, :, at] = total.astype(bf16)

    def finish(self):
        for e in range(1, 1 << self.bits, 2):
            self.first_copy(e).wait_send()
        for d in range(2):
            for level in range(self.bits - 1):
                for e in self.sent(d, level):
                    self.copy(d, level, e).wait_send()


def blocks_sum_kernel(bits, n_uly, parts_ref, out_ref, *scratch):
    me = plane_place(n_uly)
    plane_barrier(bits, me, n_uly)
    seqs, rows = out_ref.shape[0], out_ref.shape[1]

    def make(place):
        return parts_ref[:, pl.ds(pl.multiple_of(place * rows, rows), rows)].reshape(seqs * rows, -1)

    def store(at, total):
        out_ref[:, :, at] = total.reshape(seqs, rows, -1).astype(out_ref.dtype)

    job = PlaneSum(bits, n_uly, make, store, *scratch)
    job.compute()
    job.pair()
    for level in range(bits - 1):
        job.push(level)
        job.pull(level)
    job.finish()


def blocks_sum(parts, sizes, collective_id):
    n_ctx, n_uly = sizes
    count = n_ctx * n_uly
    bits = count.bit_length() - 1
    seqs, total, width = parts.shape
    rows = total // count
    if parts.size * 2 > 12 << 20 or count != 1 << bits or bits < 2:
        return lax.psum_scatter(parts, ("ctx", "uly"), scatter_dimension=1, tiled=True)
    vm = pl.BlockSpec(memory_space=pltpu.VMEM)
    return pl.pallas_call(
        functools.partial(blocks_sum_kernel, bits, n_uly),
        in_specs=[vm],
        out_specs=vm,
        out_shape=jax.ShapeDtypeStruct((seqs, rows, width), bf16),
        scratch_shapes=PlaneSum.scratch(bits, seqs * rows, width),
        compiler_params=params(collective_id=collective_id, has_side_effects=True),
        cost_estimate=cost(10 * parts.size, 100_000_000),
        name="blocks_sum",
    )(parts)


def outer_sums_kernel(bits, n_uly, use, *refs):
    count, kinds = len(use), max(use) + 1
    lefts, refs = [refs[k] for k in use], refs[kinds:]
    rights, outs, scratch = refs[:count], refs[count:2 * count], refs[2 * count:]
    plane_barrier(bits, plane_place(n_uly), n_uly)
    jobs = []
    for i in range(count):
        each = outs[i].shape[0]

        def make(place, i=i, each=each):
            left = lefts[i][:, pl.ds(pl.multiple_of(place * each, each), each)]
            return mm(left, rights[i][...], TN)

        def store(at, total, i=i):
            outs[i][:, at] = total

        jobs.append(PlaneSum(bits, n_uly, make, store, *scratch[4 * i:4 * i + 4]))
    last = bits - 2
    for i in range(count + last + 1):
        if i < count:
            jobs[i].compute()
            jobs[i].pair()
            jobs[i].push(0)
        for level in range(last + 1):
            j = i - 1 - level
            if 0 <= j < count:
                jobs[j].pull(level)
                if level < last:
                    jobs[j].push(level + 1)
                else:
                    jobs[j].finish()


def outer_sums(kinds, use, rights, sizes, collective_id):
    lefts = [kinds[k] for k in use]
    n_ctx, n_uly = sizes
    places = n_ctx * n_uly
    bits = places.bit_length() - 1
    count = len(lefts)
    if places != 1 << bits or bits < 2 or lefts[0].shape[1] // places % 128:
        return [
            lax.psum_scatter(mm(l, r, TN).astype(bf16), ("ctx", "uly"), scatter_dimension=0, tiled=True).astype(f32)
            for l, r in zip(lefts, rights)
        ]
    vm = pl.BlockSpec(memory_space=pltpu.VMEM)
    shapes = [(l.shape[1] // places, r.shape[1]) for l, r in zip(lefts, rights)]
    scratch = []
    for shape in shapes:
        scratch += PlaneSum.scratch(bits, *shape)
    work = sum(l.size * r.shape[1] for l, r in zip(lefts, rights))
    return pl.pallas_call(
        functools.partial(outer_sums_kernel, bits, n_uly, use),
        in_specs=[vm] * (len(kinds) + count),
        out_specs=[vm] * count,
        out_shape=[jax.ShapeDtypeStruct(s, f32) for s in shapes],
        scratch_shapes=scratch,
        compiler_params=pltpu.CompilerParams(
            collective_id=collective_id, has_side_effects=True, vmem_limit_bytes=60 * 1024 * 1024),
        cost_estimate=cost(2 * work, 200_000_000),
        name="outer_sums",
    )(*kinds, *rights)


def flatten(values):
    return values.reshape(-1, values.shape[-1])


def spread(values):
    return lax.all_gather(values.astype(bf16), "tp", axis=1, tiled=True)


def collect(values):
    return lax.psum_scatter(values.astype(bf16), "tp", scatter_dimension=1, tiled=True).astype(f32)


def per_device(sizes, inputs, doc_ids, attn_norm, w_query, w_key, w_value, w_headgate, query_norm, key_norm, w_output,
               mlp_norm, w_gate, w_up, w_down, cotangent):
    n_tensor = lax.axis_size("tp")
    n_uly = sizes[1]
    seqs, rows, width = inputs.shape
    group = rows * n_tensor
    dim = query_norm.shape[0]
    heads = w_query.shape[1] // dim
    kv_heads = w_key.shape[1] // dim
    scale = dim ** (-0.5)
    plane = ("ctx", "uly")
    place = lax.axis_index("ctx") * n_uly + lax.axis_index("uly")
    block_start = place * group
    positions = block_start + jnp.arange(group, dtype=jnp.int32)
    tables = rope_tables(positions, dim)
    block = min(512, group)

    def wide(values):
        return values.reshape(seqs, group, -1)

    query_doc = lax.dynamic_slice_in_dim(doc_ids, block_start, group, 1)
    before = (doc_ids[:, None, :] >= 0) & (doc_ids[:, None, :] < query_doc[:, :, None])
    start = jnp.where(query_doc >= 0, jnp.sum(before.astype(jnp.int32), axis=-1), positions[None, :])
    lowest, highest = jnp.min(start, axis=1), jnp.max(start, axis=1)
    hi = jnp.full_like(lowest, (block_start + group + block - 1) // block)
    lo = lowest // block
    full_lo = jnp.clip((highest + block - 1) // block, lo, hi)
    full_hi = jnp.clip(jnp.full_like(lowest, (block_start + 1) // block), full_lo, hi)
    bounds = jnp.stack([lo, full_lo, full_hi, hi], axis=1)

    pad = 128 - heads
    w_first = jnp.concatenate([w_query, w_key, w_value, jnp.pad(w_headgate, ((0, 0), (0, pad)))], axis=1)
    q_cols, kv_cols = heads * dim, kv_heads * dim
    n_main = q_cols + 2 * kv_cols

    xs = inputs.astype(f32)
    inv_one = rms_inverse(xs)
    first = spread(xs * inv_one * attn_norm)
    q, kv, nq, nk, rq, rk, logits = (
        wide(m) for m in project(flatten(first), w_first, tables, query_norm, key_norm, heads, kv_heads, scale))
    cot_in, _ = lax.optimization_barrier((cotangent, first))
    cot_all = spread(cot_in)
    kv = plane_gather(kv, sizes, 0)
    att, gated, lse = attend(q, kv, bounds, start[:, :, None], positions[:, None], logits, heads, kv_heads, dim, block)

    local = inputs.shape
    second, middle = line_call(
        norm_forward_kernel, n_tensor, local, wide(mm(flatten(gated), w_output).astype(bf16)),
        (inputs, mlp_norm[None]), (), 1, "norm_forward")

    a2, cot = flatten(second), flatten(cot_all)
    gate, up = mm(a2, w_gate), mm(a2, w_up)
    d_hidden = mm(cot, w_down, NT)
    sig = jax.nn.sigmoid(gate)
    silu = gate * sig
    hidden = (silu * up).astype(bf16)
    d_gate = (d_hidden * up * sig * (1.0 + gate * (1.0 - sig))).astype(bf16)
    d_up = (d_hidden * silu).astype(bf16)
    d_second = (mm(d_gate, w_gate, NT) + mm(d_up, w_up, NT)).astype(bf16)
    d_branch, d_mid, grad_mlp_norm = line_call(
        norm_back_kernel, n_tensor, local, wide(d_second), (cotangent, middle, mlp_norm[None]),
        (jax.ShapeDtypeStruct((1, width), f32),), 2, "norm_back")

    late_hidden, d_branch = lax.optimization_barrier((hidden, d_branch))
    outputs = (middle + collect(wide(mm(late_hidden, w_down)))).astype(bf16)

    d_gated = wide(mm(flatten(d_branch), w_output, NT).astype(bf16))
    d_q, d_logit, d_kv, d_qgain = attend_back(
        q, kv, d_gated, att, logits, logits.transpose(0, 2, 1), lse, bounds, start[:, None, :], positions[None, :], nq,
        rq, tables, query_norm, heads, kv_heads, dim, block, scale)
    d_kv = blocks_sum(d_kv, sizes, 3)
    d_kv, d_kgain = key_back(d_kv, nk, rk, tables, key_norm, kv_heads, dim)
    d_logit = jnp.pad(d_logit.astype(bf16).transpose(0, 2, 1), ((0, 0), (0, 0), (0, pad)))
    d_all = flatten(jnp.concatenate([d_q, d_kv, d_logit], axis=-1))
    d_first = collect(wide(mm(d_all, w_first, NT)))

    grad_first, grad_output = outer_sums(
        (flatten(first), flatten(d_branch)), (0, 1), (d_all, flatten(gated)), sizes, 4)
    grad_gate, grad_up, grad_down = outer_sums((a2, cot), (0, 0, 1), (d_gate, d_up, hidden), sizes, 5)

    share = grad_first.shape[0]
    own_rows = lax.dynamic_slice_in_dim(w_first, place * share, share, 0).astype(f32)
    own_norm = jnp.sum(grad_first * own_rows, axis=1) / lax.dynamic_slice_in_dim(attn_norm, place * share, share, 0)
    grad_attn_norm = lax.dynamic_update_slice_in_dim(jnp.zeros((width,), f32), own_norm, place * share, 0)
    grad_attn_norm, grad_query_norm, grad_key_norm, grad_mlp_norm = lax.psum(
        (grad_attn_norm, d_qgain[0], d_kgain[0], grad_mlp_norm[0]), ("ctx", "uly", "tp"))

    unit = xs * inv_one
    inner = d_first * attn_norm
    grad_inputs = d_mid + inv_one * (inner - unit * jnp.mean(inner * unit, axis=-1, keepdims=True))
    return (
        outputs,
        grad_inputs,
        grad_attn_norm,
        grad_first[:, :q_cols],
        grad_first[:, q_cols:q_cols + kv_cols],
        grad_first[:, q_cols + kv_cols:n_main],
        grad_first[:, n_main:n_main + heads],
        grad_query_norm,
        grad_key_norm,
        grad_output.T,
        grad_mlp_norm,
        grad_gate,
        grad_up,
        grad_down.T,
    )


def solution(mesh):
    tokens = P(None, ("ctx", "uly", "tp"), None)
    column, line, whole = P(None, "tp"), P("tp", None), P()
    rows_split, cols_split = P(("ctx", "uly"), "tp"), P("tp", ("ctx", "uly"))
    return jax.shard_map(
        functools.partial(per_device, (mesh.shape["ctx"], mesh.shape["uly"])),
        mesh=mesh,
        in_specs=(
            tokens, whole, whole, column, column, column, column, whole, whole, line, whole, column, column, line,
            tokens,
        ),
        out_specs=(
            tokens, tokens, whole, rows_split, rows_split, rows_split, rows_split, whole, whole, cols_split, whole,
            rows_split, rows_split, cols_split,
        ),
        check_vma=False,
    )
```

```python
import functools
import math

import jax
import jax.numpy as jnp
from jax import lax
from jax.experimental import pallas as pl
from jax.experimental.pallas import tpu as pltpu
from jax.sharding import PartitionSpec as P

epsilon = 1e-06
rope_base = 1000000.0
log2e = 1.0 / math.log(2.0)
bf16 = jnp.bfloat16
f32 = jnp.float32
vmem_bytes = 61 * 1024 * 1024

MESH = pl.DeviceIdType.MESH
NT = (((1,), (1,)), ((), ()))
NN = (((1,), (0,)), ((), ()))
TN = (((0,), (0,)), ((), ()))


def mm(left, right, dims=NN):
    return lax.dot_general(left, right, dims, preferred_element_type=f32)


def params(**more):
    return pltpu.CompilerParams(vmem_limit_bytes=vmem_bytes, **more)


def cost(flops, moved, trans=0):
    return pl.CostEstimate(flops=int(flops), bytes_accessed=int(moved), transcendentals=int(trans))


def full(shape):
    return pl.BlockSpec(shape, lambda *_: (0,) * len(shape))


def rms_inverse(values):
    return lax.rsqrt(jnp.mean(values * values, axis=-1, keepdims=True) + epsilon)


def rope_tables(positions, head_dim):
    half = head_dim // 2
    frequency = rope_base ** (-(jnp.arange(half, dtype=f32) * 2.0 / head_dim))
    angles = positions.astype(f32)[:, None] * frequency[None, :]
    cosine, sine = jnp.cos(angles), jnp.sin(angles)
    return jnp.concatenate([cosine, cosine], 1), jnp.concatenate([-sine, sine], 1)


def project_kernel(heads, kv_heads, dim, scale, x_ref, w_ref, cos_ref, sin_ref, qg_ref, kg_ref,
                   q_ref, kv_ref, nq_ref, nk_ref, rq_ref, rk_ref, logit_ref):
    cosine, sine = cos_ref[...], sin_ref[...]
    raw = mm(x_ref[...], w_ref[...])

    def rope(unit, gain):
        scaled = unit * gain
        return scaled * cosine + pltpu.roll(scaled, dim // 2, 1) * sine

    for h in range(heads + kv_heads):
        values = raw[:, h * dim:(h + 1) * dim]
        inverse = rms_inverse(values)
        unit = values * inverse
        if h < heads:
            at = slice(h * dim, (h + 1) * dim)
            q_ref[:, at] = (rope(unit, qg_ref[...]) * (scale * log2e)).astype(bf16)
            nq_ref[:, at] = unit.astype(bf16)
            rq_ref[:, h:h + 1] = inverse
        else:
            g = h - heads
            at = slice(g * dim, (g + 1) * dim)
            kv_ref[:, at] = rope(unit, kg_ref[...]).astype(bf16)
            nk_ref[:, at] = unit.astype(bf16)
            rk_ref[:, g:g + 1] = inverse
    first = (heads + kv_heads) * dim
    kv_ref[:, kv_heads * dim:] = raw[:, first:first + kv_heads * dim].astype(bf16)
    first += kv_heads * dim
    logit_ref[...] = raw[:, first:first + heads].astype(bf16).astype(f32)


def project(x, w, tables, query_norm, key_norm, heads, kv_heads, scale, block=256):
    rows, width = x.shape
    dim = query_norm.shape[0]
    cosine, sine = tables
    block = min(block, cosine.shape[0])
    around = cosine.shape[0] // block
    kernel = functools.partial(project_kernel, heads, kv_heads, dim, scale)

    def by_row(cols):
        return pl.BlockSpec((block, cols), lambda i: (i, 0))

    table = pl.BlockSpec((block, dim), lambda i: (i % around, 0))
    shapes = [
        (heads * dim, bf16), (2 * kv_heads * dim, bf16), (heads * dim, bf16), (kv_heads * dim, bf16),
        (heads, f32), (kv_heads, f32), (heads, f32),
    ]
    return pl.pallas_call(
        kernel,
        grid=(rows // block,),
        in_specs=[by_row(width), full(w.shape), table, table, full((1, dim)), full((1, dim))],
        out_specs=[by_row(c) for c, _ in shapes],
        out_shape=[jax.ShapeDtypeStruct((rows, c), t) for c, t in shapes],
        compiler_params=params(),
        cost_estimate=cost(2 * rows * width * w.shape[1], 2 * (rows * width + w.size) + rows * 4096),
        name="project",
    )(x, w, cosine, sine, query_norm[None], key_norm[None])


def bounds_loop(bounds_ref, row, body):
    lo, full_lo, full_hi, hi = (bounds_ref[row, i] for i in range(4))
    lax.fori_loop(lo, full_lo, lambda j, c: body(j, True), None)
    lax.fori_loop(full_lo, full_hi, lambda j, c: body(j, False), None)
    lax.fori_loop(full_hi, hi, lambda j, c: body(j, True), None)


def attend_kernel(heads, kv_heads, dim, block, bounds_ref, q_ref, kv_ref, start_ref, pos_ref, logit_ref,
                  att_ref, gated_ref, lse_ref, q2_ref, acc_ref, sum_ref):
    row = pl.program_id(0)
    group = q_ref.shape[1]
    repeat = heads // kv_heads
    for h in range(kv_heads):
        for g in range(repeat):
            at = slice((h * repeat + g) * dim, (h * repeat + g + 1) * dim)
            q2_ref[g * group:(g + 1) * group, :] = q_ref[0, :, at]
        acc_ref[...] = jnp.zeros_like(acc_ref)
        sum_ref[...] = jnp.zeros_like(sum_ref)

        def body(j, masked):
            at = pl.ds(pl.multiple_of(j * block, block), block)
            keys = kv_ref[0, at, h * dim:(h + 1) * dim]
            values = kv_ref[0, at, (kv_heads + h) * dim:(kv_heads + h + 1) * dim]
            if masked:
                spot = j * block + lax.broadcasted_iota(jnp.int32, (group, block), 1)
                allowed = (spot >= start_ref[0]) & (spot <= pos_ref[...])
            for g in range(repeat):
                part = slice(g * group, (g + 1) * group)
                weight = jnp.exp2(mm(q2_ref[part, :], keys, NT))
                if masked:
                    weight = jnp.where(allowed, weight, 0.0)
                total = weight[:, :dim]
                for i in range(1, block // dim):
                    total = total + weight[:, i * dim:(i + 1) * dim]
                sum_ref[part, :] += total
                acc_ref[part, :] += mm(weight.astype(bf16), values)

        bounds_loop(bounds_ref, row, body)
        for g in range(repeat):
            part = slice(g * group, (g + 1) * group)
            n = h * repeat + g
            at = slice(n * dim, (n + 1) * dim)
            total = jnp.sum(sum_ref[part, :], axis=1, keepdims=True)
            attended = acc_ref[part, :] / total
            att_ref[0, :, at] = attended.astype(bf16)
            gated_ref[0, :, at] = (attended * jax.nn.sigmoid(logit_ref[0, :, n:n + 1])).astype(bf16)
            lse_ref[0, n:n + 1, :] = jnp.log2(jnp.sum(sum_ref[part, :].T, axis=0, keepdims=True))


def attend(q, kv, bounds, start_col, pos_col, logits, heads, kv_heads, dim, block):
    rows, group, width = q.shape
    total = kv.shape[1]
    repeat = heads // kv_heads

    def by_row(*shape):
        return pl.BlockSpec((1, *shape), lambda r, *_: (r, 0, 0))

    return pl.pallas_call(
        functools.partial(attend_kernel, heads, kv_heads, dim, block),
        grid_spec=pltpu.PrefetchScalarGridSpec(
            num_scalar_prefetch=1,
            grid=(rows,),
            in_specs=[
                by_row(group, width), by_row(total, kv.shape[2]), by_row(group, 1), full((group, 1)),
                by_row(group, heads),
            ],
            out_specs=[by_row(group, width), by_row(group, width), by_row(heads, group)],
            scratch_shapes=[
                pltpu.VMEM((repeat * group, dim), bf16),
                pltpu.VMEM((repeat * group, dim), f32),
                pltpu.VMEM((repeat * group, dim), f32),
            ],
        ),
        out_shape=[
            jax.ShapeDtypeStruct((rows, group, width), bf16),
            jax.ShapeDtypeStruct((rows, group, width), bf16),
            jax.ShapeDtypeStruct((rows, heads, group), f32),
        ],
        compiler_params=params(),
        cost_estimate=cost(
            2 * rows * heads * group * total * dim, 2 * kv.size + 6 * q.size, rows * heads * group * total // 2
        ),
        name="attend",
    )(bounds, q, kv, start_col, pos_col, logits)


def attend_back_kernel(heads, kv_heads, dim, block, scale, bounds_ref, q_ref, kv_ref, dgated_ref, att_ref,
                       logit_ref, logit_row_ref, lse_ref, start_ref, pos_ref, nq_ref, rq_ref, cos_ref, sin_ref,
                       gain_ref, dq_ref, dlogit_ref, dkv_ref, dgain_ref,
                       q2_ref, da2_ref, delta_ref, lse2_ref, dq2_ref):
    row = pl.program_id(0)
    group = q_ref.shape[1]
    repeat = heads // kv_heads
    cosine, sine, gain = cos_ref[...], sin_ref[...], gain_ref[...]

    @pl.when(row == 0)
    def _():
        dgain_ref[...] = jnp.zeros_like(dgain_ref)

    dkv_ref[...] = jnp.zeros_like(dkv_ref)
    for h in range(kv_heads):
        for g in range(repeat):
            n = h * repeat + g
            at = slice(n * dim, (n + 1) * dim)
            part = slice(g * group, (g + 1) * group)
            q2_ref[part, :] = q_ref[0, :, at]
            grad = dgated_ref[0, :, at].astype(f32)
            sigma = jax.nn.sigmoid(logit_ref[0, :, n:n + 1])
            da2_ref[part, :] = (grad * sigma).astype(bf16)
            dot = jnp.sum((grad * att_ref[0, :, at].astype(f32)).T, axis=0, keepdims=True)
            sigma_row = jax.nn.sigmoid(logit_row_ref[0, n:n + 1, :])
            dlogit_ref[0, n:n + 1, :] = dot * sigma_row * (1.0 - sigma_row)
            delta_ref[:, part] = dot * sigma_row
            lse2_ref[:, part] = lse_ref[0, n:n + 1, :]
        dq2_ref[...] = jnp.zeros_like(dq2_ref)

        def body(j, masked):
            at = pl.ds(pl.multiple_of(j * block, block), block)
            keys = kv_ref[0, at, h * dim:(h + 1) * dim]
            values = kv_ref[0, at, (kv_heads + h) * dim:(kv_heads + h + 1) * dim]
            if masked:
                spot = j * block + lax.broadcasted_iota(jnp.int32, (block, group), 0)
                allowed = (spot >= start_ref[0]) & (spot <= pos_ref[...])
            dk = jnp.zeros((block, dim), f32)
            dv = jnp.zeros((block, dim), f32)
            for g in range(repeat):
                part = slice(g * group, (g + 1) * group)
                weight = jnp.exp2(mm(keys, q2_ref[part, :], NT) - lse2_ref[:, part])
                if masked:
                    weight = jnp.where(allowed, weight, 0.0)
                dv += mm(weight.astype(bf16), da2_ref[part, :])
                dprob = mm(values, da2_ref[part, :], NT)
                dscore = (weight * (dprob - delta_ref[:, part])).astype(bf16)
                dk += mm(dscore, q2_ref[part, :])
                dq2_ref[part, :] += mm(dscore, keys, TN)
            dkv_ref[0, at, h * dim:(h + 1) * dim] = (dk * (1.0 / log2e)).astype(bf16)
            dkv_ref[0, at, (kv_heads + h) * dim:(kv_heads + h + 1) * dim] = dv.astype(bf16)

        bounds_loop(bounds_ref, row, body)
        for g in range(repeat):
            n = h * repeat + g
            at = slice(n * dim, (n + 1) * dim)
            part = slice(g * group, (g + 1) * group)
            turned = (dq2_ref[part, :] * scale).astype(bf16).astype(f32)
            back = turned * cosine - pltpu.roll(turned, dim // 2, 1) * sine
            unit = nq_ref[0, :, at].astype(f32)
            dgain_ref[...] += jnp.sum(back * unit, axis=0, keepdims=True)
            inner = back * gain
            mean = jnp.mean(inner * unit, axis=1, keepdims=True)
            dq_ref[0, :, at] = (rq_ref[0, :, n:n + 1] * (inner - unit * mean)).astype(bf16)


def attend_back(q, kv, dgated, att, logits, logit_rows, lse, bounds, start_row, pos_row, nq, rq, tables, gain,
                heads, kv_heads, dim, block, scale):
    rows, group, width = q.shape
    total = kv.shape[1]
    repeat = heads // kv_heads
    cosine, sine = tables

    def by_row(*shape):
        return pl.BlockSpec((1, *shape), lambda r, *_: (r, 0, 0))

    wide = by_row(group, width)
    return pl.pallas_call(
        functools.partial(attend_back_kernel, heads, kv_heads, dim, block, scale),
        grid_spec=pltpu.PrefetchScalarGridSpec(
            num_scalar_prefetch=1,
            grid=(rows,),
            in_specs=[
                wide, by_row(total, kv.shape[2]), wide, wide, by_row(group, heads), by_row(heads, group),
                by_row(heads, group), by_row(1, group), full((1, group)), wide, by_row(group, heads),
                full((group, dim)), full((group, dim)), full((1, dim)),
            ],
            out_specs=[wide, by_row(heads, group), by_row(total, kv.shape[2]), full((1, dim))],
            scratch_shapes=[
                pltpu.VMEM((repeat * group, dim), bf16),
                pltpu.VMEM((repeat * group, dim), bf16),
                pltpu.VMEM((1, repeat * group), f32),
                pltpu.VMEM((1, repeat * group), f32),
                pltpu.VMEM((repeat * group, dim), f32),
            ],
        ),
        out_shape=[
            jax.ShapeDtypeStruct((rows, group, width), bf16),
            jax.ShapeDtypeStruct((rows, heads, group), f32),
            jax.ShapeDtypeStruct(kv.shape, bf16),
            jax.ShapeDtypeStruct((1, dim), f32),
        ],
        compiler_params=params(),
        cost_estimate=cost(
            5 * rows * heads * group * total * dim, 4 * kv.size + 10 * q.size, rows * heads * group * total // 2
        ),
        name="attend_back",
    )(bounds, q, kv, dgated, att, logits, logit_rows, lse, start_row, pos_row, nq, rq, cosine, sine, gain[None])


def key_back_kernel(kv_heads, dim, dkv_ref, nk_ref, rk_ref, cos_ref, sin_ref, gain_ref, dk_ref, dgain_ref):
    @pl.when(pl.program_id(0) == 0)
    def _():
        dgain_ref[...] = jnp.zeros_like(dgain_ref)

    for h in range(kv_heads):
        at = slice(h * dim, (h + 1) * dim)
        turned = dkv_ref[0, :, at].astype(f32)
        back = turned * cos_ref[...] - pltpu.roll(turned, dim // 2, 1) * sin_ref[...]
        unit = nk_ref[0, :, at].astype(f32)
        dgain_ref[...] += jnp.sum(back * unit, axis=0, keepdims=True)
        inner = back * gain_ref[...]
        mean = jnp.mean(inner * unit, axis=1, keepdims=True)
        dk_ref[0, :, at] = (rk_ref[0, :, h:h + 1] * (inner - unit * mean)).astype(bf16)
    dk_ref[0, :, kv_heads * dim:] = dkv_ref[0, :, kv_heads * dim:]


def key_back(dkv, nk, rk, tables, gain, kv_heads, dim):
    rows, group, width = dkv.shape

    def by_row(*shape):
        return pl.BlockSpec((1, *shape), lambda r: (r, 0, 0))

    return pl.pallas_call(
        functools.partial(key_back_kernel, kv_heads, dim),
        grid=(rows,),
        in_specs=[
            by_row(group, width), by_row(group, kv_heads * dim), by_row(group, kv_heads), full((group, dim)),
            full((group, dim)), full((1, dim)),
        ],
        out_specs=[by_row(group, width), full((1, dim))],
        out_shape=[jax.ShapeDtypeStruct((rows, group, width), bf16), jax.ShapeDtypeStruct((1, dim), f32)],
        compiler_params=params(),
        cost_estimate=cost(20 * dkv.size, 6 * dkv.size),
        name="key_back",
    )(dkv, nk, rk, *tables, gain[None])


def line_barrier(n, me):
    barrier = pltpu.get_barrier_semaphore()
    for way in (1, -1):
        @pl.when((me + way >= 0) & (me + way < n))
        def _():
            pl.semaphore_signal(barrier, inc=1, device_id={"tp": jnp.clip(me + way, 0, n - 1)}, device_id_type=MESH)
    edge = (me == 0) | (me == n - 1)

    @pl.when(edge)
    def _():
        pl.semaphore_wait(barrier, 1)

    @pl.when(jnp.logical_not(edge))
    def _():
        pl.semaphore_wait(barrier, 2)


def line_and_plane_barrier(n, me, bits, n_uly):
    barrier = pltpu.get_barrier_semaphore()
    place = plane_place(n_uly)
    for way in (1, -1):
        @pl.when((me + way >= 0) & (me + way < n))
        def _():
            pl.semaphore_signal(barrier, inc=1, device_id={"tp": jnp.clip(me + way, 0, n - 1)}, device_id_type=MESH)
    for b in range(bits):
        pl.semaphore_signal(barrier, inc=1, device_id=plane_device(place ^ (1 << b), n_uly), device_id_type=MESH)
    edge = (me == 0) | (me == n - 1)

    @pl.when(edge)
    def _():
        pl.semaphore_wait(barrier, bits + 1)

    @pl.when(jnp.logical_not(edge))
    def _():
        pl.semaphore_wait(barrier, bits + 2)


class LineSum:
    def __init__(self, n, pieces, part_at, own, land_ref, sems, out_at=None):
        self.n, self.pieces, self.part_at, self.own, self.land, self.out_at = n, pieces, part_at, own, land_ref, out_at
        self.rs_send, self.rs_recv = sems[:2]
        if out_at:
            self.ag_send, self.ag_recv = sems[2:]
        self.me = lax.axis_index("tp")
        self.stages = [functools.partial(self.reduce_step, k) for k in range(1, n)] + [self.own_step]
        if out_at:
            self.stages += [functools.partial(self.spread_step, k) for k in range(2, n + 1)]

    def inside(self, place):
        return (place >= 0) & (place < self.n)

    def near(self, way):
        return {"tp": jnp.clip(self.me + way, 0, self.n - 1)}

    def reduce_copy(self, way, k, s, source):
        d = 0 if way == 1 else 1
        return pltpu.make_async_remote_copy(
            src_ref=source, dst_ref=self.land.at[d, k - 1, s], send_sem=self.rs_send.at[d, k - 1, s],
            recv_sem=self.rs_recv.at[d, k - 1, s], device_id=self.near(way), device_id_type=MESH)

    def spread_copy(self, way, k, s, owner):
        d = 0 if way == 1 else 1
        rows = self.out_at(jnp.clip(owner, 0, self.n - 1), s)
        return pltpu.make_async_remote_copy(
            src_ref=rows, dst_ref=rows, send_sem=self.ag_send.at[d, k - 1, s], recv_sem=self.ag_recv.at[d, k - 1, s],
            device_id=self.near(way), device_id_type=MESH)

    def reduce_step(self, k, s):
        for way in (1, -1):
            d = 0 if way == 1 else 1
            first = jnp.logical_not(self.inside(self.me - way))
            dest = self.me + way * (self.n - k)
            part = self.part_at(jnp.clip(dest, 0, self.n - 1), s)

            @pl.when(first & self.inside(dest))
            def _():
                self.reduce_copy(way, k, s, part).start()

            if k > 1:
                @pl.when(self.inside(self.me - way) & self.inside(dest))
                def _():
                    landed = self.land.at[d, k - 2, s]
                    self.reduce_copy(way, k - 1, s, landed).wait_recv()
                    landed[...] = (part[...].astype(f32) + landed[...].astype(f32)).astype(bf16)
                    self.reduce_copy(way, k, s, landed).start()

    def own_step(self, s):
        for way in (1, -1):
            d = 0 if way == 1 else 1
            landed = self.land.at[d, self.n - 2, s]

            @pl.when(self.inside(self.me - way))
            def _():
                self.reduce_copy(way, self.n - 1, s, landed).wait_recv()

            @pl.when(jnp.logical_not(self.inside(self.me - way)))
            def _():
                landed[...] = jnp.zeros_like(landed)

        total = self.part_at(self.me, s)[...].astype(f32)
        for d in range(2):
            total = total + self.land[d, self.n - 2, s].astype(f32)
        rows = self.own(s, total)
        if self.out_at:
            self.out_at(self.me, s)[...] = rows
            self.spread_step(1, s)

    def spread_step(self, k, s):
        for way in (1, -1):
            owner = self.me - way * (k - 1)
            if k > 1:
                @pl.when(self.inside(owner))
                def _():
                    self.spread_copy(way, k - 1, s, owner).wait_recv()
            if k < self.n:
                @pl.when(self.inside(owner) & self.inside(self.me + way))
                def _():
                    self.spread_copy(way, k, s, owner).start()

    def drain_reduce(self):
        for s in range(self.pieces):
            for way in (1, -1):
                for k in range(1, self.n):
                    @pl.when(self.inside(self.me + way) & self.inside(self.me + way * (self.n - k)))
                    def _():
                        self.reduce_copy(way, k, s, self.land.at[0, 0, s]).wait_send()

    def drain_spread(self):
        for s in range(self.pieces):
            for way in (1, -1):
                for k in range(1, self.n):
                    owner = self.me - way * (k - 1)

                    @pl.when(self.inside(owner) & self.inside(self.me + way))
                    def _():
                        self.spread_copy(way, k, s, owner).wait_send()

    def run(self, beside=()):
        beside, done = list(beside), 0
        slots = self.pieces * len(self.stages)
        for step in range(self.pieces + len(self.stages) - 1):
            for s in range(self.pieces):
                if 0 <= step - s < len(self.stages):
                    self.stages[step - s](s)
                    slots -= 1
                    until = len(beside) if slots == 0 else done + -(-(len(beside) - done) // (slots + 1))
                    for item in beside[done:until]:
                        item()
                    done = until
        self.drain_reduce()
        self.drain_spread()


def line_all_sum(n, seqs, rows, piece, finish, part_ref, out_ref, land_ref, sems, beside=()):
    cuts = [(q, c) for q in range(seqs) for c in range(rows // piece)]

    def at(ref):
        return lambda owner, s: ref.at[
            cuts[s][0], pl.ds(pl.multiple_of(owner * rows + cuts[s][1] * piece, piece), piece)]

    LineSum(n, len(cuts), at(part_ref), lambda s, total: finish(*cuts[s], total), land_ref, sems, at(out_ref)).run(
        beside)


def line_scratch(n, seqs, rows, piece, width):
    count = seqs * (rows // piece)
    return [
        pltpu.VMEM((2, n - 1, count, piece, width), bf16),
        pltpu.SemaphoreType.DMA((2, n - 1, count)), pltpu.SemaphoreType.DMA((2, n - 1, count)),
        pltpu.SemaphoreType.DMA((2, n - 1, count)), pltpu.SemaphoreType.DMA((2, n - 1, count)),
    ]


def norm_forward_kernel(n, seqs, rows, piece, part_ref, x_ref, gain_ref, out_ref, mid_ref, land_ref, *sems):
    def finish(q, c, total):
        at = slice(c * piece, (c + 1) * piece)
        mid = x_ref[q, at].astype(f32) + total
        mid_ref[q, at] = mid
        return (mid * rms_inverse(mid) * gain_ref[...]).astype(bf16)

    line_barrier(n, lax.axis_index("tp"))
    line_all_sum(n, seqs, rows, piece, finish, part_ref, out_ref, land_ref, sems)


def line_call(kernel, n, local, part, others, extra, collective_id, name):
    seqs, rows, width = local
    piece = min(32, rows)
    vm = pl.BlockSpec(memory_space=pltpu.VMEM)
    shapes = [jax.ShapeDtypeStruct(part.shape, bf16), jax.ShapeDtypeStruct(local, f32), *extra]
    return pl.pallas_call(
        functools.partial(kernel, n, seqs, rows, piece),
        in_specs=[vm] * (1 + len(others)),
        out_specs=[vm] * len(shapes),
        out_shape=shapes,
        scratch_shapes=line_scratch(n, seqs, rows, piece, width),
        compiler_params=params(collective_id=collective_id, has_side_effects=True),
        cost_estimate=cost(20 * part.size, 100_000_000),
        name=name,
    )(part, *others)


def plane_place(n_uly):
    return lax.axis_index("ctx") * n_uly + lax.axis_index("uly")


def plane_device(place, n_uly):
    return {"ctx": place // n_uly, "uly": lax.rem(place, n_uly)}


def plane_barrier(bits, me, n_uly):
    barrier = pltpu.get_barrier_semaphore()
    for b in range(bits):
        pl.semaphore_signal(barrier, inc=1, device_id=plane_device(me ^ (1 << b), n_uly), device_id_type=MESH)
    pl.semaphore_wait(barrier, bits)


def ways(bits):
    upper = list(range(1, bits))
    return upper, upper[::-1]


def span(order):
    out = [0]
    for b in order:
        out += [e | (1 << b) for e in out]
    return out


def plane_gather_kernel(bits, n_uly, own_ref, out_ref, copy_sem, send_sem, recv_sem):
    me = plane_place(n_uly)
    rows, half = own_ref.shape[1], own_ref.shape[2] // 2
    plane_barrier(bits, me, n_uly)
    orders = [w + [0] for w in ways(bits)]

    def block(place, d):
        return out_ref.at[:, pl.ds(pl.multiple_of(place * rows, rows), rows), pl.ds(d * half, half)]

    def copy(d, level, e):
        bit = orders[d][level]
        source = own_ref.at[:, :, pl.ds(d * half, half)] if e == 0 else block(me ^ e, d)
        return pltpu.make_async_remote_copy(
            src_ref=source, dst_ref=block(me ^ e, d), send_sem=send_sem.at[d, e | (1 << bit)],
            recv_sem=recv_sem.at[d, e | (1 << bit)], device_id=plane_device(me ^ (1 << bit), n_uly),
            device_id_type=MESH)

    own = [pltpu.make_async_copy(own_ref.at[:, :, pl.ds(d * half, half)], block(me, d), copy_sem.at[d]) for d in range(2)]
    for c in own:
        c.start()
    for level in range(bits):
        for d in range(2):
            for e in span(orders[d][:level]):
                if level > 0 and e >> orders[d][level - 1] & 1:
                    continue
                copy(d, level, e).start()
        for d in range(2):
            for e in span(orders[d][:level]):
                copy(d, level, e).wait_recv()
                if level + 1 < bits:
                    copy(d, level + 1, e | (1 << orders[d][level])).start()
    for d in range(2):
        own[d].wait()
        for level in range(bits):
            for e in span(orders[d][:level]):
                copy(d, level, e).wait_send()


def plane_gather(own, sizes, collective_id):
    n_ctx, n_uly = sizes
    count = n_ctx * n_uly
    bits = count.bit_length() - 1
    seqs, rows, width = own.shape
    if own.size * count * 2 > 12 << 20 or count != 1 << bits or bits < 2:
        return lax.all_gather(own, ("ctx", "uly"), axis=1, tiled=True)
    vm = pl.BlockSpec(memory_space=pltpu.VMEM)
    return pl.pallas_call(
        functools.partial(plane_gather_kernel, bits, n_uly),
        in_specs=[vm], out_specs=vm,
        out_shape=jax.ShapeDtypeStruct((seqs, rows * count, width), own.dtype),
        scratch_shapes=[pltpu.SemaphoreType.DMA((2,)), pltpu.SemaphoreType.DMA((2, count)), pltpu.SemaphoreType.DMA((2, count))],
        compiler_params=params(collective_id=collective_id, has_side_effects=True),
        cost_estimate=cost(0, 100_000_000),
        name="plane_gather",
    )(own)


class PlaneSum:
    def __init__(self, bits, n_uly, make, store, buf_ref, land_ref, send, recv):
        self.bits, self.n_uly, self.make, self.store = bits, n_uly, make, store
        self.buf, self.land, self.send, self.recv = buf_ref, land_ref, send, recv
        self.me = plane_place(n_uly)
        width = buf_ref.shape[-1]
        half = max(width // 256, 1) * 128
        self.parts = [(0, half), (half, width - half)]
        self.orders = ways(bits)

    @staticmethod
    def scratch(bits, rows, width):
        n = 1 << bits
        return [
            pltpu.VMEM((n, rows, width), bf16), pltpu.VMEM((n - 1, rows, width), bf16),
            pltpu.SemaphoreType.DMA((3, n)), pltpu.SemaphoreType.DMA((3, n)),
        ]

    def slot(self, e):
        return e

    def view(self, ref, i, d):
        return ref.at[(i, *[slice(None)] * (len(ref.shape) - 2), pl.ds(*self.parts[d]))]

    def first_copy(self, e):
        return pltpu.make_async_remote_copy(
            src_ref=self.buf.at[e], dst_ref=self.land.at[e - 1], send_sem=self.send.at[2, e],
            recv_sem=self.recv.at[2, e], device_id=plane_device(self.me ^ 1, self.n_uly), device_id_type=MESH)

    def copy(self, d, level, e):
        return pltpu.make_async_remote_copy(
            src_ref=self.view(self.buf, self.slot(e), d), dst_ref=self.view(self.land, e - 1, d),
            send_sem=self.send.at[d, e],
            recv_sem=self.recv.at[d, e],
            device_id=plane_device(self.me ^ (1 << self.orders[d][level]), self.n_uly), device_id_type=MESH)

    def sent(self, d, level):
        return [(1 << self.orders[d][level]) | e for e in span(self.orders[d][level + 1:])]

    def compute(self):
        n = 1 << self.bits
        for e in range(1, n, 2):
            self.buf[e] = self.make(self.me ^ e).astype(bf16)
            self.first_copy(e).start()
        for e in range(0, n, 2):
            self.buf[e] = self.make(self.me ^ e).astype(bf16)

    def pair(self):
        for e in range(1, 1 << self.bits, 2):
            self.first_copy(e).wait_recv()
            kept = self.slot(e - 1)
            self.buf[kept] = (self.buf[kept].astype(f32) + self.land[e - 1].astype(f32)).astype(bf16)

    def push(self, level):
        for d in range(2):
            for e in self.sent(d, level):
                self.copy(d, level, e).start()

    def pull(self, level):
        for d in range(2):
            for e in self.sent(d, level):
                kept = self.view(self.buf, self.slot(e ^ (1 << self.orders[d][level])), d)
                self.copy(d, level, e).wait_recv()
                total = kept[...].astype(f32) + self.view(self.land, e - 1, d)[...].astype(f32)
                if level == self.bits - 2:
                    self.store(pl.ds(*self.parts[d]), total)
                else:
                    kept[...] = total.astype(bf16)

    def finish(self):
        for e in range(1, 1 << self.bits, 2):
            self.first_copy(e).wait_send()
        for d in range(2):
            for level in range(self.bits - 1):
                for e in self.sent(d, level):
                    self.copy(d, level, e).wait_send()


def blocks_sum_kernel(bits, n_uly, parts_ref, out_ref, *scratch):
    me = plane_place(n_uly)
    plane_barrier(bits, me, n_uly)
    seqs, rows = out_ref.shape[0], out_ref.shape[1]

    def make(place):
        return parts_ref[:, pl.ds(pl.multiple_of(place * rows, rows), rows)].reshape(seqs * rows, -1)

    def store(at, total):
        out_ref[:, :, at] = total.reshape(seqs, rows, -1).astype(out_ref.dtype)

    job = PlaneSum(bits, n_uly, make, store, *scratch)
    job.compute()
    job.pair()
    for level in range(bits - 1):
        job.push(level)
        job.pull(level)
    job.finish()


def blocks_sum(parts, sizes, collective_id):
    n_ctx, n_uly = sizes
    count = n_ctx * n_uly
    bits = count.bit_length() - 1
    seqs, total, width = parts.shape
    rows = total // count
    if parts.size * 2 > 12 << 20 or count != 1 << bits or bits < 2:
        return lax.psum_scatter(parts, ("ctx", "uly"), scatter_dimension=1, tiled=True)
    vm = pl.BlockSpec(memory_space=pltpu.VMEM)
    return pl.pallas_call(
        functools.partial(blocks_sum_kernel, bits, n_uly),
        in_specs=[vm],
        out_specs=vm,
        out_shape=jax.ShapeDtypeStruct((seqs, rows, width), bf16),
        scratch_shapes=PlaneSum.scratch(bits, seqs * rows, width),
        compiler_params=params(collective_id=collective_id, has_side_effects=True),
        cost_estimate=cost(10 * parts.size, 100_000_000),
        name="blocks_sum",
    )(parts)


def outer_sums_kernel(bits, n_uly, use, *refs):
    count, kinds = len(use), max(use) + 1
    lefts, refs = [refs[k] for k in use], refs[kinds:]
    rights, outs, scratch = refs[:count], refs[count:2 * count], refs[2 * count:]
    plane_barrier(bits, plane_place(n_uly), n_uly)
    jobs = []
    for i in range(count):
        each = outs[i].shape[0]

        def make(place, i=i, each=each):
            left = lefts[i][:, pl.ds(pl.multiple_of(place * each, each), each)]
            return mm(left, rights[i][...], TN)

        def store(at, total, i=i):
            outs[i][:, at] = total

        jobs.append(PlaneSum(bits, n_uly, make, store, *scratch[4 * i:4 * i + 4]))
    last = bits - 2
    for i in range(count + last + 1):
        if i < count:
            jobs[i].compute()
            jobs[i].pair()
            jobs[i].push(0)
        for level in range(last + 1):
            j = i - 1 - level
            if 0 <= j < count:
                jobs[j].pull(level)
                if level < last:
                    jobs[j].push(level + 1)
                else:
                    jobs[j].finish()


def fits_plane(sizes, width):
    places = sizes[0] * sizes[1]
    return places & (places - 1) == 0 and places >= 4 and width // places % 128 == 0


def outer_sums(kinds, use, rights, sizes, collective_id):
    lefts = [kinds[k] for k in use]
    n_ctx, n_uly = sizes
    places = n_ctx * n_uly
    bits = places.bit_length() - 1
    count = len(lefts)
    if not fits_plane(sizes, lefts[0].shape[1]):
        return [
            lax.psum_scatter(mm(l, r, TN).astype(bf16), ("ctx", "uly"), scatter_dimension=0, tiled=True).astype(f32)
            for l, r in zip(lefts, rights)
        ]
    vm = pl.BlockSpec(memory_space=pltpu.VMEM)
    shapes = [(l.shape[1] // places, r.shape[1]) for l, r in zip(lefts, rights)]
    scratch = []
    for shape in shapes:
        scratch += PlaneSum.scratch(bits, *shape)
    work = sum(l.size * r.shape[1] for l, r in zip(lefts, rights))
    return pl.pallas_call(
        functools.partial(outer_sums_kernel, bits, n_uly, use),
        in_specs=[vm] * (len(kinds) + count),
        out_specs=[vm] * count,
        out_shape=[jax.ShapeDtypeStruct(s, f32) for s in shapes],
        scratch_shapes=scratch,
        compiler_params=pltpu.CompilerParams(
            collective_id=collective_id, has_side_effects=True, vmem_limit_bytes=vmem_bytes),
        cost_estimate=cost(2 * work, 200_000_000),
        name="outer_sums",
    )(*kinds, *rights)


def back_finish(piece, cot_ref, mid_ref, gain_ref, dmid_ref, dgain_ref):
    def finish(q, c, total):
        at = slice(c * piece, (c + 1) * piece)
        mid = mid_ref[q, at]
        inverse = rms_inverse(mid)
        unit = mid * inverse
        dgain_ref[...] += jnp.sum(total * unit, axis=0, keepdims=True)
        inner = total * gain_ref[...]
        mean = jnp.mean(inner * unit, axis=-1, keepdims=True)
        d_mid = cot_ref[q, at].astype(f32) + inverse * (inner - unit * mean)
        dmid_ref[q, at] = d_mid
        return d_mid.astype(bf16)

    return finish


def plain_back_kernel(n, seqs, rows, piece, part_ref, cot_ref, mid_ref, gain_ref, out_ref, dmid_ref, dgain_ref,
                      land_ref, *sems):
    dgain_ref[...] = jnp.zeros_like(dgain_ref)
    line_barrier(n, lax.axis_index("tp"))
    line_all_sum(n, seqs, rows, piece, back_finish(piece, cot_ref, mid_ref, gain_ref, dmid_ref, dgain_ref), part_ref,
                 out_ref, land_ref, sems)


class StreamedOuter:
    def __init__(self, jobs, each, left_slots, right_slots, left_sems, right_sems):
        self.jobs, self.each = jobs, each
        self.left, self.right, self.left_sems, self.right_sems = left_slots, right_slots, left_sems, right_sems

    def right_copy(self, i):
        _, right, half, _ = self.jobs[i]
        wide = self.right.shape[-1]
        return pltpu.make_async_copy(
            right.at[:, pl.ds(half * wide, wide)], self.right.at[i % 2], self.right_sems.at[i % 2])

    def left_copy(self, i, turn, place):
        at = pl.ds(pl.multiple_of(place * self.each, self.each), self.each)
        return pltpu.make_async_copy(self.jobs[i][0].at[:, at], self.left.at[turn % 2], self.left_sems.at[turn % 2])

    def product(self, i, turn, places, take):
        if turn == 0:
            if i == 0:
                self.right_copy(0).start()
                self.left_copy(0, 0, places[0]).start()
            self.right_copy(i).wait()
            if i + 1 < len(self.jobs):
                self.right_copy(i + 1).start()
        if turn + 1 < len(places):
            self.left_copy(i, turn + 1, places[turn + 1]).start()
        self.left_copy(i, turn, places[turn]).wait()
        value = mm(self.left[turn % 2], self.right[i % 2], TN)
        if turn + 1 == len(places) and i + 1 < len(self.jobs):
            self.left_copy(i + 1, 0, places[0]).start()
        take(value)


def norm_back_kernel(n, seqs, rows, piece, bits, n_uly, part_ref, cot_ref, mid_ref, gain_ref, a2_ref, cot_all_ref,
                     dgate_ref, dup_ref, hidden_ref, out_ref, dmid_ref, dgain_ref, ggate_ref, gup_ref, gdown_ref,
                     land_ref, rs_send, rs_recv, ag_send, ag_recv, left_slots, right_slots, left_sems, right_sems,
                     *plane_scratch):
    dgain_ref[...] = jnp.zeros_like(dgain_ref)

    finish = back_finish(piece, cot_ref, mid_ref, gain_ref, dmid_ref, dgain_ref)
    wide = right_slots.shape[-1]
    halves = ggate_ref.shape[1] // wide
    jobs = [
        (left, right, half, out)
        for left, right, out in (
            (a2_ref, dgate_ref, ggate_ref), (a2_ref, dup_ref, gup_ref), (cot_all_ref, hidden_ref, gdown_ref))
        for half in range(halves)
    ]
    streamed = StreamedOuter(jobs, ggate_ref.shape[0], left_slots, right_slots, left_sems, right_sems)
    sums = []
    for i, (_, _, half, out) in enumerate(jobs):
        def store(at, total, half=half, out=out):
            to = pl.ds(half * wide + at.start, at.size)
            if out is gdown_ref:
                out[to] = total.T
            else:
                out[:, to] = total

        buf = plane_scratch[i % 2]
        land, send, recv = plane_scratch[2 + 3 * i:5 + 3 * i]
        sums.append(PlaneSum(bits, n_uly, None, store, buf, land, send, recv))
    last = bits - 2

    order = list(range(1, 1 << bits, 2)) + list(range(0, 1 << bits, 2))
    beside = []
    for i in range(len(jobs) + last + 1):
        for level in range(last, -1, -1):
            j = i - 1 - level
            if 0 <= j < len(jobs):
                beside.append(functools.partial(sums[j].pull, level))
                beside.append(functools.partial(sums[j].push, level + 1) if level < last else sums[j].finish)
        if i < len(jobs):
            job = sums[i]

            def product(turn, i=i, job=job):
                def take(value):
                    job.buf[order[turn]] = value.astype(bf16)
                    if order[turn] % 2:
                        job.first_copy(order[turn]).start()

                streamed.product(i, turn, [job.me ^ e for e in order], take)

            beside += [functools.partial(product, turn) for turn in range(len(order))]
            beside += [job.pair, functools.partial(job.push, 0)]

    line_and_plane_barrier(n, lax.axis_index("tp"), bits, n_uly)
    line_all_sum(n, seqs, rows, piece, finish, part_ref, out_ref, land_ref, (rs_send, rs_recv, ag_send, ag_recv),
                 beside)


def norm_back(part, cotangent, middle, gain, a2, cot_all, d_gate, d_up, hidden, n, sizes, collective_id):
    n_ctx, n_uly = sizes
    places = n_ctx * n_uly
    bits = places.bit_length() - 1
    seqs, rows, width = cotangent.shape
    tokens, units = d_gate.shape
    each = width // places
    if not fits_plane(sizes, width) or units % 512:
        out, d_mid, dgain = line_call(
            plain_back_kernel, n, cotangent.shape, part, (cotangent, middle, gain[None]),
            (jax.ShapeDtypeStruct((1, width), f32),), collective_id, "norm_back")
        grads = outer_sums((a2, cot_all), (0, 0, 1), (d_gate, d_up, hidden), sizes, 0)
        return (out, d_mid, dgain, *grads[:2], grads[2].T)
    piece = min(64, rows)
    half = units // 2
    vm, anywhere = pl.BlockSpec(memory_space=pltpu.VMEM), pl.BlockSpec(memory_space=pl.ANY)
    shapes = [
        jax.ShapeDtypeStruct(part.shape, bf16), jax.ShapeDtypeStruct(cotangent.shape, f32),
        jax.ShapeDtypeStruct((1, width), f32), *[jax.ShapeDtypeStruct((each, units), f32)] * 2,
        jax.ShapeDtypeStruct((units, each), f32),
    ]
    plane_scratch = [PlaneSum.scratch(bits, each, half) for _ in range(6)]
    return pl.pallas_call(
        functools.partial(norm_back_kernel, n, seqs, rows, piece, bits, n_uly),
        in_specs=[vm] * 4 + [anywhere] * 5,
        out_specs=[vm] * len(shapes),
        out_shape=shapes,
        scratch_shapes=[
            *line_scratch(n, seqs, rows, piece, width),
            pltpu.VMEM((2, tokens, each), bf16), pltpu.VMEM((2, tokens, half), bf16),
            pltpu.SemaphoreType.DMA((2,)), pltpu.SemaphoreType.DMA((2,)),
            plane_scratch[0][0], plane_scratch[0][0],
            *[item for scratch in plane_scratch for item in scratch[1:]],
        ],
        compiler_params=pltpu.CompilerParams(
            collective_id=collective_id, has_side_effects=True, vmem_limit_bytes=vmem_bytes),
        cost_estimate=cost(6 * tokens * units * width, 250_000_000),
        name="norm_back",
    )(part, cotangent, middle, gain[None], a2, cot_all, d_gate, d_up, hidden)


class StoredSum(PlaneSum):
    def __init__(self, bits, n_uly, source, store, buf_ref, land_ref, send, recv, load):
        super().__init__(bits, n_uly, None, store, buf_ref, land_ref, send, recv)
        self.source, self.load = source, load

    @staticmethod
    def scratch(bits, *shape):
        n = 1 << bits
        return [
            pltpu.VMEM((n // 2, *shape), bf16), pltpu.VMEM((n - 1, *shape), bf16),
            pltpu.SemaphoreType.DMA((3, n)), pltpu.SemaphoreType.DMA((3, n)), pltpu.SemaphoreType.DMA((n // 2,)),
        ]

    def slot(self, e):
        return e // 2

    def first_copy(self, e):
        return pltpu.make_async_remote_copy(
            src_ref=self.source(self.me ^ e), dst_ref=self.land.at[e - 1], send_sem=self.send.at[2, e],
            recv_sem=self.recv.at[2, e], device_id=plane_device(self.me ^ 1, self.n_uly), device_id_type=MESH)

    def load_copy(self, e):
        return pltpu.make_async_copy(self.source(self.me ^ e), self.buf.at[e // 2], self.load.at[e // 2])

    def compute(self):
        for e in range(1, 1 << self.bits, 2):
            self.first_copy(e).start()
            self.load_copy(e - 1).start()

    def pair(self):
        for e in range(0, 1 << self.bits, 2):
            self.load_copy(e).wait()
        super().pair()


def all_barrier(n, bits, n_uly):
    barrier = pltpu.get_barrier_semaphore()
    me, place = lax.axis_index("tp"), plane_place(n_uly)
    for d in range(1, n):
        pl.semaphore_signal(barrier, inc=1, device_id={"tp": lax.rem(me + d, n)}, device_id_type=MESH)
    for b in range(bits):
        pl.semaphore_signal(barrier, inc=1, device_id=plane_device(place ^ (1 << b), n_uly), device_id_type=MESH)
    pl.semaphore_wait(barrier, n - 1 + bits)


def layer_back_kernel(
    n, bits, n_uly, heads, kv_heads, dim, dkv_ref, first_ref, dbranch_ref, dq_ref, dlogit_ref, nk_ref, rk_ref, cos_ref,
    sin_ref, kgain_ref, wq_ref, wk_ref, wv_ref, wg_ref, gated_ref, x_ref, gain_ref, dmid_ref, dqgain_ref, dmlp_ref, gin_ref, gq_ref, gk_ref,
    gv_ref, gh_ref, gout_ref, gattn_ref, gmlp_ref, gqn_ref, gkn_ref, all_ref, cut_ref, part_ref, sum_ref, line_land, rs_send, rs_recv, left_slots, left_sems,
    vec_ref, vec_land, vec_send, vec_recv, *plane_scratch,
):
    seqs, _, cut_count, piece, _ = dq_ref.shape
    rows, width = cut_count * piece, x_ref.shape[-1]
    group = n * rows
    cuts = [(q, c) for q in range(seqs) for c in range(cut_count)]
    q_cols, kv_cols = heads * dim, kv_heads * dim
    n_main = q_cols + 2 * kv_cols
    each = gq_ref.shape[0]
    place, line_me = plane_place(n_uly), lax.axis_index("tp")

    vec_ref[0] = jnp.zeros_like(vec_ref[0])
    vec_ref[0, :, width:2 * width] = dmlp_ref[...]
    vec_ref[0, :, 2 * width:2 * width + dim] = dqgain_ref[...]

    def row_at(q, t, c):
        return q * group + t * rows + c * piece

    def key_values(s):
        q, c = cuts[s]

        def store(at, total):
            sum_ref[:, :, at] = total.astype(bf16)

        return StoredSum(
            bits, n_uly, lambda at: dkv_ref.at[q, pl.ds(pl.multiple_of(at * n, n), n), c], store,
            *plane_scratch[5 * s:5 * s + 5])

    sums = [key_values(s) for s in range(len(cuts))]

    def turn(s):
        q, c = cuts[s]
        for t in range(n):
            at = slice(t * piece, (t + 1) * piece)
            cut_ref[at, :q_cols] = dq_ref[q, t, c]
            for h in range(kv_heads):
                turned = sum_ref[t, :, h * dim:(h + 1) * dim].astype(f32)
                back = turned * cos_ref[t, c] - pltpu.roll(turned, dim // 2, 1) * sin_ref[t, c]
                unit = nk_ref[q, t, c, :, h * dim:(h + 1) * dim].astype(f32)
                vec_ref[0, :, 2 * width + dim:] += jnp.sum(back * unit, axis=0, keepdims=True)
                inner = back * kgain_ref[...]
                mean = jnp.mean(inner * unit, axis=1, keepdims=True)
                cut_ref[at, q_cols + h * dim:q_cols + (h + 1) * dim] = (
                    rk_ref[q, t, c, :, h:h + 1] * (inner - unit * mean)).astype(bf16)
            cut_ref[at, q_cols + kv_cols:n_main] = sum_ref[t, :, kv_cols:]
            cut_ref[at, n_main:] = dlogit_ref[q, t, c]
        partial = mm(cut_ref[:, :q_cols], wq_ref[...], NT)
        partial += mm(cut_ref[:, q_cols:q_cols + kv_cols], wk_ref[...], NT)
        partial += mm(cut_ref[:, q_cols + kv_cols:n_main], wv_ref[...], NT)
        partial += mm(cut_ref[:, n_main:n_main + heads], wg_ref[...], NT)
        partial = partial.astype(bf16)
        for t in range(n):
            at = slice(t * piece, (t + 1) * piece)
            to = slice(row_at(q, t, c), row_at(q, t, c) + piece)
            part_ref[to] = partial[at]
            all_ref[to] = cut_ref[at]

    def part_at(owner, s):
        q, c = cuts[s]
        return part_ref.at[pl.ds(pl.multiple_of(row_at(q, owner, c), piece), piece)]

    def own(s, total):
        q, c = cuts[s]
        at = slice(c * piece, (c + 1) * piece)
        x = x_ref[q, at].astype(f32)
        inverse = rms_inverse(x)
        unit = x * inverse
        inner = total * gain_ref[...]
        mean = jnp.mean(inner * unit, axis=-1, keepdims=True)
        gin_ref[q, at] = dmid_ref[q, at] + inverse * (inner - unit * mean)

    line = LineSum(n, len(cuts), part_at, own, line_land, (rs_send, rs_recv))

    order = list(range(1, 1 << bits, 2)) + list(range(0, 1 << bits, 2))
    turns = [(dbranch_ref, e) for e in order] + [(first_ref, e) for e in order]

    def left_copy(i):
        source, e = turns[i]
        at = pl.ds(pl.multiple_of((place ^ e) * each, each), each)
        return pltpu.make_async_copy(source.at[:, at], left_slots.at[i % 2], left_sems.at[i % 2])

    def store_out(at, total):
        gout_ref[at] = total.T

    def store_first(at, total):
        first = 0
        for out in (gq_ref, gk_ref, gv_ref, gh_ref):
            lo, hi = max(first, at.start), min(first + out.shape[1], at.start + at.size)
            if lo < hi:
                out[:, lo - first:hi - first] = total[:, lo - at.start:hi - at.start]
            first += out.shape[1]

    scratch = plane_scratch[5 * len(cuts):]
    out_sum = PlaneSum(bits, n_uly, None, store_out, *scratch[:4])
    first_sum = PlaneSum(bits, n_uly, None, store_first, *scratch[4:])

    def product(i):
        e = turns[i][1]
        if i + 1 < len(turns):
            left_copy(i + 1).start()
        left_copy(i).wait()
        job = out_sum if i < len(order) else first_sum
        value = mm(left_slots[i % 2], gated_ref[...] if i < len(order) else all_ref[...], TN)
        job.buf[e] = value.astype(bf16)
        if e % 2:
            job.first_copy(e).start()
        if job is first_sum:
            at = pl.ds(pl.multiple_of((place ^ e) * each, each), each)
            lanes, first = jnp.zeros((each, 128), f32), 0
            for w_ref in (wq_ref, wk_ref, wv_ref):
                for k in range(0, w_ref.shape[1], 128):
                    lanes += value[:, first + k:first + k + 128] * w_ref[at, k:k + 128].astype(f32)
                first += w_ref.shape[1]
            total = jnp.sum(lanes.T, axis=0, keepdims=True)
            last = value[:, n_main:n_main + heads] * wg_ref[at].astype(f32)
            total += jnp.sum(last.T, axis=0, keepdims=True)
            vec_ref[0, :, at] = total / gain_ref[:, at]

    line_bits = n.bit_length() - 1
    steps = bits + line_bits

    def vec_copy(k):
        partner = plane_device(place ^ (1 << k), n_uly) if k < bits else {"tp": line_me ^ (1 << (k - bits))}
        return pltpu.make_async_remote_copy(
            src_ref=vec_ref.at[k], dst_ref=vec_land.at[k], send_sem=vec_send.at[k], recv_sem=vec_recv.at[k],
            device_id=partner, device_id_type=MESH)

    def vec_step(k):
        if k > 0:
            vec_copy(k - 1).wait_recv()
            vec_ref[k] = vec_ref[k - 1] + vec_land[k - 1]
        if k < steps:
            vec_copy(k).start()

    def levels(job):
        items = [job.pair, functools.partial(job.push, 0)]
        for level in range(bits - 1):
            items.append(functools.partial(job.pull, level))
            if level + 1 < bits - 1:
                items.append(functools.partial(job.push, level + 1))
        return items

    early = [functools.partial(product, i) for i in range(len(order))] + levels(out_sum)
    late = [functools.partial(product, i) for i in range(len(order), len(turns))]
    late += [first_sum.pair, functools.partial(first_sum.push, 0)]
    rest = levels(first_sum)[2:]
    for k in range(steps + 1):
        late.append(functools.partial(vec_step, k))
        if rest and k % 2:
            late.append(rest.pop(0))
    late += rest

    all_barrier(n, bits, n_uly)
    for job in sums:
        job.compute()
    left_copy(0).start()
    ready = 0
    for step in range(len(cuts) + bits - 1 + n - 1):
        if step < len(cuts):
            sums[step].pair()
            sums[step].push(0)
        for level in range(bits - 1):
            j = step - 1 - level
            if 0 <= j < len(cuts):
                sums[j].pull(level)
                if level + 1 < bits - 1:
                    sums[j].push(level + 1)
                else:
                    turn(j)
                    ready += 1
        for s in range(len(cuts)):
            stage = step - s - (bits - 1)
            if 0 <= stage < n:
                line.stages[stage](s)
                queue = early or (late if ready == len(cuts) else [])
                for item in queue[:3]:
                    item()
                del queue[:3]
    for item in early + late:
        item()
    line.drain_reduce()
    first = 0
    for out in (gattn_ref, gmlp_ref, gqn_ref, gkn_ref):
        out[...] = vec_ref[steps, :, first:first + out.shape[1]]
        first += out.shape[1]
    for k in range(steps):
        vec_copy(k).wait_send()
    for job in (*sums, out_sum, first_sum):
        job.finish()


def layer_back(d_kv, first, d_branch, d_q, d_logit, nk, rk, tables, key_norm, weights, gated, x, attn_norm, d_mid, d_qgain,
               d_mlp, n, sizes, heads, kv_heads, collective_id):
    n_ctx, n_uly = sizes
    places = n_ctx * n_uly
    bits = places.bit_length() - 1
    seqs, rows, width = x.shape
    group, dim = n * rows, key_norm.shape[0]
    piece = min(64, rows)
    cut_count = rows // piece
    each = width // places
    tokens = seqs * group
    wide = (heads + 2 * kv_heads) * dim + d_logit.shape[-1]
    small = 2 * width + 2 * dim
    kv_wide = d_kv.shape[-1]
    pieces = seqs * cut_count
    steps = bits + n.bit_length() - 1

    def tiles(values):
        return values.reshape(seqs, n, cut_count, piece, values.shape[-1])

    vm, anywhere = pl.BlockSpec(memory_space=pltpu.VMEM), pl.BlockSpec(memory_space=pl.ANY)
    plane_scratch = []
    for _ in range(pieces):
        plane_scratch += StoredSum.scratch(bits, n, piece, kv_wide)
    plane_scratch += PlaneSum.scratch(bits, each, heads * dim) + PlaneSum.scratch(bits, each, wide)
    shapes = [
        jax.ShapeDtypeStruct(shape, f32) for shape in (
            x.shape, (each, heads * dim), (each, kv_heads * dim), (each, kv_heads * dim), (each, heads),
            (heads * dim, each), (1, width), (1, width), (1, dim), (1, dim))
    ]
    line = line_scratch(n, seqs, rows, piece, width)
    return pl.pallas_call(
        functools.partial(layer_back_kernel, n, bits, n_uly, heads, kv_heads, dim),
        in_specs=[anywhere] * 3 + [vm] * 17,
        out_specs=[vm] * len(shapes),
        out_shape=shapes,
        scratch_shapes=[
            pltpu.VMEM((tokens, wide), bf16), pltpu.VMEM((n * piece, wide), bf16), pltpu.VMEM((tokens, width), bf16),
            pltpu.VMEM((n, piece, kv_wide), bf16), *line[:3],
            pltpu.VMEM((2, tokens, each), bf16), pltpu.SemaphoreType.DMA((2,)),
            pltpu.VMEM((steps + 1, 1, small), f32), pltpu.VMEM((steps, 1, small), f32),
            pltpu.SemaphoreType.DMA((steps,)), pltpu.SemaphoreType.DMA((steps,)),
            *plane_scratch,
        ],
        compiler_params=pltpu.CompilerParams(
            collective_id=collective_id, has_side_effects=True, vmem_limit_bytes=vmem_bytes),
        cost_estimate=cost(4 * tokens * width * wide, 250_000_000),
        name="layer_back",
    )(d_kv.reshape(seqs, places * n, cut_count, piece, kv_wide), first, d_branch, tiles(d_q), tiles(d_logit), tiles(nk),
      tiles(rk), *[t.reshape(n, cut_count, piece, dim) for t in tables], key_norm[None], *weights, gated, x,
      attn_norm[None], d_mid, d_qgain, d_mlp)


class LineSpread(LineSum):
    def __init__(self, n, pieces, own, out_at, sems):
        super().__init__(n, pieces, None, own, None, (None, None, *sems), out_at)
        self.stages = [self.own_step] + [functools.partial(self.spread_step, k) for k in range(2, n + 1)]

    def own_step(self, s):
        self.out_at(self.me, s)[...] = self.own(s)
        self.spread_step(1, s)


class PlaneSpread:
    def __init__(self, bits, n_uly, block, send, recv):
        self.bits, self.n_uly, self.block, self.send, self.recv = bits, n_uly, block, send, recv
        self.me = plane_place(n_uly)
        self.orders = [w + [0] for w in ways(bits)]

    def copy(self, d, level, e):
        bit = 1 << self.orders[d][level]
        block = self.block(self.me ^ e, d)
        return pltpu.make_async_remote_copy(
            src_ref=block, dst_ref=block, send_sem=self.send.at[d, e | bit], recv_sem=self.recv.at[d, e | bit],
            device_id=plane_device(self.me ^ bit, self.n_uly), device_id_type=MESH)

    def pass_on(self, d, first, e):
        for level in range(first, self.bits):
            self.copy(d, level, e).start()

    def begin(self):
        for d in range(2):
            self.pass_on(d, 0, 0)

    def take(self, level):
        for d in range(2):
            for e in span(self.orders[d][:level]):
                self.copy(d, level, e).wait_recv()
                self.pass_on(d, level + 1, e | (1 << self.orders[d][level]))

    def finish(self):
        for d in range(2):
            for level in range(self.bits):
                for e in span(self.orders[d][:level]):
                    self.copy(d, level, e).wait_send()


def layer_front_kernel(
    n, bits, n_uly, heads, kv_heads, dim, scale, x_ref, gain_ref, wq_ref, wk_ref, wv_ref, wg_ref, cos_ref, sin_ref,
    qg_ref, kg_ref, a1_ref, q_ref, kv_ref, nq_ref, nk_ref, rq_ref, rk_ref, logit_ref, ag_send, ag_recv, kv_send,
    kv_recv,
):
    seqs, _, cut_count, piece, width = a1_ref.shape
    cuts = [(q, c) for q in range(seqs) for c in range(cut_count)]
    place = plane_place(n_uly)
    tokens = n * piece
    half = kv_heads * dim

    def own(s):
        q, c = cuts[s]
        x = x_ref[q, c * piece:(c + 1) * piece].astype(f32)
        return (x * rms_inverse(x) * gain_ref[...]).astype(bf16)

    line = LineSpread(
        n, len(cuts), own, lambda owner, s: a1_ref.at[cuts[s][0], owner, cuts[s][1]], (ag_send, ag_recv))

    def keys(s):
        q, c = cuts[s]
        return PlaneSpread(
            bits, n_uly,
            lambda at, d: kv_ref.at[q, pl.ds(pl.multiple_of(at * n, n), n), c, :, pl.ds(d * half, half)],
            kv_send.at[s], kv_recv.at[s])

    spreads = [keys(s) for s in range(len(cuts))]

    def turn(s):
        q, c = cuts[s]
        a1 = a1_ref[q, :, c].reshape(tokens, width)
        cosine, sine = cos_ref[:, c].reshape(tokens, dim), sin_ref[:, c].reshape(tokens, dim)

        def tiles(values):
            return values.reshape(n, piece, values.shape[-1])

        def rope(unit, gain):
            scaled = unit * gain
            return scaled * cosine + pltpu.roll(scaled, dim // 2, 1) * sine

        mine = pl.ds(pl.multiple_of(place * n, n), n)
        raw = mm(a1, wk_ref[...])
        for h in range(kv_heads):
            at = slice(h * dim, (h + 1) * dim)
            values = raw[:, at]
            inverse = rms_inverse(values)
            unit = values * inverse
            kv_ref[q, mine, c, :, at] = tiles(rope(unit, kg_ref[...]).astype(bf16))
            nk_ref[q, :, c, :, at] = tiles(unit.astype(bf16))
            rk_ref[q, :, c, :, h:h + 1] = tiles(inverse)
        kv_ref[q, mine, c, :, half:] = tiles(mm(a1, wv_ref[...]).astype(bf16))
        spreads[s].begin()
        raw = mm(a1, wq_ref[...])
        for h in range(heads):
            at = slice(h * dim, (h + 1) * dim)
            values = raw[:, at]
            inverse = rms_inverse(values)
            unit = values * inverse
            q_ref[q, :, c, :, at] = tiles((rope(unit, qg_ref[...]) * (scale * log2e)).astype(bf16))
            nq_ref[q, :, c, :, at] = tiles(unit.astype(bf16))
            rq_ref[q, :, c, :, h:h + 1] = tiles(inverse)
        logit_ref[q, :, c] = tiles(mm(a1, wg_ref[...]).astype(bf16).astype(f32))

    line_and_plane_barrier(n, lax.axis_index("tp"), bits, n_uly)
    for step in range(len(cuts) + n - 1 + bits):
        for s in range(len(cuts)):
            stage = step - s
            if 0 <= stage < n:
                line.stages[stage](s)
                if stage == n - 1:
                    turn(s)
        for s in range(len(cuts)):
            level = step - s - n
            if 0 <= level < bits:
                spreads[s].take(level)
    line.drain_spread()
    for spread in spreads:
        spread.finish()


def layer_front(x, attn_norm, w_query, w_key, w_value, w_headgate, tables, query_norm, key_norm, n, sizes, scale,
                collective_id):
    n_ctx, n_uly = sizes
    places = n_ctx * n_uly
    bits = places.bit_length() - 1
    seqs, rows, width = x.shape
    dim = query_norm.shape[0]
    heads, kv_heads = w_query.shape[1] // dim, w_key.shape[1] // dim
    piece = min(64, rows)
    cut_count = rows // piece
    pieces = seqs * cut_count
    vm = pl.BlockSpec(memory_space=pltpu.VMEM)

    def tiled(devices, cols, kind):
        return jax.ShapeDtypeStruct((seqs, devices * n, cut_count, piece, cols), kind)

    shapes = [
        tiled(1, width, bf16), tiled(1, heads * dim, bf16), tiled(places, 2 * kv_heads * dim, bf16),
        tiled(1, heads * dim, bf16), tiled(1, kv_heads * dim, bf16), tiled(1, heads, f32), tiled(1, kv_heads, f32),
        tiled(1, heads, f32),
    ]
    line_sems = [pltpu.SemaphoreType.DMA((2, n - 1, pieces))] * 2
    plane_sems = [pltpu.SemaphoreType.DMA((pieces, 2, places))] * 2
    made = pl.pallas_call(
        functools.partial(layer_front_kernel, n, bits, n_uly, heads, kv_heads, dim, scale),
        in_specs=[vm] * 10,
        out_specs=[vm] * len(shapes),
        out_shape=shapes,
        scratch_shapes=[*line_sems, *plane_sems],
        compiler_params=params(collective_id=collective_id, has_side_effects=True),
        cost_estimate=cost(2 * seqs * n * rows * width * 1024, 200_000_000),
        name="layer_front",
    )(x, attn_norm[None], w_query, w_key, w_value, w_headgate,
      *[t.reshape(n, cut_count, piece, dim) for t in tables], query_norm[None], key_norm[None])
    return [m.reshape(seqs, -1, m.shape[-1]) for m in made]


def flatten(values):
    return values.reshape(-1, values.shape[-1])


def spread(values):
    return lax.all_gather(values.astype(bf16), "tp", axis=1, tiled=True)


def collect(values):
    return lax.psum_scatter(values.astype(bf16), "tp", scatter_dimension=1, tiled=True).astype(f32)


def per_device(sizes, inputs, doc_ids, attn_norm, w_query, w_key, w_value, w_headgate, query_norm, key_norm, w_output,
               mlp_norm, w_gate, w_up, w_down, cotangent):
    n_tensor = lax.axis_size("tp")
    n_uly = sizes[1]
    seqs, rows, width = inputs.shape
    group = rows * n_tensor
    dim = query_norm.shape[0]
    heads = w_query.shape[1] // dim
    kv_heads = w_key.shape[1] // dim
    scale = dim ** (-0.5)
    plane = ("ctx", "uly")
    place = lax.axis_index("ctx") * n_uly + lax.axis_index("uly")
    block_start = place * group
    positions = block_start + jnp.arange(group, dtype=jnp.int32)
    tables = lax.optimization_barrier(rope_tables(positions, dim))
    block = min(512, group)

    def wide(values):
        return values.reshape(seqs, group, -1)

    query_doc = lax.dynamic_slice_in_dim(doc_ids, block_start, group, 1)
    start = positions[None, :]
    for d in range(4):
        first_of = jnp.sum(((doc_ids >= 0) & (doc_ids < d)).astype(jnp.int32), axis=1)
        start = jnp.where(query_doc == d, first_of[:, None], start)
    lowest, highest = jnp.min(start, axis=1), jnp.max(start, axis=1)
    hi = jnp.full_like(lowest, (block_start + group + block - 1) // block)
    lo = lowest // block
    full_lo = jnp.clip((highest + block - 1) // block, lo, hi)
    full_hi = jnp.clip(jnp.full_like(lowest, (block_start + 1) // block), full_lo, hi)
    bounds = jnp.stack([lo, full_lo, full_hi, hi], axis=1)

    pad = 128 - heads
    w_first = jnp.concatenate([w_query, w_key, w_value, jnp.pad(w_headgate, ((0, 0), (0, pad)))], axis=1)
    q_cols, kv_cols = heads * dim, kv_heads * dim
    n_main = q_cols + 2 * kv_cols

    if fits_plane(sizes, width):
        first, q, kv, nq, nk, rq, rk, logits = layer_front(
            inputs, attn_norm, w_query, w_key, w_value, w_headgate, tables, query_norm, key_norm, n_tensor, sizes, scale,
            0)
    else:
        xs = inputs.astype(f32)
        inv_one = rms_inverse(xs)
        first = spread(xs * inv_one * attn_norm)
        q, kv, nq, nk, rq, rk, logits = (
            wide(m) for m in project(flatten(first), w_first, tables, query_norm, key_norm, heads, kv_heads, scale))
        kv = plane_gather(kv, sizes, 0)
    near = (seqs + 1) // 2
    early_cot, kv = lax.optimization_barrier((cotangent[:near], kv))
    cots = [spread(early_cot)]
    att, gated, lse = attend(q, kv, bounds, start[:, :, None], positions[:, None], logits, heads, kv_heads, dim, block)

    local = inputs.shape
    part, cots = lax.optimization_barrier((wide(mm(flatten(gated), w_output).astype(bf16)), cots))
    second, middle = line_call(
        norm_forward_kernel, n_tensor, local, part,
        (inputs, mlp_norm[None]), (), 1, "norm_forward")

    if near < seqs:
        late_cot, second = lax.optimization_barrier((cotangent[near:], second))
        cots.append(spread(late_cot))
    a2 = flatten(second)
    gate, up = mm(a2, w_gate), mm(a2, w_up)
    sig = jax.nn.sigmoid(gate)
    silu = gate * sig
    hidden = (silu * up).astype(bf16)
    made, cots = lax.optimization_barrier((wide(mm(hidden, w_down).astype(bf16)), cots))
    outs = [collect(made[:near])]
    cot = flatten(jnp.concatenate(cots, axis=0))
    d_hidden = mm(cot, w_down, NT)
    d_gate = (d_hidden * up * sig * (1.0 + gate * (1.0 - sig))).astype(bf16)
    d_up = (d_hidden * silu).astype(bf16)
    d_second = (mm(d_gate, w_gate, NT) + mm(d_up, w_up, NT)).astype(bf16)
    d_branch, d_mid, grad_mlp_norm, grad_gate, grad_up, grad_down = norm_back(
        wide(d_second), cotangent, middle, mlp_norm, a2, cot, d_gate, d_up, hidden, n_tensor, sizes, 2)

    if near < seqs:
        late_made, d_branch = lax.optimization_barrier((made[near:], d_branch))
        outs.append(collect(late_made))
    outputs = (middle + jnp.concatenate(outs, axis=0)).astype(bf16)
    d_gated = wide(mm(flatten(d_branch), w_output, NT).astype(bf16))
    d_q, d_logit, d_kv, d_qgain = attend_back(
        q, kv, d_gated, att, logits, logits.transpose(0, 2, 1), lse, bounds, start[:, None, :], positions[None, :], nq,
        rq, tables, query_norm, heads, kv_heads, dim, block, scale)
    d_logit = jnp.pad(d_logit.astype(bf16).transpose(0, 2, 1), ((0, 0), (0, 0), (0, pad)))
    if fits_plane(sizes, width):
        grad_inputs, *grads = layer_back(
            d_kv, flatten(first), flatten(d_branch), d_q, d_logit, nk, rk, tables, key_norm,
            (w_query, w_key, w_value, w_headgate), flatten(gated), inputs, attn_norm, d_mid, d_qgain, grad_mlp_norm, n_tensor, sizes, heads, kv_heads, 3)
        grad_query, grad_key, grad_value, grad_headgate, grad_output = grads[:5]
        grad_attn_norm, grad_mlp_norm, grad_query_norm, grad_key_norm = (g[0] for g in grads[5:])
    else:
        d_kv = blocks_sum(d_kv, sizes, 3)
        d_kv, d_kgain = key_back(d_kv, nk, rk, tables, key_norm, kv_heads, dim)
        d_all = flatten(jnp.concatenate([d_q, d_kv, d_logit], axis=-1))
        d_first = collect(wide(mm(d_all, w_first, NT)))

        grad_first, grad_output = outer_sums(
            (flatten(first), flatten(d_branch)), (0, 1), (d_all, flatten(gated)), sizes, 4)

        share = grad_first.shape[0]
        own_rows = lax.dynamic_slice_in_dim(w_first, place * share, share, 0).astype(f32)
        own_norm = jnp.sum(grad_first * own_rows, axis=1) / lax.dynamic_slice_in_dim(attn_norm, place * share, share, 0)
        grad_attn_norm = lax.dynamic_update_slice_in_dim(jnp.zeros((width,), f32), own_norm, place * share, 0)
        grad_attn_norm, grad_query_norm, grad_key_norm, grad_mlp_norm = lax.psum(
            (grad_attn_norm, d_qgain[0], d_kgain[0], grad_mlp_norm[0]), ("ctx", "uly", "tp"))

        unit = xs * inv_one
        inner = d_first * attn_norm
        grad_inputs = d_mid + inv_one * (inner - unit * jnp.mean(inner * unit, axis=-1, keepdims=True))
        grad_query, grad_key = grad_first[:, :q_cols], grad_first[:, q_cols:q_cols + kv_cols]
        grad_value, grad_headgate = grad_first[:, q_cols + kv_cols:n_main], grad_first[:, n_main:n_main + heads]
        grad_output = grad_output.T
    return (
        outputs,
        grad_inputs,
        grad_attn_norm,
        grad_query,
        grad_key,
        grad_value,
        grad_headgate,
        grad_query_norm,
        grad_key_norm,
        grad_output,
        grad_mlp_norm,
        grad_gate,
        grad_up,
        grad_down,
    )


def solution(mesh):
    tokens = P(None, ("ctx", "uly", "tp"), None)
    column, line, whole = P(None, "tp"), P("tp", None), P()
    rows_split, cols_split = P(("ctx", "uly"), "tp"), P("tp", ("ctx", "uly"))
    return jax.shard_map(
        functools.partial(per_device, (mesh.shape["ctx"], mesh.shape["uly"])),
        mesh=mesh,
        in_specs=(
            tokens, whole, whole, column, column, column, column, whole, whole, line, whole, column, column, line,
            tokens,
        ),
        out_specs=(
            tokens, tokens, whole, rows_split, rows_split, rows_split, rows_split, whole, whole, cols_split, whole,
            rows_split, rows_split, cols_split,
        ),
        check_vma=False,
    )
```

```python
import functools
import math

import jax
import jax.numpy as jnp
from jax import lax
from jax.experimental import pallas as pl
from jax.experimental.pallas import tpu as pltpu
from jax.sharding import PartitionSpec as P

epsilon = 1e-06
rope_base = 1000000.0
log2e = 1.0 / math.log(2.0)
bf16 = jnp.bfloat16
f32 = jnp.float32
back_quiet = (0, 2)
back_piece = 32
tail_piece = 64
tail_items = 3
vmem_bytes = 61 * 1024 * 1024

MESH = pl.DeviceIdType.MESH
NT = (((1,), (1,)), ((), ()))
NN = (((1,), (0,)), ((), ()))
TN = (((0,), (0,)), ((), ()))


def mm(left, right, dims=NN):
    return lax.dot_general(left, right, dims, preferred_element_type=f32)


def params(**more):
    return pltpu.CompilerParams(vmem_limit_bytes=vmem_bytes, **more)


def cost(flops, moved, trans=0):
    return pl.CostEstimate(flops=int(flops), bytes_accessed=int(moved), transcendentals=int(trans))


def full(shape):
    return pl.BlockSpec(shape, lambda *_: (0,) * len(shape))


def rms_inverse(values):
    return lax.rsqrt(jnp.mean(values * values, axis=-1, keepdims=True) + epsilon)


def rope_tables(positions, head_dim):
    half = head_dim // 2
    frequency = rope_base ** (-(jnp.arange(half, dtype=f32) * 2.0 / head_dim))
    angles = positions.astype(f32)[:, None] * frequency[None, :]
    cosine, sine = jnp.cos(angles), jnp.sin(angles)
    return jnp.concatenate([cosine, cosine], 1), jnp.concatenate([-sine, sine], 1)


def project_kernel(heads, kv_heads, dim, scale, x_ref, w_ref, cos_ref, sin_ref, qg_ref, kg_ref,
                   q_ref, kv_ref, nq_ref, nk_ref, rq_ref, rk_ref, logit_ref):
    cosine, sine = cos_ref[...], sin_ref[...]
    raw = mm(x_ref[...], w_ref[...])

    def rope(unit, gain):
        scaled = unit * gain
        return scaled * cosine + pltpu.roll(scaled, dim // 2, 1) * sine

    for h in range(heads + kv_heads):
        values = raw[:, h * dim:(h + 1) * dim]
        inverse = rms_inverse(values)
        unit = values * inverse
        if h < heads:
            at = slice(h * dim, (h + 1) * dim)
            q_ref[:, at] = (rope(unit, qg_ref[...]) * (scale * log2e)).astype(bf16)
            nq_ref[:, at] = unit.astype(bf16)
            rq_ref[:, h:h + 1] = inverse
        else:
            g = h - heads
            at = slice(g * dim, (g + 1) * dim)
            kv_ref[:, at] = rope(unit, kg_ref[...]).astype(bf16)
            nk_ref[:, at] = unit.astype(bf16)
            rk_ref[:, g:g + 1] = inverse
    first = (heads + kv_heads) * dim
    kv_ref[:, kv_heads * dim:] = raw[:, first:first + kv_heads * dim].astype(bf16)
    first += kv_heads * dim
    logit_ref[...] = raw[:, first:first + heads].astype(bf16).astype(f32)


def project(x, w, tables, query_norm, key_norm, heads, kv_heads, scale, block=256):
    rows, width = x.shape
    dim = query_norm.shape[0]
    cosine, sine = tables
    block = min(block, cosine.shape[0])
    around = cosine.shape[0] // block
    kernel = functools.partial(project_kernel, heads, kv_heads, dim, scale)

    def by_row(cols):
        return pl.BlockSpec((block, cols), lambda i: (i, 0))

    table = pl.BlockSpec((block, dim), lambda i: (i % around, 0))
    shapes = [
        (heads * dim, bf16), (2 * kv_heads * dim, bf16), (heads * dim, bf16), (kv_heads * dim, bf16),
        (heads, f32), (kv_heads, f32), (heads, f32),
    ]
    return pl.pallas_call(
        kernel,
        grid=(rows // block,),
        in_specs=[by_row(width), full(w.shape), table, table, full((1, dim)), full((1, dim))],
        out_specs=[by_row(c) for c, _ in shapes],
        out_shape=[jax.ShapeDtypeStruct((rows, c), t) for c, t in shapes],
        compiler_params=params(),
        cost_estimate=cost(2 * rows * width * w.shape[1], 2 * (rows * width + w.size) + rows * 4096),
        name="project",
    )(x, w, cosine, sine, query_norm[None], key_norm[None])


def bounds_loop(bounds_ref, row, body):
    lo, full_lo, full_hi, hi = (bounds_ref[row, i] for i in range(4))
    lax.fori_loop(lo, full_lo, lambda j, c: body(j, True), None)
    lax.fori_loop(full_lo, full_hi, lambda j, c: body(j, False), None)
    lax.fori_loop(full_hi, hi, lambda j, c: body(j, True), None)


def attend_kernel(heads, kv_heads, dim, block, bounds_ref, q_ref, kv_ref, start_ref, pos_ref, logit_ref,
                  att_ref, gated_ref, lse_ref, q2_ref, acc_ref, sum_ref):
    row = pl.program_id(0)
    group = q_ref.shape[1]
    repeat = heads // kv_heads
    for h in range(kv_heads):
        for g in range(repeat):
            at = slice((h * repeat + g) * dim, (h * repeat + g + 1) * dim)
            q2_ref[g * group:(g + 1) * group, :] = q_ref[0, :, at]
        acc_ref[...] = jnp.zeros_like(acc_ref)
        sum_ref[...] = jnp.zeros_like(sum_ref)

        def body(j, masked):
            at = pl.ds(pl.multiple_of(j * block, block), block)
            keys = kv_ref[0, at, h * dim:(h + 1) * dim]
            values = kv_ref[0, at, (kv_heads + h) * dim:(kv_heads + h + 1) * dim]
            if masked:
                spot = j * block + lax.broadcasted_iota(jnp.int32, (group, block), 1)
                allowed = (spot >= start_ref[0]) & (spot <= pos_ref[...])
            for g in range(repeat):
                part = slice(g * group, (g + 1) * group)
                weight = jnp.exp2(mm(q2_ref[part, :], keys, NT))
                if masked:
                    weight = jnp.where(allowed, weight, 0.0)
                total = weight[:, :dim]
                for i in range(1, block // dim):
                    total = total + weight[:, i * dim:(i + 1) * dim]
                sum_ref[part, :] += total
                acc_ref[part, :] += mm(weight.astype(bf16), values)

        bounds_loop(bounds_ref, row, body)
        for g in range(repeat):
            part = slice(g * group, (g + 1) * group)
            n = h * repeat + g
            at = slice(n * dim, (n + 1) * dim)
            total = jnp.sum(sum_ref[part, :], axis=1, keepdims=True)
            attended = acc_ref[part, :] / total
            att_ref[0, :, at] = attended.astype(bf16)
            gated_ref[0, :, at] = (attended * jax.nn.sigmoid(logit_ref[0, :, n:n + 1])).astype(bf16)
            lse_ref[0, n:n + 1, :] = jnp.log2(jnp.sum(sum_ref[part, :].T, axis=0, keepdims=True))


def attend(q, kv, bounds, start_col, pos_col, logits, heads, kv_heads, dim, block):
    rows, group, width = q.shape
    total = kv.shape[1]
    repeat = heads // kv_heads

    def by_row(*shape):
        return pl.BlockSpec((1, *shape), lambda r, *_: (r, 0, 0))

    return pl.pallas_call(
        functools.partial(attend_kernel, heads, kv_heads, dim, block),
        grid_spec=pltpu.PrefetchScalarGridSpec(
            num_scalar_prefetch=1,
            grid=(rows,),
            in_specs=[
                by_row(group, width), by_row(total, kv.shape[2]), by_row(group, 1), full((group, 1)),
                by_row(group, heads),
            ],
            out_specs=[by_row(group, width), by_row(group, width), by_row(heads, group)],
            scratch_shapes=[
                pltpu.VMEM((repeat * group, dim), bf16),
                pltpu.VMEM((repeat * group, dim), f32),
                pltpu.VMEM((repeat * group, dim), f32),
            ],
        ),
        out_shape=[
            jax.ShapeDtypeStruct((rows, group, width), bf16),
            jax.ShapeDtypeStruct((rows, group, width), bf16),
            jax.ShapeDtypeStruct((rows, heads, group), f32),
        ],
        compiler_params=params(),
        cost_estimate=cost(
            2 * rows * heads * group * total * dim, 2 * kv.size + 6 * q.size, rows * heads * group * total // 2
        ),
        name="attend",
    )(bounds, q, kv, start_col, pos_col, logits)


def attend_back_kernel(heads, kv_heads, dim, block, scale, bounds_ref, q_ref, kv_ref, dgated_ref, att_ref,
                       logit_ref, logit_row_ref, lse_ref, start_ref, pos_ref, nq_ref, rq_ref, cos_ref, sin_ref,
                       gain_ref, ggate_ref, gup_ref, gdown_ref, dq_ref, dlogit_ref, dkv_ref, dgain_ref, ggate_out,
                       gup_out, gdown_out, q2_ref, da2_ref, delta_ref, lse2_ref, dq2_ref, *moved):
    row = pl.program_id(0)
    slots, move_sems = moved[:3], moved[3]
    takes = [
        pltpu.make_async_copy(source, slot, move_sems.at[0, i])
        for i, (source, slot) in enumerate(zip((ggate_ref, gup_ref, gdown_ref), slots))
    ]
    gives = [
        pltpu.make_async_copy(slot, target, move_sems.at[1, i])
        for i, (slot, target) in enumerate(zip(slots, (ggate_out, gup_out, gdown_out)))
    ]

    @pl.when(row == 0)
    def _():
        for move in takes:
            move.start()

    group = q_ref.shape[1]
    repeat = heads // kv_heads
    cosine, sine, gain = cos_ref[...], sin_ref[...], gain_ref[...]

    @pl.when(row == 0)
    def _():
        dgain_ref[...] = jnp.zeros_like(dgain_ref)

    dkv_ref[...] = jnp.zeros_like(dkv_ref)
    for h in range(kv_heads):
        for g in range(repeat):
            n = h * repeat + g
            at = slice(n * dim, (n + 1) * dim)
            part = slice(g * group, (g + 1) * group)
            q2_ref[part, :] = q_ref[0, :, at]
            grad = dgated_ref[0, :, at].astype(f32)
            sigma = jax.nn.sigmoid(logit_ref[0, :, n:n + 1])
            da2_ref[part, :] = (grad * sigma).astype(bf16)
            dot = jnp.sum((grad * att_ref[0, :, at].astype(f32)).T, axis=0, keepdims=True)
            sigma_row = jax.nn.sigmoid(logit_row_ref[0, n:n + 1, :])
            dlogit_ref[0, n:n + 1, :] = dot * sigma_row * (1.0 - sigma_row)
            delta_ref[:, part] = dot * sigma_row
            lse2_ref[:, part] = lse_ref[0, n:n + 1, :]
        dq2_ref[...] = jnp.zeros_like(dq2_ref)

        def body(j, masked):
            at = pl.ds(pl.multiple_of(j * block, block), block)
            keys = kv_ref[0, at, h * dim:(h + 1) * dim]
            values = kv_ref[0, at, (kv_heads + h) * dim:(kv_heads + h + 1) * dim]
            if masked:
                spot = j * block + lax.broadcasted_iota(jnp.int32, (block, group), 0)
                allowed = (spot >= start_ref[0]) & (spot <= pos_ref[...])
            dk = jnp.zeros((block, dim), f32)
            dv = jnp.zeros((block, dim), f32)
            for g in range(repeat):
                part = slice(g * group, (g + 1) * group)
                weight = jnp.exp2(mm(keys, q2_ref[part, :], NT) - lse2_ref[:, part])
                if masked:
                    weight = jnp.where(allowed, weight, 0.0)
                dv += mm(weight.astype(bf16), da2_ref[part, :])
                dprob = mm(values, da2_ref[part, :], NT)
                dscore = (weight * (dprob - delta_ref[:, part])).astype(bf16)
                dk += mm(dscore, q2_ref[part, :])
                dq2_ref[part, :] += mm(dscore, keys, TN)
            dkv_ref[0, at, h * dim:(h + 1) * dim] = (dk * (1.0 / log2e)).astype(bf16)
            dkv_ref[0, at, (kv_heads + h) * dim:(kv_heads + h + 1) * dim] = dv.astype(bf16)

        bounds_loop(bounds_ref, row, body)
        for g in range(repeat):
            n = h * repeat + g
            at = slice(n * dim, (n + 1) * dim)
            part = slice(g * group, (g + 1) * group)
            turned = (dq2_ref[part, :] * scale).astype(bf16).astype(f32)
            back = turned * cosine - pltpu.roll(turned, dim // 2, 1) * sine
            unit = nq_ref[0, :, at].astype(f32)
            dgain_ref[...] += jnp.sum(back * unit, axis=0, keepdims=True)
            inner = back * gain
            mean = jnp.mean(inner * unit, axis=1, keepdims=True)
            dq_ref[0, :, at] = (rq_ref[0, :, n:n + 1] * (inner - unit * mean)).astype(bf16)

    @pl.when(row == 0)
    def _():
        for take, give in zip(takes, gives):
            take.wait()
            give.start()

    @pl.when(row == pl.num_programs(0) - 1)
    def _():
        for give in gives:
            give.wait()


def attend_back(q, kv, dgated, att, logits, logit_rows, lse, bounds, start_row, pos_row, nq, rq, tables, gain, moved,
                heads, kv_heads, dim, block, scale):
    rows, group, width = q.shape
    total = kv.shape[1]
    repeat = heads // kv_heads
    cosine, sine = tables

    def by_row(*shape):
        return pl.BlockSpec((1, *shape), lambda r, *_: (r, 0, 0))

    wide = by_row(group, width)
    return pl.pallas_call(
        functools.partial(attend_back_kernel, heads, kv_heads, dim, block, scale),
        grid_spec=pltpu.PrefetchScalarGridSpec(
            num_scalar_prefetch=1,
            grid=(rows,),
            in_specs=[
                wide, by_row(total, kv.shape[2]), wide, wide, by_row(group, heads), by_row(heads, group),
                by_row(heads, group), by_row(1, group), full((1, group)), wide, by_row(group, heads),
                full((group, dim)), full((group, dim)), full((1, dim)), *[pl.BlockSpec(memory_space=pl.ANY)] * 3,
            ],
            out_specs=[
                wide, by_row(heads, group), by_row(total, kv.shape[2]), full((1, dim)),
                *[pl.BlockSpec(memory_space=pl.ANY)] * 3,
            ],
            scratch_shapes=[
                pltpu.VMEM((repeat * group, dim), bf16),
                pltpu.VMEM((repeat * group, dim), bf16),
                pltpu.VMEM((1, repeat * group), f32),
                pltpu.VMEM((1, repeat * group), f32),
                pltpu.VMEM((repeat * group, dim), f32),
                *[pltpu.VMEM(m.shape, m.dtype) for m in moved],
                pltpu.SemaphoreType.DMA((2, 3)),
            ],
        ),
        out_shape=[
            jax.ShapeDtypeStruct((rows, group, width), bf16),
            jax.ShapeDtypeStruct((rows, heads, group), f32),
            jax.ShapeDtypeStruct(kv.shape, bf16),
            jax.ShapeDtypeStruct((1, dim), f32),
            *[jax.ShapeDtypeStruct(m.shape, m.dtype) for m in moved],
        ],
        compiler_params=params(),
        cost_estimate=cost(
            5 * rows * heads * group * total * dim, 4 * kv.size + 10 * q.size, rows * heads * group * total // 2
        ),
        name="attend_back",
    )(bounds, q, kv, dgated, att, logits, logit_rows, lse, start_row, pos_row, nq, rq, cosine, sine, gain[None], *moved)


def key_back_kernel(kv_heads, dim, dkv_ref, nk_ref, rk_ref, cos_ref, sin_ref, gain_ref, dk_ref, dgain_ref):
    @pl.when(pl.program_id(0) == 0)
    def _():
        dgain_ref[...] = jnp.zeros_like(dgain_ref)

    for h in range(kv_heads):
        at = slice(h * dim, (h + 1) * dim)
        turned = dkv_ref[0, :, at].astype(f32)
        back = turned * cos_ref[...] - pltpu.roll(turned, dim // 2, 1) * sin_ref[...]
        unit = nk_ref[0, :, at].astype(f32)
        dgain_ref[...] += jnp.sum(back * unit, axis=0, keepdims=True)
        inner = back * gain_ref[...]
        mean = jnp.mean(inner * unit, axis=1, keepdims=True)
        dk_ref[0, :, at] = (rk_ref[0, :, h:h + 1] * (inner - unit * mean)).astype(bf16)
    dk_ref[0, :, kv_heads * dim:] = dkv_ref[0, :, kv_heads * dim:]


def key_back(dkv, nk, rk, tables, gain, kv_heads, dim):
    rows, group, width = dkv.shape

    def by_row(*shape):
        return pl.BlockSpec((1, *shape), lambda r: (r, 0, 0))

    return pl.pallas_call(
        functools.partial(key_back_kernel, kv_heads, dim),
        grid=(rows,),
        in_specs=[
            by_row(group, width), by_row(group, kv_heads * dim), by_row(group, kv_heads), full((group, dim)),
            full((group, dim)), full((1, dim)),
        ],
        out_specs=[by_row(group, width), full((1, dim))],
        out_shape=[jax.ShapeDtypeStruct((rows, group, width), bf16), jax.ShapeDtypeStruct((1, dim), f32)],
        compiler_params=params(),
        cost_estimate=cost(20 * dkv.size, 6 * dkv.size),
        name="key_back",
    )(dkv, nk, rk, *tables, gain[None])


def line_barrier(n, me):
    barrier = pltpu.get_barrier_semaphore()
    for way in (1, -1):
        @pl.when((me + way >= 0) & (me + way < n))
        def _():
            pl.semaphore_signal(barrier, inc=1, device_id={"tp": jnp.clip(me + way, 0, n - 1)}, device_id_type=MESH)
    edge = (me == 0) | (me == n - 1)

    @pl.when(edge)
    def _():
        pl.semaphore_wait(barrier, 1)

    @pl.when(jnp.logical_not(edge))
    def _():
        pl.semaphore_wait(barrier, 2)


def line_and_plane_barrier(n, me, bits, n_uly):
    barrier = pltpu.get_barrier_semaphore()
    place = plane_place(n_uly)
    for way in (1, -1):
        @pl.when((me + way >= 0) & (me + way < n))
        def _():
            pl.semaphore_signal(barrier, inc=1, device_id={"tp": jnp.clip(me + way, 0, n - 1)}, device_id_type=MESH)
    for b in range(bits):
        pl.semaphore_signal(barrier, inc=1, device_id=plane_device(place ^ (1 << b), n_uly), device_id_type=MESH)
    edge = (me == 0) | (me == n - 1)

    @pl.when(edge)
    def _():
        pl.semaphore_wait(barrier, bits + 1)

    @pl.when(jnp.logical_not(edge))
    def _():
        pl.semaphore_wait(barrier, bits + 2)


class LineSum:
    def __init__(self, n, pieces, part_at, own, land_ref, sems, out_at=None):
        self.n, self.pieces, self.part_at, self.own, self.land, self.out_at = n, pieces, part_at, own, land_ref, out_at
        self.rs_send, self.rs_recv = sems[:2]
        if out_at:
            self.ag_send, self.ag_recv = sems[2:]
        self.me = lax.axis_index("tp")
        self.stages = [functools.partial(self.reduce_step, k) for k in range(1, n)] + [self.own_step]
        if out_at:
            self.stages += [functools.partial(self.spread_step, k) for k in range(2, n + 1)]

    def inside(self, place):
        return (place >= 0) & (place < self.n)

    def near(self, way):
        return {"tp": jnp.clip(self.me + way, 0, self.n - 1)}

    def reduce_copy(self, way, k, s, source):
        d = 0 if way == 1 else 1
        return pltpu.make_async_remote_copy(
            src_ref=source, dst_ref=self.land.at[d, k - 1, s], send_sem=self.rs_send.at[d, k - 1, s],
            recv_sem=self.rs_recv.at[d, k - 1, s], device_id=self.near(way), device_id_type=MESH)

    def spread_copy(self, way, k, s, owner):
        d = 0 if way == 1 else 1
        rows = self.out_at(jnp.clip(owner, 0, self.n - 1), s)
        return pltpu.make_async_remote_copy(
            src_ref=rows, dst_ref=rows, send_sem=self.ag_send.at[d, k - 1, s], recv_sem=self.ag_recv.at[d, k - 1, s],
            device_id=self.near(way), device_id_type=MESH)

    def reduce_step(self, k, s):
        for way in (1, -1):
            d = 0 if way == 1 else 1
            first = jnp.logical_not(self.inside(self.me - way))
            dest = self.me + way * (self.n - k)
            part = self.part_at(jnp.clip(dest, 0, self.n - 1), s)

            @pl.when(first & self.inside(dest))
            def _():
                self.reduce_copy(way, k, s, part).start()

            if k > 1:
                @pl.when(self.inside(self.me - way) & self.inside(dest))
                def _():
                    landed = self.land.at[d, k - 2, s]
                    self.reduce_copy(way, k - 1, s, landed).wait_recv()
                    landed[...] = (part[...].astype(f32) + landed[...].astype(f32)).astype(bf16)
                    self.reduce_copy(way, k, s, landed).start()

    def own_step(self, s):
        for way in (1, -1):
            d = 0 if way == 1 else 1
            landed = self.land.at[d, self.n - 2, s]

            @pl.when(self.inside(self.me - way))
            def _():
                self.reduce_copy(way, self.n - 1, s, landed).wait_recv()

            @pl.when(jnp.logical_not(self.inside(self.me - way)))
            def _():
                landed[...] = jnp.zeros_like(landed)

        total = self.part_at(self.me, s)[...].astype(f32)
        for d in range(2):
            total = total + self.land[d, self.n - 2, s].astype(f32)
        rows = self.own(s, total)
        if self.out_at:
            self.out_at(self.me, s)[...] = rows
            self.spread_step(1, s)

    def spread_step(self, k, s):
        for way in (1, -1):
            owner = self.me - way * (k - 1)
            if k > 1:
                @pl.when(self.inside(owner))
                def _():
                    self.spread_copy(way, k - 1, s, owner).wait_recv()
            if k < self.n:
                @pl.when(self.inside(owner) & self.inside(self.me + way))
                def _():
                    self.spread_copy(way, k, s, owner).start()

    def drain_reduce(self):
        for s in range(self.pieces):
            for way in (1, -1):
                for k in range(1, self.n):
                    @pl.when(self.inside(self.me + way) & self.inside(self.me + way * (self.n - k)))
                    def _():
                        self.reduce_copy(way, k, s, self.land.at[0, 0, s]).wait_send()

    def drain_spread(self):
        for s in range(self.pieces):
            for way in (1, -1):
                for k in range(1, self.n):
                    owner = self.me - way * (k - 1)

                    @pl.when(self.inside(owner) & self.inside(self.me + way))
                    def _():
                        self.spread_copy(way, k, s, owner).wait_send()

    def run(self, beside=(), quiet=(0, 0)):
        beside, done = list(beside), 0
        steps = self.pieces + len(self.stages) - 1
        turns = [(step, s) for step in range(steps) for s in range(self.pieces) if 0 <= step - s < len(self.stages)]
        slots = [i for i, (step, _) in enumerate(turns) if quiet[0] <= step < steps - quiet[1]]
        for i, (step, s) in enumerate(turns):
            self.stages[step - s](s)
            if i in slots:
                until = len(beside) * (slots.index(i) + 1) // len(slots)
                for item in beside[done:until]:
                    item()
                done = until
        self.drain_reduce()
        self.drain_spread()


def line_all_sum(n, seqs, rows, piece, finish, part_ref, out_ref, land_ref, sems, beside=(), quiet=(0, 0)):
    cuts = [(q, c) for q in range(seqs) for c in range(rows // piece)]

    def at(ref):
        return lambda owner, s: ref.at[
            cuts[s][0], pl.ds(pl.multiple_of(owner * rows + cuts[s][1] * piece, piece), piece)]

    LineSum(n, len(cuts), at(part_ref), lambda s, total: finish(*cuts[s], total), land_ref, sems, at(out_ref)).run(
        beside, quiet)


def line_scratch(n, seqs, rows, piece, width):
    count = seqs * (rows // piece)
    return [
        pltpu.VMEM((2, n - 1, count, piece, width), bf16),
        pltpu.SemaphoreType.DMA((2, n - 1, count)), pltpu.SemaphoreType.DMA((2, n - 1, count)),
        pltpu.SemaphoreType.DMA((2, n - 1, count)), pltpu.SemaphoreType.DMA((2, n - 1, count)),
    ]


def norm_forward_kernel(n, seqs, rows, piece, part_ref, x_ref, gain_ref, out_ref, mid_ref, land_ref, *sems):
    def finish(q, c, total):
        at = slice(c * piece, (c + 1) * piece)
        mid = x_ref[q, at].astype(f32) + total
        mid_ref[q, at] = mid
        return (mid * rms_inverse(mid) * gain_ref[...]).astype(bf16)

    line_barrier(n, lax.axis_index("tp"))
    line_all_sum(n, seqs, rows, piece, finish, part_ref, out_ref, land_ref, sems)


def line_call(kernel, n, local, part, others, extra, collective_id, name):
    seqs, rows, width = local
    piece = min(32, rows)
    vm = pl.BlockSpec(memory_space=pltpu.VMEM)
    shapes = [jax.ShapeDtypeStruct(part.shape, bf16), jax.ShapeDtypeStruct(local, f32), *extra]
    return pl.pallas_call(
        functools.partial(kernel, n, seqs, rows, piece),
        in_specs=[vm] * (1 + len(others)),
        out_specs=[vm] * len(shapes),
        out_shape=shapes,
        scratch_shapes=line_scratch(n, seqs, rows, piece, width),
        compiler_params=params(collective_id=collective_id, has_side_effects=True),
        cost_estimate=cost(20 * part.size, 100_000_000),
        name=name,
    )(part, *others)


def plane_place(n_uly):
    return lax.axis_index("ctx") * n_uly + lax.axis_index("uly")


def plane_device(place, n_uly):
    return {"ctx": place // n_uly, "uly": lax.rem(place, n_uly)}


def plane_barrier(bits, me, n_uly):
    barrier = pltpu.get_barrier_semaphore()
    for b in range(bits):
        pl.semaphore_signal(barrier, inc=1, device_id=plane_device(me ^ (1 << b), n_uly), device_id_type=MESH)
    pl.semaphore_wait(barrier, bits)


def ways(bits):
    upper = list(range(1, bits))
    return upper, upper[::-1]


def span(order):
    out = [0]
    for b in order:
        out += [e | (1 << b) for e in out]
    return out


def plane_gather_kernel(bits, n_uly, own_ref, out_ref, copy_sem, send_sem, recv_sem):
    me = plane_place(n_uly)
    rows, half = own_ref.shape[1], own_ref.shape[2] // 2
    plane_barrier(bits, me, n_uly)
    orders = [w + [0] for w in ways(bits)]

    def block(place, d):
        return out_ref.at[:, pl.ds(pl.multiple_of(place * rows, rows), rows), pl.ds(d * half, half)]

    def copy(d, level, e):
        bit = orders[d][level]
        source = own_ref.at[:, :, pl.ds(d * half, half)] if e == 0 else block(me ^ e, d)
        return pltpu.make_async_remote_copy(
            src_ref=source, dst_ref=block(me ^ e, d), send_sem=send_sem.at[d, e | (1 << bit)],
            recv_sem=recv_sem.at[d, e | (1 << bit)], device_id=plane_device(me ^ (1 << bit), n_uly),
            device_id_type=MESH)

    own = [pltpu.make_async_copy(own_ref.at[:, :, pl.ds(d * half, half)], block(me, d), copy_sem.at[d]) for d in range(2)]
    for c in own:
        c.start()
    for level in range(bits):
        for d in range(2):
            for e in span(orders[d][:level]):
                if level > 0 and e >> orders[d][level - 1] & 1:
                    continue
                copy(d, level, e).start()
        for d in range(2):
            for e in span(orders[d][:level]):
                copy(d, level, e).wait_recv()
                if level + 1 < bits:
                    copy(d, level + 1, e | (1 << orders[d][level])).start()
    for d in range(2):
        own[d].wait()
        for level in range(bits):
            for e in span(orders[d][:level]):
                copy(d, level, e).wait_send()


def plane_gather(own, sizes, collective_id):
    n_ctx, n_uly = sizes
    count = n_ctx * n_uly
    bits = count.bit_length() - 1
    seqs, rows, width = own.shape
    if own.size * count * 2 > 12 << 20 or count != 1 << bits or bits < 2:
        return lax.all_gather(own, ("ctx", "uly"), axis=1, tiled=True)
    vm = pl.BlockSpec(memory_space=pltpu.VMEM)
    return pl.pallas_call(
        functools.partial(plane_gather_kernel, bits, n_uly),
        in_specs=[vm], out_specs=vm,
        out_shape=jax.ShapeDtypeStruct((seqs, rows * count, width), own.dtype),
        scratch_shapes=[pltpu.SemaphoreType.DMA((2,)), pltpu.SemaphoreType.DMA((2, count)), pltpu.SemaphoreType.DMA((2, count))],
        compiler_params=params(collective_id=collective_id, has_side_effects=True),
        cost_estimate=cost(0, 100_000_000),
        name="plane_gather",
    )(own)


class PlaneSum:
    def __init__(self, bits, n_uly, make, store, buf_ref, land_ref, send, recv):
        self.bits, self.n_uly, self.make, self.store = bits, n_uly, make, store
        self.buf, self.land, self.send, self.recv = buf_ref, land_ref, send, recv
        self.me = plane_place(n_uly)
        width = buf_ref.shape[-1]
        half = max(width // 256, 1) * 128
        self.parts = [(0, half), (half, width - half)]
        self.orders = ways(bits)

    @staticmethod
    def scratch(bits, rows, width):
        n = 1 << bits
        return [
            pltpu.VMEM((n, rows, width), bf16), pltpu.VMEM((n - 1, rows, width), bf16),
            pltpu.SemaphoreType.DMA((3, n)), pltpu.SemaphoreType.DMA((3, n)),
        ]

    def slot(self, e):
        return e

    def view(self, ref, i, d):
        return ref.at[(i, *[slice(None)] * (len(ref.shape) - 2), pl.ds(*self.parts[d]))]

    def first_copy(self, e):
        return pltpu.make_async_remote_copy(
            src_ref=self.buf.at[e], dst_ref=self.land.at[e - 1], send_sem=self.send.at[2, e],
            recv_sem=self.recv.at[2, e], device_id=plane_device(self.me ^ 1, self.n_uly), device_id_type=MESH)

    def copy(self, d, level, e):
        return pltpu.make_async_remote_copy(
            src_ref=self.view(self.buf, self.slot(e), d), dst_ref=self.view(self.land, e - 1, d),
            send_sem=self.send.at[d, e],
            recv_sem=self.recv.at[d, e],
            device_id=plane_device(self.me ^ (1 << self.orders[d][level]), self.n_uly), device_id_type=MESH)

    def sent(self, d, level):
        return [(1 << self.orders[d][level]) | e for e in span(self.orders[d][level + 1:])]

    def compute(self):
        n = 1 << self.bits
        for e in range(1, n, 2):
            self.buf[e] = self.make(self.me ^ e).astype(bf16)
            self.first_copy(e).start()
        for e in range(0, n, 2):
            self.buf[e] = self.make(self.me ^ e).astype(bf16)

    def pair(self):
        for e in range(1, 1 << self.bits, 2):
            self.first_copy(e).wait_recv()
            kept = self.slot(e - 1)
            self.buf[kept] = (self.buf[kept].astype(f32) + self.land[e - 1].astype(f32)).astype(bf16)

    def push(self, level):
        for d in range(2):
            for e in self.sent(d, level):
                self.copy(d, level, e).start()

    def pull(self, level):
        for d in range(2):
            for e in self.sent(d, level):
                kept = self.view(self.buf, self.slot(e ^ (1 << self.orders[d][level])), d)
                self.copy(d, level, e).wait_recv()
                total = kept[...].astype(f32) + self.view(self.land, e - 1, d)[...].astype(f32)
                if level == self.bits - 2:
                    self.store(pl.ds(*self.parts[d]), total)
                else:
                    kept[...] = total.astype(bf16)

    def finish(self):
        for e in range(1, 1 << self.bits, 2):
            self.first_copy(e).wait_send()
        for d in range(2):
            for level in range(self.bits - 1):
                for e in self.sent(d, level):
                    self.copy(d, level, e).wait_send()


def blocks_sum_kernel(bits, n_uly, parts_ref, out_ref, *scratch):
    me = plane_place(n_uly)
    plane_barrier(bits, me, n_uly)
    seqs, rows = out_ref.shape[0], out_ref.shape[1]

    def make(place):
        return parts_ref[:, pl.ds(pl.multiple_of(place * rows, rows), rows)].reshape(seqs * rows, -1)

    def store(at, total):
        out_ref[:, :, at] = total.reshape(seqs, rows, -1).astype(out_ref.dtype)

    job = PlaneSum(bits, n_uly, make, store, *scratch)
    job.compute()
    job.pair()
    for level in range(bits - 1):
        job.push(level)
        job.pull(level)
    job.finish()


def blocks_sum(parts, sizes, collective_id):
    n_ctx, n_uly = sizes
    count = n_ctx * n_uly
    bits = count.bit_length() - 1
    seqs, total, width = parts.shape
    rows = total // count
    if parts.size * 2 > 12 << 20 or count != 1 << bits or bits < 2:
        return lax.psum_scatter(parts, ("ctx", "uly"), scatter_dimension=1, tiled=True)
    vm = pl.BlockSpec(memory_space=pltpu.VMEM)
    return pl.pallas_call(
        functools.partial(blocks_sum_kernel, bits, n_uly),
        in_specs=[vm],
        out_specs=vm,
        out_shape=jax.ShapeDtypeStruct((seqs, rows, width), bf16),
        scratch_shapes=PlaneSum.scratch(bits, seqs * rows, width),
        compiler_params=params(collective_id=collective_id, has_side_effects=True),
        cost_estimate=cost(10 * parts.size, 100_000_000),
        name="blocks_sum",
    )(parts)


def outer_sums_kernel(bits, n_uly, use, *refs):
    count, kinds = len(use), max(use) + 1
    lefts, refs = [refs[k] for k in use], refs[kinds:]
    rights, outs, scratch = refs[:count], refs[count:2 * count], refs[2 * count:]
    plane_barrier(bits, plane_place(n_uly), n_uly)
    jobs = []
    for i in range(count):
        each = outs[i].shape[0]

        def make(place, i=i, each=each):
            left = lefts[i][:, pl.ds(pl.multiple_of(place * each, each), each)]
            return mm(left, rights[i][...], TN)

        def store(at, total, i=i):
            outs[i][:, at] = total

        jobs.append(PlaneSum(bits, n_uly, make, store, *scratch[4 * i:4 * i + 4]))
    last = bits - 2
    for i in range(count + last + 1):
        if i < count:
            jobs[i].compute()
            jobs[i].pair()
            jobs[i].push(0)
        for level in range(last + 1):
            j = i - 1 - level
            if 0 <= j < count:
                jobs[j].pull(level)
                if level < last:
                    jobs[j].push(level + 1)
                else:
                    jobs[j].finish()


def fits_plane(sizes, width):
    places = sizes[0] * sizes[1]
    return places & (places - 1) == 0 and places >= 4 and width // places % 128 == 0


def outer_sums(kinds, use, rights, sizes, collective_id):
    lefts = [kinds[k] for k in use]
    n_ctx, n_uly = sizes
    places = n_ctx * n_uly
    bits = places.bit_length() - 1
    count = len(lefts)
    if not fits_plane(sizes, lefts[0].shape[1]):
        return [
            lax.psum_scatter(mm(l, r, TN).astype(bf16), ("ctx", "uly"), scatter_dimension=0, tiled=True).astype(f32)
            for l, r in zip(lefts, rights)
        ]
    vm = pl.BlockSpec(memory_space=pltpu.VMEM)
    shapes = [(l.shape[1] // places, r.shape[1]) for l, r in zip(lefts, rights)]
    scratch = []
    for shape in shapes:
        scratch += PlaneSum.scratch(bits, *shape)
    work = sum(l.size * r.shape[1] for l, r in zip(lefts, rights))
    return pl.pallas_call(
        functools.partial(outer_sums_kernel, bits, n_uly, use),
        in_specs=[vm] * (len(kinds) + count),
        out_specs=[vm] * count,
        out_shape=[jax.ShapeDtypeStruct(s, f32) for s in shapes],
        scratch_shapes=scratch,
        compiler_params=pltpu.CompilerParams(
            collective_id=collective_id, has_side_effects=True, vmem_limit_bytes=vmem_bytes),
        cost_estimate=cost(2 * work, 200_000_000),
        name="outer_sums",
    )(*kinds, *rights)


def back_finish(piece, cot_ref, mid_ref, gain_ref, dmid_ref, dgain_ref):
    def finish(q, c, total):
        at = slice(c * piece, (c + 1) * piece)
        mid = mid_ref[q, at]
        inverse = rms_inverse(mid)
        unit = mid * inverse
        dgain_ref[...] += jnp.sum(total * unit, axis=0, keepdims=True)
        inner = total * gain_ref[...]
        mean = jnp.mean(inner * unit, axis=-1, keepdims=True)
        d_mid = cot_ref[q, at].astype(f32) + inverse * (inner - unit * mean)
        dmid_ref[q, at] = d_mid
        return d_mid.astype(bf16)

    return finish


def plain_back_kernel(n, seqs, rows, piece, part_ref, cot_ref, mid_ref, gain_ref, out_ref, dmid_ref, dgain_ref,
                      land_ref, *sems):
    dgain_ref[...] = jnp.zeros_like(dgain_ref)
    line_barrier(n, lax.axis_index("tp"))
    line_all_sum(n, seqs, rows, piece, back_finish(piece, cot_ref, mid_ref, gain_ref, dmid_ref, dgain_ref), part_ref,
                 out_ref, land_ref, sems)


class StreamedOuter:
    def __init__(self, jobs, each, left_slots, right_slots, left_sems, right_sems):
        self.jobs, self.each = jobs, each
        self.left, self.right, self.left_sems, self.right_sems = left_slots, right_slots, left_sems, right_sems

    def right_copy(self, i):
        _, right, half, _ = self.jobs[i]
        wide = self.right.shape[-1]
        return pltpu.make_async_copy(
            right.at[:, pl.ds(half * wide, wide)], self.right.at[i % 2], self.right_sems.at[i % 2])

    def left_copy(self, i, turn, place):
        at = pl.ds(pl.multiple_of(place * self.each, self.each), self.each)
        return pltpu.make_async_copy(self.jobs[i][0].at[:, at], self.left.at[turn % 2], self.left_sems.at[turn % 2])

    def product(self, i, turn, places, take):
        if turn == 0:
            if i == 0:
                self.right_copy(0).start()
                self.left_copy(0, 0, places[0]).start()
            self.right_copy(i).wait()
            if i + 1 < len(self.jobs):
                self.right_copy(i + 1).start()
        if turn + 1 < len(places):
            self.left_copy(i, turn + 1, places[turn + 1]).start()
        self.left_copy(i, turn, places[turn]).wait()
        value = mm(self.left[turn % 2], self.right[i % 2], TN)
        if turn + 1 == len(places) and i + 1 < len(self.jobs):
            self.left_copy(i + 1, 0, places[0]).start()
        take(value)


def norm_back_kernel(n, seqs, rows, piece, bits, n_uly, part_ref, cot_ref, mid_ref, gain_ref, a2_ref, cot_all_ref,
                     dgate_ref, dup_ref, hidden_ref, out_ref, dmid_ref, dgain_ref, ggate_ref, gup_ref, gdown_ref,
                     land_ref, rs_send, rs_recv, ag_send, ag_recv, left_slots, right_slots, left_sems, right_sems,
                     *plane_scratch):
    dgain_ref[...] = jnp.zeros_like(dgain_ref)

    finish = back_finish(piece, cot_ref, mid_ref, gain_ref, dmid_ref, dgain_ref)
    wide = right_slots.shape[-1]
    halves = ggate_ref.shape[1] // wide
    jobs = [
        (left, right, half, out)
        for left, right, out in (
            (a2_ref, dgate_ref, ggate_ref), (a2_ref, dup_ref, gup_ref), (cot_all_ref, hidden_ref, gdown_ref))
        for half in range(halves)
    ]
    streamed = StreamedOuter(jobs, ggate_ref.shape[0], left_slots, right_slots, left_sems, right_sems)
    sums = []
    for i, (_, _, half, out) in enumerate(jobs):
        def store(at, total, half=half, out=out):
            to = pl.ds(half * wide + at.start, at.size)
            if out is gdown_ref:
                out[to] = total.T
            else:
                out[:, to] = total

        buf = plane_scratch[i % 3]
        land, send, recv = plane_scratch[3 + 3 * i:6 + 3 * i]
        sums.append(PlaneSum(bits, n_uly, None, store, buf, land, send, recv))
    last = bits - 2

    order = list(range(1, 1 << bits, 2)) + list(range(0, 1 << bits, 2))
    quiet = back_quiet
    beside = []

    def product(i, turn):
        def take(value):
            sums[i].buf[order[turn]] = value.astype(bf16)
            if order[turn] % 2:
                sums[i].first_copy(order[turn]).start()

        streamed.product(i, turn, [sums[i].me ^ e for e in order], take)

    for i in range(len(jobs) + last + 1):
        if i < len(jobs):
            beside += [functools.partial(product, i, turn) for turn in range(len(order))]
        for level in range(last):
            j = i - 1 - level
            if 0 <= j < len(jobs):
                beside += [functools.partial(sums[j].pull, level), functools.partial(sums[j].push, level + 1)]
        if i < len(jobs):
            beside += [sums[i].pair, functools.partial(sums[i].push, 0)]
        if 0 <= i - 1 - last < len(jobs):
            beside += [functools.partial(sums[i - 1 - last].pull, last), sums[i - 1 - last].finish]

    line_and_plane_barrier(n, lax.axis_index("tp"), bits, n_uly)
    line_all_sum(n, seqs, rows, piece, finish, part_ref, out_ref, land_ref, (rs_send, rs_recv, ag_send, ag_recv),
                 beside, quiet)


def norm_back(part, cotangent, middle, gain, a2, cot_all, d_gate, d_up, hidden, n, sizes, collective_id):
    n_ctx, n_uly = sizes
    places = n_ctx * n_uly
    bits = places.bit_length() - 1
    seqs, rows, width = cotangent.shape
    tokens, units = d_gate.shape
    each = width // places
    if not fits_plane(sizes, width) or units % 512:
        out, d_mid, dgain = line_call(
            plain_back_kernel, n, cotangent.shape, part, (cotangent, middle, gain[None]),
            (jax.ShapeDtypeStruct((1, width), f32),), collective_id, "norm_back")
        grads = outer_sums((a2, cot_all), (0, 0, 1), (d_gate, d_up, hidden), sizes, 0)
        return (out, d_mid, dgain, *grads[:2], grads[2].T)
    piece = min(back_piece, rows)
    half = units // 2
    vm, anywhere = pl.BlockSpec(memory_space=pltpu.VMEM), pl.BlockSpec(memory_space=pl.ANY)
    shapes = [
        jax.ShapeDtypeStruct(part.shape, bf16), jax.ShapeDtypeStruct(cotangent.shape, f32),
        jax.ShapeDtypeStruct((1, width), f32), *[jax.ShapeDtypeStruct((each, units), f32)] * 2,
        jax.ShapeDtypeStruct((units, each), f32),
    ]
    plane_scratch = [PlaneSum.scratch(bits, each, half) for _ in range(6)]
    return pl.pallas_call(
        functools.partial(norm_back_kernel, n, seqs, rows, piece, bits, n_uly),
        in_specs=[vm] * 4 + [anywhere] * 5,
        out_specs=[vm] * len(shapes),
        out_shape=shapes,
        scratch_shapes=[
            *line_scratch(n, seqs, rows, piece, width),
            pltpu.VMEM((2, tokens, each), bf16), pltpu.VMEM((2, tokens, half), bf16),
            pltpu.SemaphoreType.DMA((2,)), pltpu.SemaphoreType.DMA((2,)),
            plane_scratch[0][0], plane_scratch[0][0], plane_scratch[0][0],
            *[item for scratch in plane_scratch for item in scratch[1:]],
        ],
        compiler_params=pltpu.CompilerParams(
            collective_id=collective_id, has_side_effects=True, vmem_limit_bytes=vmem_bytes),
        cost_estimate=cost(6 * tokens * units * width, 250_000_000),
        name="norm_back",
    )(part, cotangent, middle, gain[None], a2, cot_all, d_gate, d_up, hidden)


class StoredSum(PlaneSum):
    def __init__(self, bits, n_uly, source, store, buf_ref, land_ref, send, recv, load):
        super().__init__(bits, n_uly, None, store, buf_ref, land_ref, send, recv)
        self.source, self.load = source, load

    @staticmethod
    def scratch(bits, *shape):
        n = 1 << bits
        return [
            pltpu.VMEM((n // 2, *shape), bf16), pltpu.VMEM((n - 1, *shape), bf16),
            pltpu.SemaphoreType.DMA((3, n)), pltpu.SemaphoreType.DMA((3, n)), pltpu.SemaphoreType.DMA((n // 2,)),
        ]

    def slot(self, e):
        return e // 2

    def first_copy(self, e):
        return pltpu.make_async_remote_copy(
            src_ref=self.source(self.me ^ e), dst_ref=self.land.at[e - 1], send_sem=self.send.at[2, e],
            recv_sem=self.recv.at[2, e], device_id=plane_device(self.me ^ 1, self.n_uly), device_id_type=MESH)

    def load_copy(self, e):
        return pltpu.make_async_copy(self.source(self.me ^ e), self.buf.at[e // 2], self.load.at[e // 2])

    def compute(self):
        for e in range(1, 1 << self.bits, 2):
            self.first_copy(e).start()
            self.load_copy(e - 1).start()

    def pair(self):
        for e in range(0, 1 << self.bits, 2):
            self.load_copy(e).wait()
        super().pair()


def all_barrier(n, bits, n_uly):
    barrier = pltpu.get_barrier_semaphore()
    me, place = lax.axis_index("tp"), plane_place(n_uly)
    for d in range(1, n):
        pl.semaphore_signal(barrier, inc=1, device_id={"tp": lax.rem(me + d, n)}, device_id_type=MESH)
    for b in range(bits):
        pl.semaphore_signal(barrier, inc=1, device_id=plane_device(place ^ (1 << b), n_uly), device_id_type=MESH)
    pl.semaphore_wait(barrier, n - 1 + bits)


def layer_back_kernel(
    n, bits, n_uly, heads, kv_heads, dim, dkv_ref, first_ref, dbranch_ref, dq_ref, dlogit_ref, nk_ref, rk_ref, cos_ref,
    sin_ref, kgain_ref, wq_ref, wk_ref, wv_ref, wg_ref, gated_ref, x_ref, gain_ref, dmid_ref, dqgain_ref, dmlp_ref, gin_ref, gq_ref, gk_ref,
    gv_ref, gh_ref, gout_ref, gattn_ref, gmlp_ref, gqn_ref, gkn_ref, all_ref, cut_ref, part_ref, sum_ref, line_land, rs_send, rs_recv, left_slots, left_sems,
    vec_ref, vec_land, vec_send, vec_recv, *plane_scratch,
):
    seqs, _, cut_count, piece, _ = dq_ref.shape
    rows, width = cut_count * piece, x_ref.shape[-1]
    group = n * rows
    cuts = [(q, c) for q in range(seqs) for c in range(cut_count)]
    q_cols, kv_cols = heads * dim, kv_heads * dim
    n_main = q_cols + 2 * kv_cols
    each = gq_ref.shape[0]
    place, line_me = plane_place(n_uly), lax.axis_index("tp")

    vec_ref[0] = jnp.zeros_like(vec_ref[0])
    vec_ref[0, :, width:2 * width] = dmlp_ref[...]
    vec_ref[0, :, 2 * width:2 * width + dim] = dqgain_ref[...]

    def row_at(q, t, c):
        return q * group + t * rows + c * piece

    def key_values(s):
        q, c = cuts[s]

        def store(at, total):
            sum_ref[:, :, at] = total.astype(bf16)

        return StoredSum(
            bits, n_uly, lambda at: dkv_ref.at[q, pl.ds(pl.multiple_of(at * n, n), n), c], store,
            *plane_scratch[5 * s:5 * s + 5])

    sums = [key_values(s) for s in range(len(cuts))]

    def turn(s):
        q, c = cuts[s]
        for t in range(n):
            at = slice(t * piece, (t + 1) * piece)
            cut_ref[at, :q_cols] = dq_ref[q, t, c]
            for h in range(kv_heads):
                turned = sum_ref[t, :, h * dim:(h + 1) * dim].astype(f32)
                back = turned * cos_ref[t, c] - pltpu.roll(turned, dim // 2, 1) * sin_ref[t, c]
                unit = nk_ref[q, t, c, :, h * dim:(h + 1) * dim].astype(f32)
                vec_ref[0, :, 2 * width + dim:] += jnp.sum(back * unit, axis=0, keepdims=True)
                inner = back * kgain_ref[...]
                mean = jnp.mean(inner * unit, axis=1, keepdims=True)
                cut_ref[at, q_cols + h * dim:q_cols + (h + 1) * dim] = (
                    rk_ref[q, t, c, :, h:h + 1] * (inner - unit * mean)).astype(bf16)
            cut_ref[at, q_cols + kv_cols:n_main] = sum_ref[t, :, kv_cols:]
            cut_ref[at, n_main:] = dlogit_ref[q, t, c]
        partial = mm(cut_ref[:, :q_cols], wq_ref[...], NT)
        partial += mm(cut_ref[:, q_cols:q_cols + kv_cols], wk_ref[...], NT)
        partial += mm(cut_ref[:, q_cols + kv_cols:n_main], wv_ref[...], NT)
        partial += mm(cut_ref[:, n_main:n_main + heads], wg_ref[...])
        partial = partial.astype(bf16)
        for t in range(n):
            at = slice(t * piece, (t + 1) * piece)
            to = slice(row_at(q, t, c), row_at(q, t, c) + piece)
            part_ref[to] = partial[at]
            all_ref[to] = cut_ref[at]

    split = line_land.shape[2] // len(cuts)
    short = piece // split

    def part_at(owner, p):
        q, c = cuts[p // split]
        return part_ref.at[pl.ds(pl.multiple_of(row_at(q, owner, c) + p % split * short, short), short)]

    def own(p, total):
        q, c = cuts[p // split]
        at = slice(c * piece + p % split * short, c * piece + (p % split + 1) * short)
        x = x_ref[q, at].astype(f32)
        inverse = rms_inverse(x)
        unit = x * inverse
        inner = total * gain_ref[...]
        mean = jnp.mean(inner * unit, axis=-1, keepdims=True)
        gin_ref[q, at] = dmid_ref[q, at] + inverse * (inner - unit * mean)

    line = LineSum(n, len(cuts) * split, part_at, own, line_land, (rs_send, rs_recv))

    order = list(range(1, 1 << bits, 2)) + list(range(0, 1 << bits, 2))
    turns = [(dbranch_ref, e) for e in order] + [(first_ref, e) for e in order]

    def left_copy(i):
        source, e = turns[i]
        at = pl.ds(pl.multiple_of((place ^ e) * each, each), each)
        return pltpu.make_async_copy(source.at[:, at], left_slots.at[i % 2], left_sems.at[i % 2])

    def store_out(at, total):
        gout_ref[at] = total.T

    def store_first(at, total):
        if at.start + at.size > n_main:
            gh_ref[...] = total[:, n_main - at.start:].T[:heads]
        first = 0
        for out in (gq_ref, gk_ref, gv_ref):
            lo, hi = max(first, at.start), min(first + out.shape[1], at.start + at.size)
            if lo < hi:
                out[:, lo - first:hi - first] = total[:, lo - at.start:hi - at.start]
            first += out.shape[1]

    scratch = plane_scratch[5 * len(cuts):]
    out_sum = PlaneSum(bits, n_uly, None, store_out, *scratch[:4])
    first_sum = PlaneSum(bits, n_uly, None, store_first, *scratch[4:])

    def product(i):
        e = turns[i][1]
        if i + 1 < len(turns):
            left_copy(i + 1).start()
        left_copy(i).wait()
        job = out_sum if i < len(order) else first_sum
        value = mm(left_slots[i % 2], gated_ref[...] if i < len(order) else all_ref[...], TN)
        job.buf[e] = value.astype(bf16)
        if e % 2:
            job.first_copy(e).start()
        if job is first_sum:
            at = pl.ds(pl.multiple_of((place ^ e) * each, each), each)
            lanes, first = jnp.zeros((each, 128), f32), 0
            for w_ref in (wq_ref, wk_ref, wv_ref):
                for k in range(0, w_ref.shape[1], 128):
                    lanes += value[:, first + k:first + k + 128] * w_ref[at, k:k + 128].astype(f32)
                first += w_ref.shape[1]
            total = jnp.sum(lanes.T, axis=0, keepdims=True)
            last = value[:, n_main:].T[:heads] * wg_ref[:, at].astype(f32)
            total += jnp.sum(last, axis=0, keepdims=True)
            vec_ref[0, :, at] = total / gain_ref[:, at]

    line_bits = n.bit_length() - 1
    steps = bits + line_bits

    def vec_copy(k):
        partner = plane_device(place ^ (1 << k), n_uly) if k < bits else {"tp": line_me ^ (1 << (k - bits))}
        return pltpu.make_async_remote_copy(
            src_ref=vec_ref.at[k], dst_ref=vec_land.at[k], send_sem=vec_send.at[k], recv_sem=vec_recv.at[k],
            device_id=partner, device_id_type=MESH)

    def vec_step(k):
        if k > 0:
            vec_copy(k - 1).wait_recv()
            vec_ref[k] = vec_ref[k - 1] + vec_land[k - 1]
        if k < steps:
            vec_copy(k).start()

    def levels(job):
        items = []
        for level in range(bits - 1):
            items.append(functools.partial(job.pull, level))
            if level + 1 < bits - 1:
                items.append(functools.partial(job.push, level + 1))
        return items

    early = [functools.partial(product, i) for i in range(len(order))]
    early += [out_sum.pair, functools.partial(out_sum.push, 0)]
    late = [functools.partial(product, i) for i in range(len(order), len(turns))]
    late.append(functools.partial(vec_step, 0))
    late += levels(out_sum)[:2]
    late += [first_sum.pair, functools.partial(first_sum.push, 0)]
    rest = levels(out_sum)[2:] + levels(first_sum)
    for k in range(1, steps + 1):
        late.append(functools.partial(vec_step, k))
        if k % 2 == 0 and rest:
            late.append(rest.pop(0))
    late += rest

    all_barrier(n, bits, n_uly)
    for job in sums:
        job.compute()
    left_copy(0).start()
    ready = 0
    line_steps = split * (len(cuts) + bits - 1) + n - 1
    for step in range(-(-line_steps // split)):
        if step < len(cuts):
            sums[step].pair()
            sums[step].push(0)
        for level in range(bits - 1):
            j = step - 1 - level
            if 0 <= j < len(cuts):
                sums[j].pull(level)
                if level + 1 < bits - 1:
                    sums[j].push(level + 1)
                else:
                    turn(j)
                    ready += 1
        for turn_of in range(split * step, split * (step + 1)):
            for p in range(line.pieces):
                stage = turn_of - p - split * (bits - 1)
                if 0 <= stage < n:
                    line.stages[stage](p)
                    queue = early or (late if ready == len(cuts) else [])
                    for item in queue[:tail_items]:
                        item()
                    del queue[:tail_items]
    for item in early + late:
        item()
    line.drain_reduce()
    first = 0
    for out in (gattn_ref, gmlp_ref, gqn_ref, gkn_ref):
        out[...] = vec_ref[steps, :, first:first + out.shape[1]]
        first += out.shape[1]
    for k in range(steps):
        vec_copy(k).wait_send()
    for job in (*sums, out_sum, first_sum):
        job.finish()


def layer_back(d_kv, first, d_branch, d_q, d_logit, nk, rk, tables, key_norm, weights, gated, x, attn_norm, d_mid, d_qgain,
               d_mlp, n, sizes, heads, kv_heads, collective_id):
    n_ctx, n_uly = sizes
    places = n_ctx * n_uly
    bits = places.bit_length() - 1
    seqs, rows, width = x.shape
    group, dim = n * rows, key_norm.shape[0]
    piece = min(64, rows)
    cut_count = rows // piece
    each = width // places
    tokens = seqs * group
    wide = (heads + 2 * kv_heads) * dim + d_logit.shape[-1]
    small = 2 * width + 2 * dim
    kv_wide = d_kv.shape[-1]
    pieces = seqs * cut_count
    steps = bits + n.bit_length() - 1

    def tiles(values):
        return values.reshape(seqs, n, cut_count, piece, values.shape[-1])

    vm, anywhere = pl.BlockSpec(memory_space=pltpu.VMEM), pl.BlockSpec(memory_space=pl.ANY)
    plane_scratch = []
    for _ in range(pieces):
        plane_scratch += StoredSum.scratch(bits, n, piece, kv_wide)
    plane_scratch += PlaneSum.scratch(bits, each, heads * dim) + PlaneSum.scratch(bits, each, wide)
    shapes = [
        jax.ShapeDtypeStruct(shape, f32) for shape in (
            x.shape, (each, heads * dim), (each, kv_heads * dim), (each, kv_heads * dim), (heads, each),
            (heads * dim, each), (1, width), (1, width), (1, dim), (1, dim))
    ]
    line = line_scratch(n, seqs, rows, min(tail_piece, piece), width)
    return pl.pallas_call(
        functools.partial(layer_back_kernel, n, bits, n_uly, heads, kv_heads, dim),
        in_specs=[anywhere] * 3 + [vm] * 17,
        out_specs=[vm] * len(shapes),
        out_shape=shapes,
        scratch_shapes=[
            pltpu.VMEM((tokens, wide), bf16), pltpu.VMEM((n * piece, wide), bf16), pltpu.VMEM((tokens, width), bf16),
            pltpu.VMEM((n, piece, kv_wide), bf16), *line[:3],
            pltpu.VMEM((2, tokens, each), bf16), pltpu.SemaphoreType.DMA((2,)),
            pltpu.VMEM((steps + 1, 1, small), f32), pltpu.VMEM((steps, 1, small), f32),
            pltpu.SemaphoreType.DMA((steps,)), pltpu.SemaphoreType.DMA((steps,)),
            *plane_scratch,
        ],
        compiler_params=pltpu.CompilerParams(
            collective_id=collective_id, has_side_effects=True, vmem_limit_bytes=vmem_bytes),
        cost_estimate=cost(4 * tokens * width * wide, 250_000_000),
        name="layer_back",
    )(d_kv.reshape(seqs, places * n, cut_count, piece, kv_wide), first, d_branch, tiles(d_q), tiles(d_logit), tiles(nk),
      tiles(rk), *[t.reshape(n, cut_count, piece, dim) for t in tables], key_norm[None], *weights, gated, x,
      attn_norm[None], d_mid, d_qgain, d_mlp)


class LineSpread(LineSum):
    def __init__(self, n, pieces, own, out_at, sems):
        super().__init__(n, pieces, None, own, None, (None, None, *sems), out_at)
        self.stages = [self.own_step] + [functools.partial(self.spread_step, k) for k in range(2, n + 1)]

    def own_step(self, s):
        self.out_at(self.me, s)[...] = self.own(s)
        self.spread_step(1, s)


class PlaneSpread:
    def __init__(self, bits, n_uly, block, send, recv):
        self.bits, self.n_uly, self.block, self.send, self.recv = bits, n_uly, block, send, recv
        self.me = plane_place(n_uly)
        self.orders = [w + [0] for w in ways(bits)]

    def copy(self, d, level, e):
        bit = 1 << self.orders[d][level]
        block = self.block(self.me ^ e, d)
        return pltpu.make_async_remote_copy(
            src_ref=block, dst_ref=block, send_sem=self.send.at[d, e | bit], recv_sem=self.recv.at[d, e | bit],
            device_id=plane_device(self.me ^ bit, self.n_uly), device_id_type=MESH)

    def pass_on(self, d, first, e):
        for level in range(first, self.bits):
            self.copy(d, level, e).start()

    def begin(self):
        for d in range(2):
            self.pass_on(d, 0, 0)

    def take(self, level):
        for d in range(2):
            for e in span(self.orders[d][:level]):
                self.copy(d, level, e).wait_recv()
                self.pass_on(d, level + 1, e | (1 << self.orders[d][level]))

    def finish(self):
        for d in range(2):
            for level in range(self.bits):
                for e in span(self.orders[d][:level]):
                    self.copy(d, level, e).wait_send()


def layer_front_kernel(
    n, bits, n_uly, heads, kv_heads, dim, scale, x_ref, gain_ref, wq_ref, wk_ref, wv_ref, wg_ref, cos_ref, sin_ref,
    qg_ref, kg_ref, a1_ref, q_ref, kv_ref, nq_ref, nk_ref, rq_ref, rk_ref, logit_ref, ag_send, ag_recv, kv_send,
    kv_recv,
):
    seqs, _, cut_count, piece, width = a1_ref.shape
    cuts = [(q, c) for q in range(seqs) for c in range(cut_count)]
    place = plane_place(n_uly)
    tokens = n * piece
    half = kv_heads * dim

    def own(s):
        q, c = cuts[s]
        x = x_ref[q, c * piece:(c + 1) * piece].astype(f32)
        return (x * rms_inverse(x) * gain_ref[...]).astype(bf16)

    line = LineSpread(
        n, len(cuts), own, lambda owner, s: a1_ref.at[cuts[s][0], owner, cuts[s][1]], (ag_send, ag_recv))

    def keys(s):
        q, c = cuts[s]
        return PlaneSpread(
            bits, n_uly,
            lambda at, d: kv_ref.at[q, pl.ds(pl.multiple_of(at * n, n), n), c, :, pl.ds(d * half, half)],
            kv_send.at[s], kv_recv.at[s])

    spreads = [keys(s) for s in range(len(cuts))]

    def turn(s):
        q, c = cuts[s]
        a1 = a1_ref[q, :, c].reshape(tokens, width)
        cosine, sine = cos_ref[:, c].reshape(tokens, dim), sin_ref[:, c].reshape(tokens, dim)

        def tiles(values):
            return values.reshape(n, piece, values.shape[-1])

        def rope(unit, gain):
            scaled = unit * gain
            return scaled * cosine + pltpu.roll(scaled, dim // 2, 1) * sine

        mine = pl.ds(pl.multiple_of(place * n, n), n)
        raw = mm(a1, wk_ref[...])
        for h in range(kv_heads):
            at = slice(h * dim, (h + 1) * dim)
            values = raw[:, at]
            inverse = rms_inverse(values)
            unit = values * inverse
            kv_ref[q, mine, c, :, at] = tiles(rope(unit, kg_ref[...]).astype(bf16))
            nk_ref[q, :, c, :, at] = tiles(unit.astype(bf16))
            rk_ref[q, :, c, :, h:h + 1] = tiles(inverse)
        kv_ref[q, mine, c, :, half:] = tiles(mm(a1, wv_ref[...]).astype(bf16))
        spreads[s].begin()
        raw = mm(a1, wq_ref[...])
        for h in range(heads):
            at = slice(h * dim, (h + 1) * dim)
            values = raw[:, at]
            inverse = rms_inverse(values)
            unit = values * inverse
            q_ref[q, :, c, :, at] = tiles((rope(unit, qg_ref[...]) * (scale * log2e)).astype(bf16))
            nq_ref[q, :, c, :, at] = tiles(unit.astype(bf16))
            rq_ref[q, :, c, :, h:h + 1] = tiles(inverse)
        logit_ref[q, :, c] = tiles(mm(a1, wg_ref[...], NT).astype(bf16).astype(f32))

    line_and_plane_barrier(n, lax.axis_index("tp"), bits, n_uly)
    for step in range(len(cuts) + n - 1 + bits):
        for s in range(len(cuts)):
            stage = step - s
            if 0 <= stage < n:
                line.stages[stage](s)
                if stage == n - 1:
                    turn(s)
        for s in range(len(cuts)):
            level = step - s - n
            if 0 <= level < bits:
                spreads[s].take(level)
    line.drain_spread()
    for spread in spreads:
        spread.finish()


def layer_front(x, attn_norm, w_query, w_key, w_value, w_headgate, tables, query_norm, key_norm, n, sizes, scale,
                collective_id):
    n_ctx, n_uly = sizes
    places = n_ctx * n_uly
    bits = places.bit_length() - 1
    seqs, rows, width = x.shape
    dim = query_norm.shape[0]
    heads, kv_heads = w_query.shape[1] // dim, w_key.shape[1] // dim
    piece = min(64, rows)
    cut_count = rows // piece
    pieces = seqs * cut_count
    vm = pl.BlockSpec(memory_space=pltpu.VMEM)

    def tiled(devices, cols, kind):
        return jax.ShapeDtypeStruct((seqs, devices * n, cut_count, piece, cols), kind)

    shapes = [
        tiled(1, width, bf16), tiled(1, heads * dim, bf16), tiled(places, 2 * kv_heads * dim, bf16),
        tiled(1, heads * dim, bf16), tiled(1, kv_heads * dim, bf16), tiled(1, heads, f32), tiled(1, kv_heads, f32),
        tiled(1, heads, f32),
    ]
    line_sems = [pltpu.SemaphoreType.DMA((2, n - 1, pieces))] * 2
    plane_sems = [pltpu.SemaphoreType.DMA((pieces, 2, places))] * 2
    made = pl.pallas_call(
        functools.partial(layer_front_kernel, n, bits, n_uly, heads, kv_heads, dim, scale),
        in_specs=[vm] * 10,
        out_specs=[vm] * len(shapes),
        out_shape=shapes,
        scratch_shapes=[*line_sems, *plane_sems],
        compiler_params=params(collective_id=collective_id, has_side_effects=True),
        cost_estimate=cost(2 * seqs * n * rows * width * 1024, 200_000_000),
        name="layer_front",
    )(x, attn_norm[None], w_query, w_key, w_value, w_headgate.T,
      *[t.reshape(n, cut_count, piece, dim) for t in tables], query_norm[None], key_norm[None])
    return [m.reshape(seqs, -1, m.shape[-1]) for m in made]


def finish_kernel(count, *refs):
    sources, mid_ref, adds, targets, out_ref = refs[:count], refs[count], refs[count + 1:-count - 1], refs[-count - 1:-1], refs[-1]
    for source, target in zip(sources, targets):
        target[...] = source[...]
    first = 0
    for add_ref in adds:
        last = first + add_ref.shape[0]
        out_ref[first:last] = (mid_ref[first:last] + add_ref[...].astype(f32)).astype(bf16)
        first = last


def finish(sources, middle, adds):
    vm = pl.BlockSpec(memory_space=pltpu.VMEM)
    count = len(sources)
    made = pl.pallas_call(
        functools.partial(finish_kernel, count),
        in_specs=[vm] * (count + 1 + len(adds)),
        out_specs=[vm] * (count + 1),
        out_shape=[jax.ShapeDtypeStruct(s.shape, s.dtype) for s in sources]
        + [jax.ShapeDtypeStruct(middle.shape, bf16)],
        compiler_params=params(),
        cost_estimate=cost(middle.size, 20 * middle.size),
        name="finish",
    )(*sources, middle, *adds)
    return made[:-1], made[-1]


def flatten(values):
    return values.reshape(-1, values.shape[-1])


def spread(values):
    return lax.all_gather(values.astype(bf16), "tp", axis=1, tiled=True)


def collect(values):
    return lax.psum_scatter(values.astype(bf16), "tp", scatter_dimension=1, tiled=True)


def per_device(sizes, inputs, doc_ids, attn_norm, w_query, w_key, w_value, w_headgate, query_norm, key_norm, w_output,
               mlp_norm, w_gate, w_up, w_down, cotangent):
    n_tensor = lax.axis_size("tp")
    n_uly = sizes[1]
    seqs, rows, width = inputs.shape
    group = rows * n_tensor
    dim = query_norm.shape[0]
    heads = w_query.shape[1] // dim
    kv_heads = w_key.shape[1] // dim
    scale = dim ** (-0.5)
    plane = ("ctx", "uly")
    place = lax.axis_index("ctx") * n_uly + lax.axis_index("uly")
    block_start = place * group
    positions = block_start + jnp.arange(group, dtype=jnp.int32)
    tables = lax.optimization_barrier(rope_tables(positions, dim))
    block = min(512, group)

    def wide(values):
        return values.reshape(seqs, group, -1)

    query_doc = lax.dynamic_slice_in_dim(doc_ids, block_start, group, 1)
    start = positions[None, :]
    for d in range(4):
        first_of = jnp.sum(((doc_ids >= 0) & (doc_ids < d)).astype(jnp.int32), axis=1)
        start = jnp.where(query_doc == d, first_of[:, None], start)
    lowest, highest = jnp.min(start, axis=1), jnp.max(start, axis=1)
    hi = jnp.full_like(lowest, (block_start + group + block - 1) // block)
    lo = lowest // block
    full_lo = jnp.clip((highest + block - 1) // block, lo, hi)
    full_hi = jnp.clip(jnp.full_like(lowest, (block_start + 1) // block), full_lo, hi)
    bounds = jnp.stack([lo, full_lo, full_hi, hi], axis=1)

    pad = 128 - heads
    w_first = jnp.concatenate([w_query, w_key, w_value, jnp.pad(w_headgate, ((0, 0), (0, pad)))], axis=1)
    q_cols, kv_cols = heads * dim, kv_heads * dim
    n_main = q_cols + 2 * kv_cols

    if fits_plane(sizes, width):
        first, q, kv, nq, nk, rq, rk, logits = layer_front(
            inputs, attn_norm, w_query, w_key, w_value, w_headgate, tables, query_norm, key_norm, n_tensor, sizes, scale,
            0)
    else:
        xs = inputs.astype(f32)
        inv_one = rms_inverse(xs)
        first = spread(xs * inv_one * attn_norm)
        q, kv, nq, nk, rq, rk, logits = (
            wide(m) for m in project(flatten(first), w_first, tables, query_norm, key_norm, heads, kv_heads, scale))
        kv = plane_gather(kv, sizes, 0)
    near = (seqs + 1) // 2
    early_cot, kv = lax.optimization_barrier((cotangent[:near], kv))
    cots = [spread(early_cot)]
    att, gated, lse = attend(q, kv, bounds, start[:, :, None], positions[:, None], logits, heads, kv_heads, dim, block)

    local = inputs.shape
    part, cots = lax.optimization_barrier((wide(mm(flatten(gated), w_output).astype(bf16)), cots))
    second, middle = line_call(
        norm_forward_kernel, n_tensor, local, part,
        (inputs, mlp_norm[None]), (), 1, "norm_forward")

    if near < seqs:
        late_cot, second = lax.optimization_barrier((cotangent[near:], second))
        cots.append(spread(late_cot))
    a2 = flatten(second)
    gate, up = mm(a2, w_gate), mm(a2, w_up)
    sig = jax.nn.sigmoid(gate)
    silu = gate * sig
    hidden = (silu * up).astype(bf16)
    made, cots = lax.optimization_barrier((wide(mm(hidden, w_down).astype(bf16)), cots))
    outs = [collect(made[:near])]
    cot = flatten(jnp.concatenate(cots, axis=0))
    d_hidden = mm(cot, w_down, NT)
    d_gate = (d_hidden * up * sig * (1.0 + gate * (1.0 - sig))).astype(bf16)
    d_up = (d_hidden * silu).astype(bf16)
    d_second = (mm(d_gate, w_gate, NT) + mm(d_up, w_up, NT)).astype(bf16)
    d_branch, d_mid, grad_mlp_norm, grad_gate, grad_up, grad_down = norm_back(
        wide(d_second), cotangent, middle, mlp_norm, a2, cot, d_gate, d_up, hidden, n_tensor, sizes, 2)

    if near < seqs:
        late_made, d_branch = lax.optimization_barrier((made[near:], d_branch))
        outs.append(collect(late_made))
    d_gated = wide(mm(flatten(d_branch), w_output, NT).astype(bf16))
    d_q, d_logit, d_kv, d_qgain, grad_gate, grad_up, grad_down = attend_back(
        q, kv, d_gated, att, logits, logits.transpose(0, 2, 1), lse, bounds, start[:, None, :], positions[None, :], nq,
        rq, tables, query_norm, (grad_gate, grad_up, grad_down), heads, kv_heads, dim, block, scale)
    d_logit = jnp.pad(d_logit.astype(bf16).transpose(0, 2, 1), ((0, 0), (0, 0), (0, pad)))
    if fits_plane(sizes, width):
        grad_inputs, *grads = layer_back(
            d_kv, flatten(first), flatten(d_branch), d_q, d_logit, nk, rk, tables, key_norm,
            (w_query, w_key, w_value, w_headgate.T), flatten(gated), inputs, attn_norm, d_mid, d_qgain, grad_mlp_norm, n_tensor, sizes, heads, kv_heads, 3)
        (grad_inputs, grad_query, grad_key, grad_value, grad_headgate, grad_output), outputs = finish(
            (grad_inputs, *grads[:5]), middle, outs)
        grad_headgate = grad_headgate.T
        grad_attn_norm, grad_mlp_norm, grad_query_norm, grad_key_norm = (g[0] for g in grads[5:])
    else:
        outputs = (middle + jnp.concatenate(outs, axis=0).astype(f32)).astype(bf16)
        d_kv = blocks_sum(d_kv, sizes, 3)
        d_kv, d_kgain = key_back(d_kv, nk, rk, tables, key_norm, kv_heads, dim)
        d_all = flatten(jnp.concatenate([d_q, d_kv, d_logit], axis=-1))
        d_first = collect(wide(mm(d_all, w_first, NT))).astype(f32)

        grad_first, grad_output = outer_sums(
            (flatten(first), flatten(d_branch)), (0, 1), (d_all, flatten(gated)), sizes, 4)

        share = grad_first.shape[0]
        own_rows = lax.dynamic_slice_in_dim(w_first, place * share, share, 0).astype(f32)
        own_norm = jnp.sum(grad_first * own_rows, axis=1) / lax.dynamic_slice_in_dim(attn_norm, place * share, share, 0)
        grad_attn_norm = lax.dynamic_update_slice_in_dim(jnp.zeros((width,), f32), own_norm, place * share, 0)
        grad_attn_norm, grad_query_norm, grad_key_norm, grad_mlp_norm = lax.psum(
            (grad_attn_norm, d_qgain[0], d_kgain[0], grad_mlp_norm[0]), ("ctx", "uly", "tp"))

        unit = xs * inv_one
        inner = d_first * attn_norm
        grad_inputs = d_mid + inv_one * (inner - unit * jnp.mean(inner * unit, axis=-1, keepdims=True))
        grad_query, grad_key = grad_first[:, :q_cols], grad_first[:, q_cols:q_cols + kv_cols]
        grad_value, grad_headgate = grad_first[:, q_cols + kv_cols:n_main], grad_first[:, n_main:n_main + heads]
        grad_output = grad_output.T
    return (
        outputs,
        grad_inputs,
        grad_attn_norm,
        grad_query,
        grad_key,
        grad_value,
        grad_headgate,
        grad_query_norm,
        grad_key_norm,
        grad_output,
        grad_mlp_norm,
        grad_gate,
        grad_up,
        grad_down,
    )


def solution(mesh):
    tokens = P(None, ("ctx", "uly", "tp"), None)
    column, line, whole = P(None, "tp"), P("tp", None), P()
    rows_split, cols_split = P(("ctx", "uly"), "tp"), P("tp", ("ctx", "uly"))
    return jax.shard_map(
        functools.partial(per_device, (mesh.shape["ctx"], mesh.shape["uly"])),
        mesh=mesh,
        in_specs=(
            tokens, whole, whole, column, column, column, column, whole, whole, line, whole, column, column, line,
            tokens,
        ),
        out_specs=(
            tokens, tokens, whole, rows_split, rows_split, rows_split, rows_split, whole, whole, cols_split, whole,
            rows_split, rows_split, cols_split,
        ),
        check_vma=False,
    )
```

```python
import functools
import math

import jax
import jax.numpy as jnp
from jax import lax
from jax.experimental import pallas as pl
from jax.experimental.pallas import tpu as pltpu
from jax.sharding import PartitionSpec as P

epsilon = 1e-06
rope_base = 1000000.0
log2e = 1.0 / math.log(2.0)
bf16 = jnp.bfloat16
f32 = jnp.float32
back_quiet = (0, 2)
back_piece = 32
tail_piece = 64
tail_items = 3
vmem_bytes = 61 * 1024 * 1024

MESH = pl.DeviceIdType.MESH
NT = (((1,), (1,)), ((), ()))
NN = (((1,), (0,)), ((), ()))
TN = (((0,), (0,)), ((), ()))


def mm(left, right, dims=NN):
    return lax.dot_general(left, right, dims, preferred_element_type=f32)


def params(**more):
    return pltpu.CompilerParams(vmem_limit_bytes=vmem_bytes, **more)


def cost(flops, moved, trans=0):
    return pl.CostEstimate(flops=int(flops), bytes_accessed=int(moved), transcendentals=int(trans))


def full(shape):
    return pl.BlockSpec(shape, lambda *_: (0,) * len(shape))


def rms_inverse(values):
    return lax.rsqrt(jnp.mean(values * values, axis=-1, keepdims=True) + epsilon)


def rope_tables(positions, head_dim):
    half = head_dim // 2
    frequency = rope_base ** (-(jnp.arange(half, dtype=f32) * 2.0 / head_dim))
    angles = positions.astype(f32)[:, None] * frequency[None, :]
    cosine, sine = jnp.cos(angles), jnp.sin(angles)
    return jnp.concatenate([cosine, cosine], 1), jnp.concatenate([-sine, sine], 1)


def project_kernel(heads, kv_heads, dim, scale, x_ref, w_ref, cos_ref, sin_ref, qg_ref, kg_ref,
                   q_ref, kv_ref, nq_ref, nk_ref, rq_ref, rk_ref, logit_ref):
    cosine, sine = cos_ref[...], sin_ref[...]
    raw = mm(x_ref[...], w_ref[...])

    def rope(unit, gain):
        scaled = unit * gain
        return scaled * cosine + pltpu.roll(scaled, dim // 2, 1) * sine

    for h in range(heads + kv_heads):
        values = raw[:, h * dim:(h + 1) * dim]
        inverse = rms_inverse(values)
        unit = values * inverse
        if h < heads:
            at = slice(h * dim, (h + 1) * dim)
            q_ref[:, at] = (rope(unit, qg_ref[...]) * (scale * log2e)).astype(bf16)
            nq_ref[:, at] = unit.astype(bf16)
            rq_ref[:, h:h + 1] = inverse
        else:
            g = h - heads
            at = slice(g * dim, (g + 1) * dim)
            kv_ref[:, at] = rope(unit, kg_ref[...]).astype(bf16)
            nk_ref[:, at] = unit.astype(bf16)
            rk_ref[:, g:g + 1] = inverse
    first = (heads + kv_heads) * dim
    kv_ref[:, kv_heads * dim:] = raw[:, first:first + kv_heads * dim].astype(bf16)
    first += kv_heads * dim
    logit_ref[...] = raw[:, first:first + heads].astype(bf16).astype(f32)


def project(x, w, tables, query_norm, key_norm, heads, kv_heads, scale, block=256):
    rows, width = x.shape
    dim = query_norm.shape[0]
    cosine, sine = tables
    block = min(block, cosine.shape[0])
    around = cosine.shape[0] // block
    kernel = functools.partial(project_kernel, heads, kv_heads, dim, scale)

    def by_row(cols):
        return pl.BlockSpec((block, cols), lambda i: (i, 0))

    table = pl.BlockSpec((block, dim), lambda i: (i % around, 0))
    shapes = [
        (heads * dim, bf16), (2 * kv_heads * dim, bf16), (heads * dim, bf16), (kv_heads * dim, bf16),
        (heads, f32), (kv_heads, f32), (heads, f32),
    ]
    return pl.pallas_call(
        kernel,
        grid=(rows // block,),
        in_specs=[by_row(width), full(w.shape), table, table, full((1, dim)), full((1, dim))],
        out_specs=[by_row(c) for c, _ in shapes],
        out_shape=[jax.ShapeDtypeStruct((rows, c), t) for c, t in shapes],
        compiler_params=params(),
        cost_estimate=cost(2 * rows * width * w.shape[1], 2 * (rows * width + w.size) + rows * 4096),
        name="project",
    )(x, w, cosine, sine, query_norm[None], key_norm[None])


def bounds_loop(bounds_ref, row, body):
    lo, full_lo, full_hi, hi = (bounds_ref[row, i] for i in range(4))
    lax.fori_loop(lo, full_lo, lambda j, c: body(j, True), None)
    lax.fori_loop(full_lo, full_hi, lambda j, c: body(j, False), None)
    lax.fori_loop(full_hi, hi, lambda j, c: body(j, True), None)


def attend_kernel(heads, kv_heads, dim, block, bounds_ref, q_ref, kv_ref, start_ref, pos_ref, logit_ref,
                  att_ref, gated_ref, lse_ref, q2_ref, acc_ref, sum_ref):
    row = pl.program_id(0)
    group = q_ref.shape[1]
    repeat = heads // kv_heads
    for h in range(kv_heads):
        for g in range(repeat):
            at = slice((h * repeat + g) * dim, (h * repeat + g + 1) * dim)
            q2_ref[g * group:(g + 1) * group, :] = q_ref[0, :, at]
        acc_ref[...] = jnp.zeros_like(acc_ref)
        sum_ref[...] = jnp.zeros_like(sum_ref)

        def body(j, masked):
            at = pl.ds(pl.multiple_of(j * block, block), block)
            keys = kv_ref[0, at, h * dim:(h + 1) * dim]
            values = kv_ref[0, at, (kv_heads + h) * dim:(kv_heads + h + 1) * dim]
            if masked:
                spot = j * block + lax.broadcasted_iota(jnp.int32, (group, block), 1)
                allowed = (spot >= start_ref[0]) & (spot <= pos_ref[...])
            for g in range(repeat):
                part = slice(g * group, (g + 1) * group)
                weight = jnp.exp2(mm(q2_ref[part, :], keys, NT))
                if masked:
                    weight = jnp.where(allowed, weight, 0.0)
                total = weight[:, :dim]
                for i in range(1, block // dim):
                    total = total + weight[:, i * dim:(i + 1) * dim]
                sum_ref[part, :] += total
                acc_ref[part, :] += mm(weight.astype(bf16), values)

        bounds_loop(bounds_ref, row, body)
        for g in range(repeat):
            part = slice(g * group, (g + 1) * group)
            n = h * repeat + g
            at = slice(n * dim, (n + 1) * dim)
            total = jnp.sum(sum_ref[part, :], axis=1, keepdims=True)
            attended = acc_ref[part, :] / total
            att_ref[0, :, at] = attended.astype(bf16)
            gated_ref[0, :, at] = (attended * jax.nn.sigmoid(logit_ref[0, :, n:n + 1])).astype(bf16)
            lse_ref[0, n:n + 1, :] = jnp.log2(jnp.sum(sum_ref[part, :].T, axis=0, keepdims=True))


def attend(q, kv, bounds, start_col, pos_col, logits, heads, kv_heads, dim, block):
    rows, group, width = q.shape
    total = kv.shape[1]
    repeat = heads // kv_heads

    def by_row(*shape):
        return pl.BlockSpec((1, *shape), lambda r, *_: (r, 0, 0))

    return pl.pallas_call(
        functools.partial(attend_kernel, heads, kv_heads, dim, block),
        grid_spec=pltpu.PrefetchScalarGridSpec(
            num_scalar_prefetch=1,
            grid=(rows,),
            in_specs=[
                by_row(group, width), by_row(total, kv.shape[2]), by_row(group, 1), full((group, 1)),
                by_row(group, heads),
            ],
            out_specs=[by_row(group, width), by_row(group, width), by_row(heads, group)],
            scratch_shapes=[
                pltpu.VMEM((repeat * group, dim), bf16),
                pltpu.VMEM((repeat * group, dim), f32),
                pltpu.VMEM((repeat * group, dim), f32),
            ],
        ),
        out_shape=[
            jax.ShapeDtypeStruct((rows, group, width), bf16),
            jax.ShapeDtypeStruct((rows, group, width), bf16),
            jax.ShapeDtypeStruct((rows, heads, group), f32),
        ],
        compiler_params=params(),
        cost_estimate=cost(
            2 * rows * heads * group * total * dim, 2 * kv.size + 6 * q.size, rows * heads * group * total // 2
        ),
        name="attend",
    )(bounds, q, kv, start_col, pos_col, logits)


def attend_back_kernel(heads, kv_heads, dim, block, scale, bounds_ref, q_ref, kv_ref, dgated_ref, att_ref,
                       logit_ref, logit_row_ref, lse_ref, start_ref, pos_ref, nq_ref, rq_ref, cos_ref, sin_ref,
                       gain_ref, ggate_ref, gup_ref, gdown_ref, dq_ref, dlogit_ref, dkv_ref, dgain_ref, ggate_out,
                       gup_out, gdown_out, q2_ref, da2_ref, delta_ref, lse2_ref, dq2_ref, *moved):
    row = pl.program_id(0)
    slots, move_sems = moved[:3], moved[3]
    takes = [
        pltpu.make_async_copy(source, slot, move_sems.at[0, i])
        for i, (source, slot) in enumerate(zip((ggate_ref, gup_ref, gdown_ref), slots))
    ]
    gives = [
        pltpu.make_async_copy(slot, target, move_sems.at[1, i])
        for i, (slot, target) in enumerate(zip(slots, (ggate_out, gup_out, gdown_out)))
    ]

    @pl.when(row == 0)
    def _():
        for move in takes:
            move.start()

    group = q_ref.shape[1]
    repeat = heads // kv_heads
    cosine, sine, gain = cos_ref[...], sin_ref[...], gain_ref[...]

    @pl.when(row == 0)
    def _():
        dgain_ref[...] = jnp.zeros_like(dgain_ref)

    dkv_ref[...] = jnp.zeros_like(dkv_ref)
    for h in range(kv_heads):
        for g in range(repeat):
            n = h * repeat + g
            at = slice(n * dim, (n + 1) * dim)
            part = slice(g * group, (g + 1) * group)
            q2_ref[part, :] = q_ref[0, :, at]
            grad = dgated_ref[0, :, at].astype(f32)
            sigma = jax.nn.sigmoid(logit_ref[0, :, n:n + 1])
            da2_ref[part, :] = (grad * sigma).astype(bf16)
            dot = jnp.sum((grad * att_ref[0, :, at].astype(f32)).T, axis=0, keepdims=True)
            sigma_row = jax.nn.sigmoid(logit_row_ref[0, n:n + 1, :])
            dlogit_ref[0, n:n + 1, :] = dot * sigma_row * (1.0 - sigma_row)
            delta_ref[:, part] = dot * sigma_row
            lse2_ref[:, part] = lse_ref[0, n:n + 1, :]
        dq2_ref[...] = jnp.zeros_like(dq2_ref)

        def body(j, masked):
            at = pl.ds(pl.multiple_of(j * block, block), block)
            keys = kv_ref[0, at, h * dim:(h + 1) * dim]
            values = kv_ref[0, at, (kv_heads + h) * dim:(kv_heads + h + 1) * dim]
            if masked:
                spot = j * block + lax.broadcasted_iota(jnp.int32, (block, group), 0)
                allowed = (spot >= start_ref[0]) & (spot <= pos_ref[...])
            dk = jnp.zeros((block, dim), f32)
            dv = jnp.zeros((block, dim), f32)
            for g in range(repeat):
                part = slice(g * group, (g + 1) * group)
                weight = jnp.exp2(mm(keys, q2_ref[part, :], NT) - lse2_ref[:, part])
                if masked:
                    weight = jnp.where(allowed, weight, 0.0)
                dv += mm(weight.astype(bf16), da2_ref[part, :])
                dprob = mm(values, da2_ref[part, :], NT)
                dscore = (weight * (dprob - delta_ref[:, part])).astype(bf16)
                dk += mm(dscore, q2_ref[part, :])
                dq2_ref[part, :] += mm(dscore, keys, TN)
            dkv_ref[0, at, h * dim:(h + 1) * dim] = (dk * (1.0 / log2e)).astype(bf16)
            dkv_ref[0, at, (kv_heads + h) * dim:(kv_heads + h + 1) * dim] = dv.astype(bf16)

        bounds_loop(bounds_ref, row, body)
        for g in range(repeat):
            n = h * repeat + g
            at = slice(n * dim, (n + 1) * dim)
            part = slice(g * group, (g + 1) * group)
            turned = (dq2_ref[part, :] * scale).astype(bf16).astype(f32)
            back = turned * cosine - pltpu.roll(turned, dim // 2, 1) * sine
            unit = nq_ref[0, :, at].astype(f32)
            dgain_ref[...] += jnp.sum(back * unit, axis=0, keepdims=True)
            inner = back * gain
            mean = jnp.mean(inner * unit, axis=1, keepdims=True)
            dq_ref[0, :, at] = (rq_ref[0, :, n:n + 1] * (inner - unit * mean)).astype(bf16)

    @pl.when(row == 0)
    def _():
        for take, give in zip(takes, gives):
            take.wait()
            give.start()

    @pl.when(row == pl.num_programs(0) - 1)
    def _():
        for give in gives:
            give.wait()


def attend_back(q, kv, dgated, att, logits, logit_rows, lse, bounds, start_row, pos_row, nq, rq, tables, gain, moved,
                heads, kv_heads, dim, block, scale):
    rows, group, width = q.shape
    total = kv.shape[1]
    repeat = heads // kv_heads
    cosine, sine = tables

    def by_row(*shape):
        return pl.BlockSpec((1, *shape), lambda r, *_: (r, 0, 0))

    wide = by_row(group, width)
    return pl.pallas_call(
        functools.partial(attend_back_kernel, heads, kv_heads, dim, block, scale),
        grid_spec=pltpu.PrefetchScalarGridSpec(
            num_scalar_prefetch=1,
            grid=(rows,),
            in_specs=[
                wide, by_row(total, kv.shape[2]), wide, wide, by_row(group, heads), by_row(heads, group),
                by_row(heads, group), by_row(1, group), full((1, group)), wide, by_row(group, heads),
                full((group, dim)), full((group, dim)), full((1, dim)), *[pl.BlockSpec(memory_space=pl.ANY)] * 3,
            ],
            out_specs=[
                wide, by_row(heads, group), by_row(total, kv.shape[2]), full((1, dim)),
                *[pl.BlockSpec(memory_space=pl.ANY)] * 3,
            ],
            scratch_shapes=[
                pltpu.VMEM((repeat * group, dim), bf16),
                pltpu.VMEM((repeat * group, dim), bf16),
                pltpu.VMEM((1, repeat * group), f32),
                pltpu.VMEM((1, repeat * group), f32),
                pltpu.VMEM((repeat * group, dim), f32),
                *[pltpu.VMEM(m.shape, m.dtype) for m in moved],
                pltpu.SemaphoreType.DMA((2, 3)),
            ],
        ),
        out_shape=[
            jax.ShapeDtypeStruct((rows, group, width), bf16),
            jax.ShapeDtypeStruct((rows, heads, group), f32),
            jax.ShapeDtypeStruct(kv.shape, bf16),
            jax.ShapeDtypeStruct((1, dim), f32),
            *[jax.ShapeDtypeStruct(m.shape, m.dtype) for m in moved],
        ],
        compiler_params=params(),
        cost_estimate=cost(
            5 * rows * heads * group * total * dim, 4 * kv.size + 10 * q.size, rows * heads * group * total // 2
        ),
        name="attend_back",
    )(bounds, q, kv, dgated, att, logits, logit_rows, lse, start_row, pos_row, nq, rq, cosine, sine, gain[None], *moved)


def key_back_kernel(kv_heads, dim, dkv_ref, nk_ref, rk_ref, cos_ref, sin_ref, gain_ref, dk_ref, dgain_ref):
    @pl.when(pl.program_id(0) == 0)
    def _():
        dgain_ref[...] = jnp.zeros_like(dgain_ref)

    for h in range(kv_heads):
        at = slice(h * dim, (h + 1) * dim)
        turned = dkv_ref[0, :, at].astype(f32)
        back = turned * cos_ref[...] - pltpu.roll(turned, dim // 2, 1) * sin_ref[...]
        unit = nk_ref[0, :, at].astype(f32)
        dgain_ref[...] += jnp.sum(back * unit, axis=0, keepdims=True)
        inner = back * gain_ref[...]
        mean = jnp.mean(inner * unit, axis=1, keepdims=True)
        dk_ref[0, :, at] = (rk_ref[0, :, h:h + 1] * (inner - unit * mean)).astype(bf16)
    dk_ref[0, :, kv_heads * dim:] = dkv_ref[0, :, kv_heads * dim:]


def key_back(dkv, nk, rk, tables, gain, kv_heads, dim):
    rows, group, width = dkv.shape

    def by_row(*shape):
        return pl.BlockSpec((1, *shape), lambda r: (r, 0, 0))

    return pl.pallas_call(
        functools.partial(key_back_kernel, kv_heads, dim),
        grid=(rows,),
        in_specs=[
            by_row(group, width), by_row(group, kv_heads * dim), by_row(group, kv_heads), full((group, dim)),
            full((group, dim)), full((1, dim)),
        ],
        out_specs=[by_row(group, width), full((1, dim))],
        out_shape=[jax.ShapeDtypeStruct((rows, group, width), bf16), jax.ShapeDtypeStruct((1, dim), f32)],
        compiler_params=params(),
        cost_estimate=cost(20 * dkv.size, 6 * dkv.size),
        name="key_back",
    )(dkv, nk, rk, *tables, gain[None])


def hidden_back_kernel(parts, *refs):
    cots, (w_ref, gate_ref, up_ref, dgate_ref, dup_ref) = refs[:parts], refs[parts:]
    first = 0
    for cot_ref in cots:
        at = slice(first, first + cot_ref.shape[0])
        grad = mm(cot_ref[...], w_ref[...], NT)
        gate, up = gate_ref[at], up_ref[at]
        sigma = jax.nn.sigmoid(gate)
        dgate_ref[at] = (grad * up * sigma * (1.0 + gate * (1.0 - sigma))).astype(bf16)
        dup_ref[at] = (grad * gate * sigma).astype(bf16)
        first = at.stop


def hidden_back(cots, w_down, gate, up, block=256):
    units, width = w_down.shape
    tokens = gate.shape[0]
    column = pl.BlockSpec((tokens, block), lambda j: (0, j))
    return pl.pallas_call(
        functools.partial(hidden_back_kernel, len(cots)),
        grid=(units // block,),
        in_specs=[*[full(c.shape) for c in cots], pl.BlockSpec((block, width), lambda j: (j, 0)), column, column],
        out_specs=[column, column],
        out_shape=[jax.ShapeDtypeStruct((tokens, units), bf16)] * 2,
        compiler_params=params(),
        cost_estimate=cost(2 * tokens * units * width, 40_000_000),
        name="hidden_back",
    )(*cots, w_down, gate, up)


def second_back_kernel(dgate_ref, dup_ref, wgate_ref, wup_ref, out_ref):
    total = mm(dgate_ref[...], wgate_ref[...], NT) + mm(dup_ref[...], wup_ref[...], NT)
    out_ref[...] = total.astype(bf16)


def second_back(d_gate, d_up, w_gate, w_up, block=256):
    width, units = w_gate.shape
    tokens = d_gate.shape[0]
    rows = pl.BlockSpec((block, units), lambda j: (j, 0))
    return pl.pallas_call(
        second_back_kernel,
        grid=(width // block,),
        in_specs=[full(d_gate.shape), full(d_up.shape), rows, rows],
        out_specs=pl.BlockSpec((tokens, block), lambda j: (0, j)),
        out_shape=jax.ShapeDtypeStruct((tokens, width), bf16),
        compiler_params=params(),
        cost_estimate=cost(4 * tokens * units * width, 30_000_000),
        name="second_back",
    )(d_gate, d_up, w_gate, w_up)


def line_barrier(n, me):
    barrier = pltpu.get_barrier_semaphore()
    for way in (1, -1):
        @pl.when((me + way >= 0) & (me + way < n))
        def _():
            pl.semaphore_signal(barrier, inc=1, device_id={"tp": jnp.clip(me + way, 0, n - 1)}, device_id_type=MESH)
    edge = (me == 0) | (me == n - 1)

    @pl.when(edge)
    def _():
        pl.semaphore_wait(barrier, 1)

    @pl.when(jnp.logical_not(edge))
    def _():
        pl.semaphore_wait(barrier, 2)


def line_and_plane_barrier(n, me, bits, n_uly):
    barrier = pltpu.get_barrier_semaphore()
    place = plane_place(n_uly)
    for way in (1, -1):
        @pl.when((me + way >= 0) & (me + way < n))
        def _():
            pl.semaphore_signal(barrier, inc=1, device_id={"tp": jnp.clip(me + way, 0, n - 1)}, device_id_type=MESH)
    for b in range(bits):
        pl.semaphore_signal(barrier, inc=1, device_id=plane_device(place ^ (1 << b), n_uly), device_id_type=MESH)
    edge = (me == 0) | (me == n - 1)

    @pl.when(edge)
    def _():
        pl.semaphore_wait(barrier, bits + 1)

    @pl.when(jnp.logical_not(edge))
    def _():
        pl.semaphore_wait(barrier, bits + 2)


class LineSum:
    def __init__(self, n, pieces, part_at, own, land_ref, sems, out_at=None):
        self.n, self.pieces, self.part_at, self.own, self.land, self.out_at = n, pieces, part_at, own, land_ref, out_at
        self.rs_send, self.rs_recv = sems[:2]
        if out_at:
            self.ag_send, self.ag_recv = sems[2:]
        self.me = lax.axis_index("tp")
        self.stages = [functools.partial(self.reduce_step, k) for k in range(1, n)] + [self.own_step]
        if out_at:
            self.stages += [functools.partial(self.spread_step, k) for k in range(2, n + 1)]

    def inside(self, place):
        return (place >= 0) & (place < self.n)

    def near(self, way):
        return {"tp": jnp.clip(self.me + way, 0, self.n - 1)}

    def reduce_copy(self, way, k, s, source):
        d = 0 if way == 1 else 1
        return pltpu.make_async_remote_copy(
            src_ref=source, dst_ref=self.land.at[d, k - 1, s], send_sem=self.rs_send.at[d, k - 1, s],
            recv_sem=self.rs_recv.at[d, k - 1, s], device_id=self.near(way), device_id_type=MESH)

    def spread_copy(self, way, k, s, owner):
        d = 0 if way == 1 else 1
        rows = self.out_at(jnp.clip(owner, 0, self.n - 1), s)
        return pltpu.make_async_remote_copy(
            src_ref=rows, dst_ref=rows, send_sem=self.ag_send.at[d, k - 1, s], recv_sem=self.ag_recv.at[d, k - 1, s],
            device_id=self.near(way), device_id_type=MESH)

    def reduce_step(self, k, s):
        for way in (1, -1):
            d = 0 if way == 1 else 1
            first = jnp.logical_not(self.inside(self.me - way))
            dest = self.me + way * (self.n - k)
            part = self.part_at(jnp.clip(dest, 0, self.n - 1), s)

            @pl.when(first & self.inside(dest))
            def _():
                self.reduce_copy(way, k, s, part).start()

            if k > 1:
                @pl.when(self.inside(self.me - way) & self.inside(dest))
                def _():
                    landed = self.land.at[d, k - 2, s]
                    self.reduce_copy(way, k - 1, s, landed).wait_recv()
                    landed[...] = (part[...].astype(f32) + landed[...].astype(f32)).astype(bf16)
                    self.reduce_copy(way, k, s, landed).start()

    def own_step(self, s):
        for way in (1, -1):
            d = 0 if way == 1 else 1
            landed = self.land.at[d, self.n - 2, s]

            @pl.when(self.inside(self.me - way))
            def _():
                self.reduce_copy(way, self.n - 1, s, landed).wait_recv()

            @pl.when(jnp.logical_not(self.inside(self.me - way)))
            def _():
                landed[...] = jnp.zeros_like(landed)

        total = self.part_at(self.me, s)[...].astype(f32)
        for d in range(2):
            total = total + self.land[d, self.n - 2, s].astype(f32)
        rows = self.own(s, total)
        if self.out_at:
            self.out_at(self.me, s)[...] = rows
            self.spread_step(1, s)

    def spread_step(self, k, s):
        for way in (1, -1):
            owner = self.me - way * (k - 1)
            if k > 1:
                @pl.when(self.inside(owner))
                def _():
                    self.spread_copy(way, k - 1, s, owner).wait_recv()
            if k < self.n:
                @pl.when(self.inside(owner) & self.inside(self.me + way))
                def _():
                    self.spread_copy(way, k, s, owner).start()

    def drain_reduce(self):
        for s in range(self.pieces):
            for way in (1, -1):
                for k in range(1, self.n):
                    @pl.when(self.inside(self.me + way) & self.inside(self.me + way * (self.n - k)))
                    def _():
                        self.reduce_copy(way, k, s, self.land.at[0, 0, s]).wait_send()

    def drain_spread(self):
        for s in range(self.pieces):
            for way in (1, -1):
                for k in range(1, self.n):
                    owner = self.me - way * (k - 1)

                    @pl.when(self.inside(owner) & self.inside(self.me + way))
                    def _():
                        self.spread_copy(way, k, s, owner).wait_send()

    def run(self, beside=(), quiet=(0, 0)):
        beside, done = list(beside), 0
        steps = self.pieces + len(self.stages) - 1
        turns = [(step, s) for step in range(steps) for s in range(self.pieces) if 0 <= step - s < len(self.stages)]
        slots = [i for i, (step, _) in enumerate(turns) if quiet[0] <= step < steps - quiet[1]]
        for i, (step, s) in enumerate(turns):
            self.stages[step - s](s)
            if i in slots:
                until = len(beside) * (slots.index(i) + 1) // len(slots)
                for item in beside[done:until]:
                    item()
                done = until
        self.drain_reduce()
        self.drain_spread()


def line_all_sum(n, seqs, rows, piece, finish, part_ref, out_ref, land_ref, sems, beside=(), quiet=(0, 0)):
    cuts = [(q, c) for q in range(seqs) for c in range(rows // piece)]

    def at(ref):
        return lambda owner, s: ref.at[
            cuts[s][0], pl.ds(pl.multiple_of(owner * rows + cuts[s][1] * piece, piece), piece)]

    LineSum(n, len(cuts), at(part_ref), lambda s, total: finish(*cuts[s], total), land_ref, sems, at(out_ref)).run(
        beside, quiet)


def line_scratch(n, seqs, rows, piece, width):
    count = seqs * (rows // piece)
    return [
        pltpu.VMEM((2, n - 1, count, piece, width), bf16),
        pltpu.SemaphoreType.DMA((2, n - 1, count)), pltpu.SemaphoreType.DMA((2, n - 1, count)),
        pltpu.SemaphoreType.DMA((2, n - 1, count)), pltpu.SemaphoreType.DMA((2, n - 1, count)),
    ]


def norm_forward_kernel(n, seqs, rows, piece, part_ref, x_ref, gain_ref, out_ref, mid_ref, land_ref, *sems):
    def finish(q, c, total):
        at = slice(c * piece, (c + 1) * piece)
        mid = x_ref[q, at].astype(f32) + total
        mid_ref[q, at] = mid
        return (mid * rms_inverse(mid) * gain_ref[...]).astype(bf16)

    line_barrier(n, lax.axis_index("tp"))
    line_all_sum(n, seqs, rows, piece, finish, part_ref, out_ref, land_ref, sems)


def line_call(kernel, n, local, part, others, extra, collective_id, name):
    seqs, rows, width = local
    piece = min(32, rows)
    vm = pl.BlockSpec(memory_space=pltpu.VMEM)
    shapes = [jax.ShapeDtypeStruct(part.shape, bf16), jax.ShapeDtypeStruct(local, f32), *extra]
    return pl.pallas_call(
        functools.partial(kernel, n, seqs, rows, piece),
        in_specs=[vm] * (1 + len(others)),
        out_specs=[vm] * len(shapes),
        out_shape=shapes,
        scratch_shapes=line_scratch(n, seqs, rows, piece, width),
        compiler_params=params(collective_id=collective_id, has_side_effects=True),
        cost_estimate=cost(20 * part.size, 100_000_000),
        name=name,
    )(part, *others)


def plane_place(n_uly):
    return lax.axis_index("ctx") * n_uly + lax.axis_index("uly")


def plane_device(place, n_uly):
    return {"ctx": place // n_uly, "uly": lax.rem(place, n_uly)}


def plane_barrier(bits, me, n_uly):
    barrier = pltpu.get_barrier_semaphore()
    for b in range(bits):
        pl.semaphore_signal(barrier, inc=1, device_id=plane_device(me ^ (1 << b), n_uly), device_id_type=MESH)
    pl.semaphore_wait(barrier, bits)


def ways(bits):
    upper = list(range(1, bits))
    return upper, upper[::-1]


def span(order):
    out = [0]
    for b in order:
        out += [e | (1 << b) for e in out]
    return out


def plane_gather_kernel(bits, n_uly, own_ref, out_ref, copy_sem, send_sem, recv_sem):
    me = plane_place(n_uly)
    rows, half = own_ref.shape[1], own_ref.shape[2] // 2
    plane_barrier(bits, me, n_uly)
    orders = [w + [0] for w in ways(bits)]

    def block(place, d):
        return out_ref.at[:, pl.ds(pl.multiple_of(place * rows, rows), rows), pl.ds(d * half, half)]

    def copy(d, level, e):
        bit = orders[d][level]
        source = own_ref.at[:, :, pl.ds(d * half, half)] if e == 0 else block(me ^ e, d)
        return pltpu.make_async_remote_copy(
            src_ref=source, dst_ref=block(me ^ e, d), send_sem=send_sem.at[d, e | (1 << bit)],
            recv_sem=recv_sem.at[d, e | (1 << bit)], device_id=plane_device(me ^ (1 << bit), n_uly),
            device_id_type=MESH)

    own = [pltpu.make_async_copy(own_ref.at[:, :, pl.ds(d * half, half)], block(me, d), copy_sem.at[d]) for d in range(2)]
    for c in own:
        c.start()
    for level in range(bits):
        for d in range(2):
            for e in span(orders[d][:level]):
                if level > 0 and e >> orders[d][level - 1] & 1:
                    continue
                copy(d, level, e).start()
        for d in range(2):
            for e in span(orders[d][:level]):
                copy(d, level, e).wait_recv()
                if level + 1 < bits:
                    copy(d, level + 1, e | (1 << orders[d][level])).start()
    for d in range(2):
        own[d].wait()
        for level in range(bits):
            for e in span(orders[d][:level]):
                copy(d, level, e).wait_send()


def plane_gather(own, sizes, collective_id):
    n_ctx, n_uly = sizes
    count = n_ctx * n_uly
    bits = count.bit_length() - 1
    seqs, rows, width = own.shape
    if own.size * count * 2 > 12 << 20 or count != 1 << bits or bits < 2:
        return lax.all_gather(own, ("ctx", "uly"), axis=1, tiled=True)
    vm = pl.BlockSpec(memory_space=pltpu.VMEM)
    return pl.pallas_call(
        functools.partial(plane_gather_kernel, bits, n_uly),
        in_specs=[vm], out_specs=vm,
        out_shape=jax.ShapeDtypeStruct((seqs, rows * count, width), own.dtype),
        scratch_shapes=[pltpu.SemaphoreType.DMA((2,)), pltpu.SemaphoreType.DMA((2, count)), pltpu.SemaphoreType.DMA((2, count))],
        compiler_params=params(collective_id=collective_id, has_side_effects=True),
        cost_estimate=cost(0, 100_000_000),
        name="plane_gather",
    )(own)


class PlaneSum:
    def __init__(self, bits, n_uly, make, store, buf_ref, land_ref, send, recv):
        self.bits, self.n_uly, self.make, self.store = bits, n_uly, make, store
        self.buf, self.land, self.send, self.recv = buf_ref, land_ref, send, recv
        self.me = plane_place(n_uly)
        width = buf_ref.shape[-1]
        half = max(width // 256, 1) * 128
        self.parts = [(0, half), (half, width - half)]
        self.orders = ways(bits)

    @staticmethod
    def scratch(bits, rows, width):
        n = 1 << bits
        return [
            pltpu.VMEM((n, rows, width), bf16), pltpu.VMEM((n - 1, rows, width), bf16),
            pltpu.SemaphoreType.DMA((3, n)), pltpu.SemaphoreType.DMA((3, n)),
        ]

    def slot(self, e):
        return e

    def view(self, ref, i, d):
        return ref.at[(i, *[slice(None)] * (len(ref.shape) - 2), pl.ds(*self.parts[d]))]

    def first_copy(self, e):
        return pltpu.make_async_remote_copy(
            src_ref=self.buf.at[e], dst_ref=self.land.at[e - 1], send_sem=self.send.at[2, e],
            recv_sem=self.recv.at[2, e], device_id=plane_device(self.me ^ 1, self.n_uly), device_id_type=MESH)

    def copy(self, d, level, e):
        return pltpu.make_async_remote_copy(
            src_ref=self.view(self.buf, self.slot(e), d), dst_ref=self.view(self.land, e - 1, d),
            send_sem=self.send.at[d, e],
            recv_sem=self.recv.at[d, e],
            device_id=plane_device(self.me ^ (1 << self.orders[d][level]), self.n_uly), device_id_type=MESH)

    def sent(self, d, level):
        return [(1 << self.orders[d][level]) | e for e in span(self.orders[d][level + 1:])]

    def compute(self):
        n = 1 << self.bits
        for e in range(1, n, 2):
            self.buf[e] = self.make(self.me ^ e).astype(bf16)
            self.first_copy(e).start()
        for e in range(0, n, 2):
            self.buf[e] = self.make(self.me ^ e).astype(bf16)

    def pair(self):
        for e in range(1, 1 << self.bits, 2):
            self.first_copy(e).wait_recv()
            kept = self.slot(e - 1)
            self.buf[kept] = (self.buf[kept].astype(f32) + self.land[e - 1].astype(f32)).astype(bf16)

    def push(self, level):
        for d in range(2):
            for e in self.sent(d, level):
                self.copy(d, level, e).start()

    def pull(self, level):
        for d in range(2):
            for e in self.sent(d, level):
                kept = self.view(self.buf, self.slot(e ^ (1 << self.orders[d][level])), d)
                self.copy(d, level, e).wait_recv()
                total = kept[...].astype(f32) + self.view(self.land, e - 1, d)[...].astype(f32)
                if level == self.bits - 2:
                    self.store(pl.ds(*self.parts[d]), total)
                else:
                    kept[...] = total.astype(bf16)

    def finish(self):
        for e in range(1, 1 << self.bits, 2):
            self.first_copy(e).wait_send()
        for d in range(2):
            for level in range(self.bits - 1):
                for e in self.sent(d, level):
                    self.copy(d, level, e).wait_send()


def blocks_sum_kernel(bits, n_uly, parts_ref, out_ref, *scratch):
    me = plane_place(n_uly)
    plane_barrier(bits, me, n_uly)
    seqs, rows = out_ref.shape[0], out_ref.shape[1]

    def make(place):
        return parts_ref[:, pl.ds(pl.multiple_of(place * rows, rows), rows)].reshape(seqs * rows, -1)

    def store(at, total):
        out_ref[:, :, at] = total.reshape(seqs, rows, -1).astype(out_ref.dtype)

    job = PlaneSum(bits, n_uly, make, store, *scratch)
    job.compute()
    job.pair()
    for level in range(bits - 1):
        job.push(level)
        job.pull(level)
    job.finish()


def blocks_sum(parts, sizes, collective_id):
    n_ctx, n_uly = sizes
    count = n_ctx * n_uly
    bits = count.bit_length() - 1
    seqs, total, width = parts.shape
    rows = total // count
    if parts.size * 2 > 12 << 20 or count != 1 << bits or bits < 2:
        return lax.psum_scatter(parts, ("ctx", "uly"), scatter_dimension=1, tiled=True)
    vm = pl.BlockSpec(memory_space=pltpu.VMEM)
    return pl.pallas_call(
        functools.partial(blocks_sum_kernel, bits, n_uly),
        in_specs=[vm],
        out_specs=vm,
        out_shape=jax.ShapeDtypeStruct((seqs, rows, width), bf16),
        scratch_shapes=PlaneSum.scratch(bits, seqs * rows, width),
        compiler_params=params(collective_id=collective_id, has_side_effects=True),
        cost_estimate=cost(10 * parts.size, 100_000_000),
        name="blocks_sum",
    )(parts)


def outer_sums_kernel(bits, n_uly, use, *refs):
    count, kinds = len(use), max(use) + 1
    lefts, refs = [refs[k] for k in use], refs[kinds:]
    rights, outs, scratch = refs[:count], refs[count:2 * count], refs[2 * count:]
    plane_barrier(bits, plane_place(n_uly), n_uly)
    jobs = []
    for i in range(count):
        each = outs[i].shape[0]

        def make(place, i=i, each=each):
            left = lefts[i][:, pl.ds(pl.multiple_of(place * each, each), each)]
            return mm(left, rights[i][...], TN)

        def store(at, total, i=i):
            outs[i][:, at] = total

        jobs.append(PlaneSum(bits, n_uly, make, store, *scratch[4 * i:4 * i + 4]))
    last = bits - 2
    for i in range(count + last + 1):
        if i < count:
            jobs[i].compute()
            jobs[i].pair()
            jobs[i].push(0)
        for level in range(last + 1):
            j = i - 1 - level
            if 0 <= j < count:
                jobs[j].pull(level)
                if level < last:
                    jobs[j].push(level + 1)
                else:
                    jobs[j].finish()


def fits_plane(sizes, width):
    places = sizes[0] * sizes[1]
    return places & (places - 1) == 0 and places >= 4 and width // places % 128 == 0


def outer_sums(kinds, use, rights, sizes, collective_id):
    lefts = [kinds[k] for k in use]
    n_ctx, n_uly = sizes
    places = n_ctx * n_uly
    bits = places.bit_length() - 1
    count = len(lefts)
    if not fits_plane(sizes, lefts[0].shape[1]):
        return [
            lax.psum_scatter(mm(l, r, TN).astype(bf16), ("ctx", "uly"), scatter_dimension=0, tiled=True).astype(f32)
            for l, r in zip(lefts, rights)
        ]
    vm = pl.BlockSpec(memory_space=pltpu.VMEM)
    shapes = [(l.shape[1] // places, r.shape[1]) for l, r in zip(lefts, rights)]
    scratch = []
    for shape in shapes:
        scratch += PlaneSum.scratch(bits, *shape)
    work = sum(l.size * r.shape[1] for l, r in zip(lefts, rights))
    return pl.pallas_call(
        functools.partial(outer_sums_kernel, bits, n_uly, use),
        in_specs=[vm] * (len(kinds) + count),
        out_specs=[vm] * count,
        out_shape=[jax.ShapeDtypeStruct(s, f32) for s in shapes],
        scratch_shapes=scratch,
        compiler_params=pltpu.CompilerParams(
            collective_id=collective_id, has_side_effects=True, vmem_limit_bytes=vmem_bytes),
        cost_estimate=cost(2 * work, 200_000_000),
        name="outer_sums",
    )(*kinds, *rights)


def back_finish(piece, cot_ref, mid_ref, gain_ref, dmid_ref, dgain_ref):
    def finish(q, c, total):
        at = slice(c * piece, (c + 1) * piece)
        mid = mid_ref[q, at]
        inverse = rms_inverse(mid)
        unit = mid * inverse
        dgain_ref[...] += jnp.sum(total * unit, axis=0, keepdims=True)
        inner = total * gain_ref[...]
        mean = jnp.mean(inner * unit, axis=-1, keepdims=True)
        d_mid = cot_ref[q, at].astype(f32) + inverse * (inner - unit * mean)
        dmid_ref[q, at] = d_mid
        return d_mid.astype(bf16)

    return finish


def plain_back_kernel(n, seqs, rows, piece, part_ref, cot_ref, mid_ref, gain_ref, out_ref, dmid_ref, dgain_ref,
                      land_ref, *sems):
    dgain_ref[...] = jnp.zeros_like(dgain_ref)
    line_barrier(n, lax.axis_index("tp"))
    line_all_sum(n, seqs, rows, piece, back_finish(piece, cot_ref, mid_ref, gain_ref, dmid_ref, dgain_ref), part_ref,
                 out_ref, land_ref, sems)


class StreamedOuter:
    def __init__(self, jobs, each, left_slots, right_slots, left_sems, right_sems):
        self.jobs, self.each = jobs, each
        self.left, self.right, self.left_sems, self.right_sems = left_slots, right_slots, left_sems, right_sems

    def right_copy(self, i):
        _, right, half, _ = self.jobs[i]
        wide = self.right.shape[-1]
        return pltpu.make_async_copy(
            right.at[:, pl.ds(half * wide, wide)], self.right.at[i % 2], self.right_sems.at[i % 2])

    def left_copies(self, i, turn, place):
        at = pl.ds(pl.multiple_of(place * self.each, self.each), self.each)
        copies, first = [], 0
        for k, source in enumerate(self.jobs[i][0]):
            rows = pl.ds(first, source.shape[0])
            copies.append(pltpu.make_async_copy(
                source.at[:, at], self.left.at[turn % 2, rows], self.left_sems.at[turn % 2, k]))
            first += source.shape[0]
        return copies

    def product(self, i, turn, places, take):
        if turn == 0:
            if i == 0:
                self.right_copy(0).start()
                for copy in self.left_copies(0, 0, places[0]):
                    copy.start()
            self.right_copy(i).wait()
            if i + 1 < len(self.jobs):
                self.right_copy(i + 1).start()
        if turn + 1 < len(places):
            for copy in self.left_copies(i, turn + 1, places[turn + 1]):
                copy.start()
        for copy in self.left_copies(i, turn, places[turn]):
            copy.wait()
        value = mm(self.left[turn % 2], self.right[i % 2], TN)
        if turn + 1 == len(places) and i + 1 < len(self.jobs):
            for copy in self.left_copies(i + 1, 0, places[0]):
                copy.start()
        take(value)


def norm_back_kernel(n, seqs, rows, piece, bits, n_uly, parts, part_ref, cot_ref, mid_ref, gain_ref, a2_ref, *refs):
    cot_refs, refs = refs[:parts], refs[parts:]
    norm_back_body(n, seqs, rows, piece, bits, n_uly, part_ref, cot_ref, mid_ref, gain_ref, a2_ref, cot_refs, *refs)


def norm_back_body(n, seqs, rows, piece, bits, n_uly, part_ref, cot_ref, mid_ref, gain_ref, a2_ref, cot_refs,
                   dgate_ref, dup_ref, hidden_ref, out_ref, dmid_ref, dgain_ref, ggate_ref, gup_ref, gdown_ref,
                     land_ref, rs_send, rs_recv, ag_send, ag_recv, left_slots, right_slots, left_sems, right_sems,
                     *plane_scratch):
    dgain_ref[...] = jnp.zeros_like(dgain_ref)

    finish = back_finish(piece, cot_ref, mid_ref, gain_ref, dmid_ref, dgain_ref)
    wide = right_slots.shape[-1]
    halves = ggate_ref.shape[1] // wide
    jobs = [
        (left, right, half, out)
        for left, right, out in (
            ((a2_ref,), dgate_ref, ggate_ref), ((a2_ref,), dup_ref, gup_ref), (cot_refs, hidden_ref, gdown_ref))
        for half in range(halves)
    ]
    streamed = StreamedOuter(jobs, ggate_ref.shape[0], left_slots, right_slots, left_sems, right_sems)
    sums = []
    for i, (_, _, half, out) in enumerate(jobs):
        def store(at, total, half=half, out=out):
            to = pl.ds(half * wide + at.start, at.size)
            if out is gdown_ref:
                out[to] = total.T
            else:
                out[:, to] = total

        buf = plane_scratch[i % 3]
        land, send, recv = plane_scratch[3 + 3 * i:6 + 3 * i]
        sums.append(PlaneSum(bits, n_uly, None, store, buf, land, send, recv))
    last = bits - 2

    order = list(range(1, 1 << bits, 2)) + list(range(0, 1 << bits, 2))
    quiet = back_quiet
    beside = []

    def product(i, turn):
        def take(value):
            sums[i].buf[order[turn]] = value.astype(bf16)
            if order[turn] % 2:
                sums[i].first_copy(order[turn]).start()

        streamed.product(i, turn, [sums[i].me ^ e for e in order], take)

    for i in range(len(jobs) + last + 1):
        if i < len(jobs):
            beside += [functools.partial(product, i, turn) for turn in range(len(order))]
        for level in range(last):
            j = i - 1 - level
            if 0 <= j < len(jobs):
                beside += [functools.partial(sums[j].pull, level), functools.partial(sums[j].push, level + 1)]
        if i < len(jobs):
            beside += [sums[i].pair, functools.partial(sums[i].push, 0)]
        if 0 <= i - 1 - last < len(jobs):
            beside += [functools.partial(sums[i - 1 - last].pull, last), sums[i - 1 - last].finish]

    line_and_plane_barrier(n, lax.axis_index("tp"), bits, n_uly)
    line_all_sum(n, seqs, rows, piece, finish, part_ref, out_ref, land_ref, (rs_send, rs_recv, ag_send, ag_recv),
                 beside, quiet)


def norm_back(part, cotangent, middle, gain, a2, cots, d_gate, d_up, hidden, n, sizes, collective_id):
    n_ctx, n_uly = sizes
    places = n_ctx * n_uly
    bits = places.bit_length() - 1
    seqs, rows, width = cotangent.shape
    tokens, units = d_gate.shape
    each = width // places
    if not fits_plane(sizes, width) or units % 512:
        out, d_mid, dgain = line_call(
            plain_back_kernel, n, cotangent.shape, part, (cotangent, middle, gain[None]),
            (jax.ShapeDtypeStruct((1, width), f32),), collective_id, "norm_back")
        grads = outer_sums((a2, jnp.concatenate(cots)), (0, 0, 1), (d_gate, d_up, hidden), sizes, 0)
        return (out, d_mid, dgain, *grads[:2], grads[2].T)
    piece = min(back_piece, rows)
    half = units // 2
    vm, anywhere = pl.BlockSpec(memory_space=pltpu.VMEM), pl.BlockSpec(memory_space=pl.ANY)
    shapes = [
        jax.ShapeDtypeStruct(part.shape, bf16), jax.ShapeDtypeStruct(cotangent.shape, f32),
        jax.ShapeDtypeStruct((1, width), f32), *[jax.ShapeDtypeStruct((each, units), f32)] * 2,
        jax.ShapeDtypeStruct((units, each), f32),
    ]
    plane_scratch = [PlaneSum.scratch(bits, each, half) for _ in range(6)]
    return pl.pallas_call(
        functools.partial(norm_back_kernel, n, seqs, rows, piece, bits, n_uly, len(cots)),
        in_specs=[vm] * 4 + [anywhere] * (4 + len(cots)),
        out_specs=[vm] * len(shapes),
        out_shape=shapes,
        scratch_shapes=[
            *line_scratch(n, seqs, rows, piece, width),
            pltpu.VMEM((2, tokens, each), bf16), pltpu.VMEM((2, tokens, half), bf16),
            pltpu.SemaphoreType.DMA((2, len(cots))), pltpu.SemaphoreType.DMA((2,)),
            plane_scratch[0][0], plane_scratch[0][0], plane_scratch[0][0],
            *[item for scratch in plane_scratch for item in scratch[1:]],
        ],
        compiler_params=pltpu.CompilerParams(
            collective_id=collective_id, has_side_effects=True, vmem_limit_bytes=vmem_bytes),
        cost_estimate=cost(6 * tokens * units * width, 250_000_000),
        name="norm_back",
    )(part, cotangent, middle, gain[None], a2, *cots, d_gate, d_up, hidden)


class StoredSum(PlaneSum):
    def __init__(self, bits, n_uly, source, store, buf_ref, land_ref, send, recv, load):
        super().__init__(bits, n_uly, None, store, buf_ref, land_ref, send, recv)
        self.source, self.load = source, load

    @staticmethod
    def scratch(bits, *shape):
        n = 1 << bits
        return [
            pltpu.VMEM((n // 2, *shape), bf16), pltpu.VMEM((n - 1, *shape), bf16),
            pltpu.SemaphoreType.DMA((3, n)), pltpu.SemaphoreType.DMA((3, n)), pltpu.SemaphoreType.DMA((n // 2,)),
        ]

    def slot(self, e):
        return e // 2

    def first_copy(self, e):
        return pltpu.make_async_remote_copy(
            src_ref=self.source(self.me ^ e), dst_ref=self.land.at[e - 1], send_sem=self.send.at[2, e],
            recv_sem=self.recv.at[2, e], device_id=plane_device(self.me ^ 1, self.n_uly), device_id_type=MESH)

    def load_copy(self, e):
        return pltpu.make_async_copy(self.source(self.me ^ e), self.buf.at[e // 2], self.load.at[e // 2])

    def compute(self):
        for e in range(1, 1 << self.bits, 2):
            self.first_copy(e).start()
            self.load_copy(e - 1).start()

    def pair(self):
        for e in range(0, 1 << self.bits, 2):
            self.load_copy(e).wait()
        super().pair()


def all_barrier(n, bits, n_uly):
    barrier = pltpu.get_barrier_semaphore()
    me, place = lax.axis_index("tp"), plane_place(n_uly)
    for d in range(1, n):
        pl.semaphore_signal(barrier, inc=1, device_id={"tp": lax.rem(me + d, n)}, device_id_type=MESH)
    for b in range(bits):
        pl.semaphore_signal(barrier, inc=1, device_id=plane_device(place ^ (1 << b), n_uly), device_id_type=MESH)
    pl.semaphore_wait(barrier, n - 1 + bits)


def layer_back_kernel(
    n, bits, n_uly, heads, kv_heads, dim, dkv_ref, first_ref, dbranch_ref, dq_ref, dlogit_ref, nk_ref, rk_ref, cos_ref,
    sin_ref, kgain_ref, wq_ref, wk_ref, wv_ref, wg_ref, gated_ref, x_ref, gain_ref, dmid_ref, dqgain_ref, dmlp_ref, gin_ref, gq_ref, gk_ref,
    gv_ref, gh_ref, gout_ref, gattn_ref, gmlp_ref, gqn_ref, gkn_ref, all_ref, cut_ref, part_ref, sum_ref, line_land, rs_send, rs_recv, left_slots, left_sems,
    vec_ref, vec_land, vec_send, vec_recv, *plane_scratch,
):
    seqs, _, cut_count, piece, _ = dq_ref.shape
    rows, width = cut_count * piece, x_ref.shape[-1]
    group = n * rows
    cuts = [(q, c) for q in range(seqs) for c in range(cut_count)]
    q_cols, kv_cols = heads * dim, kv_heads * dim
    n_main = q_cols + 2 * kv_cols
    each = gq_ref.shape[0]
    place, line_me = plane_place(n_uly), lax.axis_index("tp")

    vec_ref[0] = jnp.zeros_like(vec_ref[0])
    vec_ref[0, :, width:2 * width] = dmlp_ref[...]
    vec_ref[0, :, 2 * width:2 * width + dim] = dqgain_ref[...]

    def row_at(q, t, c):
        return q * group + t * rows + c * piece

    def key_values(s):
        q, c = cuts[s]

        def store(at, total):
            sum_ref[:, :, at] = total.astype(bf16)

        return StoredSum(
            bits, n_uly, lambda at: dkv_ref.at[q, pl.ds(pl.multiple_of(at * n, n), n), c], store,
            *plane_scratch[5 * s:5 * s + 5])

    sums = [key_values(s) for s in range(len(cuts))]

    def turn(s):
        q, c = cuts[s]
        for t in range(n):
            at = slice(t * piece, (t + 1) * piece)
            cut_ref[at, :q_cols] = dq_ref[q, t, c]
            for h in range(kv_heads):
                turned = sum_ref[t, :, h * dim:(h + 1) * dim].astype(f32)
                back = turned * cos_ref[t, c] - pltpu.roll(turned, dim // 2, 1) * sin_ref[t, c]
                unit = nk_ref[q, t, c, :, h * dim:(h + 1) * dim].astype(f32)
                vec_ref[0, :, 2 * width + dim:] += jnp.sum(back * unit, axis=0, keepdims=True)
                inner = back * kgain_ref[...]
                mean = jnp.mean(inner * unit, axis=1, keepdims=True)
                cut_ref[at, q_cols + h * dim:q_cols + (h + 1) * dim] = (
                    rk_ref[q, t, c, :, h:h + 1] * (inner - unit * mean)).astype(bf16)
            cut_ref[at, q_cols + kv_cols:n_main] = sum_ref[t, :, kv_cols:]
            cut_ref[at, n_main:] = dlogit_ref[q, t, c]
        partial = mm(cut_ref[:, :q_cols], wq_ref[...], NT)
        partial += mm(cut_ref[:, q_cols:q_cols + kv_cols], wk_ref[...], NT)
        partial += mm(cut_ref[:, q_cols + kv_cols:n_main], wv_ref[...], NT)
        partial += mm(cut_ref[:, n_main:n_main + heads], wg_ref[...])
        partial = partial.astype(bf16)
        for t in range(n):
            at = slice(t * piece, (t + 1) * piece)
            to = slice(row_at(q, t, c), row_at(q, t, c) + piece)
            part_ref[to] = partial[at]
            all_ref[to] = cut_ref[at]

    split = line_land.shape[2] // len(cuts)
    short = piece // split

    def part_at(owner, p):
        q, c = cuts[p // split]
        return part_ref.at[pl.ds(pl.multiple_of(row_at(q, owner, c) + p % split * short, short), short)]

    def own(p, total):
        q, c = cuts[p // split]
        at = slice(c * piece + p % split * short, c * piece + (p % split + 1) * short)
        x = x_ref[q, at].astype(f32)
        inverse = rms_inverse(x)
        unit = x * inverse
        inner = total * gain_ref[...]
        mean = jnp.mean(inner * unit, axis=-1, keepdims=True)
        gin_ref[q, at] = dmid_ref[q, at] + inverse * (inner - unit * mean)

    line = LineSum(n, len(cuts) * split, part_at, own, line_land, (rs_send, rs_recv))

    order = list(range(1, 1 << bits, 2)) + list(range(0, 1 << bits, 2))
    turns = [(dbranch_ref, e) for e in order] + [(first_ref, e) for e in order]

    def left_copy(i):
        source, e = turns[i]
        at = pl.ds(pl.multiple_of((place ^ e) * each, each), each)
        return pltpu.make_async_copy(source.at[:, at], left_slots.at[i % 2], left_sems.at[i % 2])

    def store_out(at, total):
        gout_ref[at] = total.T

    def store_first(at, total):
        if at.start + at.size > n_main:
            gh_ref[...] = total[:, n_main - at.start:].T[:heads]
        first = 0
        for out in (gq_ref, gk_ref, gv_ref):
            lo, hi = max(first, at.start), min(first + out.shape[1], at.start + at.size)
            if lo < hi:
                out[:, lo - first:hi - first] = total[:, lo - at.start:hi - at.start]
            first += out.shape[1]

    scratch = plane_scratch[5 * len(cuts):]
    out_sum = PlaneSum(bits, n_uly, None, store_out, *scratch[:4])
    first_sum = PlaneSum(bits, n_uly, None, store_first, *scratch[4:])

    def product(i):
        e = turns[i][1]
        if i + 1 < len(turns):
            left_copy(i + 1).start()
        left_copy(i).wait()
        job = out_sum if i < len(order) else first_sum
        value = mm(left_slots[i % 2], gated_ref[...] if i < len(order) else all_ref[...], TN)
        job.buf[e] = value.astype(bf16)
        if e % 2:
            job.first_copy(e).start()
        if job is first_sum:
            at = pl.ds(pl.multiple_of((place ^ e) * each, each), each)
            lanes, first = jnp.zeros((each, 128), f32), 0
            for w_ref in (wq_ref, wk_ref, wv_ref):
                for k in range(0, w_ref.shape[1], 128):
                    lanes += value[:, first + k:first + k + 128] * w_ref[at, k:k + 128].astype(f32)
                first += w_ref.shape[1]
            total = jnp.sum(lanes.T, axis=0, keepdims=True)
            last = value[:, n_main:].T[:heads] * wg_ref[:, at].astype(f32)
            total += jnp.sum(last, axis=0, keepdims=True)
            vec_ref[0, :, at] = total / gain_ref[:, at]

    line_bits = n.bit_length() - 1
    steps = bits + line_bits

    def vec_copy(k):
        partner = plane_device(place ^ (1 << k), n_uly) if k < bits else {"tp": line_me ^ (1 << (k - bits))}
        return pltpu.make_async_remote_copy(
            src_ref=vec_ref.at[k], dst_ref=vec_land.at[k], send_sem=vec_send.at[k], recv_sem=vec_recv.at[k],
            device_id=partner, device_id_type=MESH)

    def vec_step(k):
        if k > 0:
            vec_copy(k - 1).wait_recv()
            vec_ref[k] = vec_ref[k - 1] + vec_land[k - 1]
        if k < steps:
            vec_copy(k).start()

    def levels(job):
        items = []
        for level in range(bits - 1):
            items.append(functools.partial(job.pull, level))
            if level + 1 < bits - 1:
                items.append(functools.partial(job.push, level + 1))
        return items

    early = [functools.partial(product, i) for i in range(len(order))]
    early += [out_sum.pair, functools.partial(out_sum.push, 0)]
    late = [functools.partial(product, i) for i in range(len(order), len(turns))]
    late.append(functools.partial(vec_step, 0))
    late += levels(out_sum)[:2]
    late += [first_sum.pair, functools.partial(first_sum.push, 0)]
    rest = levels(out_sum)[2:] + levels(first_sum)
    for k in range(1, steps + 1):
        late.append(functools.partial(vec_step, k))
        if k % 2 == 0 and rest:
            late.append(rest.pop(0))
    late += rest

    all_barrier(n, bits, n_uly)
    for job in sums:
        job.compute()
    left_copy(0).start()
    ready = 0
    line_steps = split * (len(cuts) + bits - 1) + n - 1
    for step in range(-(-line_steps // split)):
        if step < len(cuts):
            sums[step].pair()
            sums[step].push(0)
        for level in range(bits - 1):
            j = step - 1 - level
            if 0 <= j < len(cuts):
                sums[j].pull(level)
                if level + 1 < bits - 1:
                    sums[j].push(level + 1)
                else:
                    turn(j)
                    ready += 1
        for turn_of in range(split * step, split * (step + 1)):
            for p in range(line.pieces):
                stage = turn_of - p - split * (bits - 1)
                if 0 <= stage < n:
                    line.stages[stage](p)
                    queue = early or (late if ready == len(cuts) else [])
                    for item in queue[:tail_items]:
                        item()
                    del queue[:tail_items]
    for item in early + late:
        item()
    line.drain_reduce()
    first = 0
    for out in (gattn_ref, gmlp_ref, gqn_ref, gkn_ref):
        out[...] = vec_ref[steps, :, first:first + out.shape[1]]
        first += out.shape[1]
    for k in range(steps):
        vec_copy(k).wait_send()
    for job in (*sums, out_sum, first_sum):
        job.finish()


def layer_back(d_kv, first, d_branch, d_q, d_logit, nk, rk, tables, key_norm, weights, gated, x, attn_norm, d_mid, d_qgain,
               d_mlp, n, sizes, heads, kv_heads, collective_id):
    n_ctx, n_uly = sizes
    places = n_ctx * n_uly
    bits = places.bit_length() - 1
    seqs, rows, width = x.shape
    group, dim = n * rows, key_norm.shape[0]
    piece = min(64, rows)
    cut_count = rows // piece
    each = width // places
    tokens = seqs * group
    wide = (heads + 2 * kv_heads) * dim + d_logit.shape[-1]
    small = 2 * width + 2 * dim
    kv_wide = d_kv.shape[-1]
    pieces = seqs * cut_count
    steps = bits + n.bit_length() - 1

    def tiles(values):
        return values.reshape(seqs, n, cut_count, piece, values.shape[-1])

    vm, anywhere = pl.BlockSpec(memory_space=pltpu.VMEM), pl.BlockSpec(memory_space=pl.ANY)
    plane_scratch = []
    for _ in range(pieces):
        plane_scratch += StoredSum.scratch(bits, n, piece, kv_wide)
    plane_scratch += PlaneSum.scratch(bits, each, heads * dim) + PlaneSum.scratch(bits, each, wide)
    shapes = [
        jax.ShapeDtypeStruct(shape, f32) for shape in (
            x.shape, (each, heads * dim), (each, kv_heads * dim), (each, kv_heads * dim), (heads, each),
            (heads * dim, each), (1, width), (1, width), (1, dim), (1, dim))
    ]
    line = line_scratch(n, seqs, rows, min(tail_piece, piece), width)
    return pl.pallas_call(
        functools.partial(layer_back_kernel, n, bits, n_uly, heads, kv_heads, dim),
        in_specs=[anywhere] * 3 + [vm] * 17,
        out_specs=[vm] * len(shapes),
        out_shape=shapes,
        scratch_shapes=[
            pltpu.VMEM((tokens, wide), bf16), pltpu.VMEM((n * piece, wide), bf16), pltpu.VMEM((tokens, width), bf16),
            pltpu.VMEM((n, piece, kv_wide), bf16), *line[:3],
            pltpu.VMEM((2, tokens, each), bf16), pltpu.SemaphoreType.DMA((2,)),
            pltpu.VMEM((steps + 1, 1, small), f32), pltpu.VMEM((steps, 1, small), f32),
            pltpu.SemaphoreType.DMA((steps,)), pltpu.SemaphoreType.DMA((steps,)),
            *plane_scratch,
        ],
        compiler_params=pltpu.CompilerParams(
            collective_id=collective_id, has_side_effects=True, vmem_limit_bytes=vmem_bytes),
        cost_estimate=cost(4 * tokens * width * wide, 250_000_000),
        name="layer_back",
    )(d_kv.reshape(seqs, places * n, cut_count, piece, kv_wide), first, d_branch, tiles(d_q), tiles(d_logit), tiles(nk),
      tiles(rk), *[t.reshape(n, cut_count, piece, dim) for t in tables], key_norm[None], *weights, gated, x,
      attn_norm[None], d_mid, d_qgain, d_mlp)


class LineSpread(LineSum):
    def __init__(self, n, pieces, own, out_at, sems):
        super().__init__(n, pieces, None, own, None, (None, None, *sems), out_at)
        self.stages = [self.own_step] + [functools.partial(self.spread_step, k) for k in range(2, n + 1)]

    def own_step(self, s):
        self.out_at(self.me, s)[...] = self.own(s)
        self.spread_step(1, s)


class PlaneSpread:
    def __init__(self, bits, n_uly, block, send, recv):
        self.bits, self.n_uly, self.block, self.send, self.recv = bits, n_uly, block, send, recv
        self.me = plane_place(n_uly)
        self.orders = [w + [0] for w in ways(bits)]

    def copy(self, d, level, e):
        bit = 1 << self.orders[d][level]
        block = self.block(self.me ^ e, d)
        return pltpu.make_async_remote_copy(
            src_ref=block, dst_ref=block, send_sem=self.send.at[d, e | bit], recv_sem=self.recv.at[d, e | bit],
            device_id=plane_device(self.me ^ bit, self.n_uly), device_id_type=MESH)

    def pass_on(self, d, first, e):
        for level in range(first, self.bits):
            self.copy(d, level, e).start()

    def begin(self):
        for d in range(2):
            self.pass_on(d, 0, 0)

    def take(self, level):
        for d in range(2):
            for e in span(self.orders[d][:level]):
                self.copy(d, level, e).wait_recv()
                self.pass_on(d, level + 1, e | (1 << self.orders[d][level]))

    def finish(self):
        for d in range(2):
            for level in range(self.bits):
                for e in span(self.orders[d][:level]):
                    self.copy(d, level, e).wait_send()


def layer_front_kernel(
    n, bits, n_uly, heads, kv_heads, dim, scale, x_ref, gain_ref, wq_ref, wk_ref, wv_ref, wg_ref, cos_ref, sin_ref,
    qg_ref, kg_ref, a1_ref, q_ref, kv_ref, nq_ref, nk_ref, rq_ref, rk_ref, logit_ref, ag_send, ag_recv, kv_send,
    kv_recv,
):
    seqs, _, cut_count, piece, width = a1_ref.shape
    cuts = [(q, c) for q in range(seqs) for c in range(cut_count)]
    place = plane_place(n_uly)
    tokens = n * piece
    half = kv_heads * dim

    def own(s):
        q, c = cuts[s]
        x = x_ref[q, c * piece:(c + 1) * piece].astype(f32)
        return (x * rms_inverse(x) * gain_ref[...]).astype(bf16)

    line = LineSpread(
        n, len(cuts), own, lambda owner, s: a1_ref.at[cuts[s][0], owner, cuts[s][1]], (ag_send, ag_recv))

    def keys(s):
        q, c = cuts[s]
        return PlaneSpread(
            bits, n_uly,
            lambda at, d: kv_ref.at[q, pl.ds(pl.multiple_of(at * n, n), n), c, :, pl.ds(d * half, half)],
            kv_send.at[s], kv_recv.at[s])

    spreads = [keys(s) for s in range(len(cuts))]

    def turn(s):
        q, c = cuts[s]
        a1 = a1_ref[q, :, c].reshape(tokens, width)
        cosine, sine = cos_ref[:, c].reshape(tokens, dim), sin_ref[:, c].reshape(tokens, dim)

        def tiles(values):
            return values.reshape(n, piece, values.shape[-1])

        def rope(unit, gain):
            scaled = unit * gain
            return scaled * cosine + pltpu.roll(scaled, dim // 2, 1) * sine

        mine = pl.ds(pl.multiple_of(place * n, n), n)
        raw = mm(a1, wk_ref[...])
        for h in range(kv_heads):
            at = slice(h * dim, (h + 1) * dim)
            values = raw[:, at]
            inverse = rms_inverse(values)
            unit = values * inverse
            kv_ref[q, mine, c, :, at] = tiles(rope(unit, kg_ref[...]).astype(bf16))
            nk_ref[q, :, c, :, at] = tiles(unit.astype(bf16))
            rk_ref[q, :, c, :, h:h + 1] = tiles(inverse)
        kv_ref[q, mine, c, :, half:] = tiles(mm(a1, wv_ref[...]).astype(bf16))
        spreads[s].begin()
        raw = mm(a1, wq_ref[...])
        for h in range(heads):
            at = slice(h * dim, (h + 1) * dim)
            values = raw[:, at]
            inverse = rms_inverse(values)
            unit = values * inverse
            q_ref[q, :, c, :, at] = tiles((rope(unit, qg_ref[...]) * (scale * log2e)).astype(bf16))
            nq_ref[q, :, c, :, at] = tiles(unit.astype(bf16))
            rq_ref[q, :, c, :, h:h + 1] = tiles(inverse)
        logit_ref[q, :, c] = tiles(mm(a1, wg_ref[...], NT).astype(bf16).astype(f32))

    line_and_plane_barrier(n, lax.axis_index("tp"), bits, n_uly)
    for step in range(len(cuts) + n - 1 + bits):
        for s in range(len(cuts)):
            stage = step - s
            if 0 <= stage < n:
                line.stages[stage](s)
                if stage == n - 1:
                    turn(s)
        for s in range(len(cuts)):
            level = step - s - n
            if 0 <= level < bits:
                spreads[s].take(level)
    line.drain_spread()
    for spread in spreads:
        spread.finish()


def layer_front(x, attn_norm, w_query, w_key, w_value, w_headgate, tables, query_norm, key_norm, n, sizes, scale,
                collective_id):
    n_ctx, n_uly = sizes
    places = n_ctx * n_uly
    bits = places.bit_length() - 1
    seqs, rows, width = x.shape
    dim = query_norm.shape[0]
    heads, kv_heads = w_query.shape[1] // dim, w_key.shape[1] // dim
    piece = min(32, rows)
    cut_count = rows // piece
    pieces = seqs * cut_count
    vm = pl.BlockSpec(memory_space=pltpu.VMEM)

    def tiled(devices, cols, kind):
        return jax.ShapeDtypeStruct((seqs, devices * n, cut_count, piece, cols), kind)

    shapes = [
        tiled(1, width, bf16), tiled(1, heads * dim, bf16), tiled(places, 2 * kv_heads * dim, bf16),
        tiled(1, heads * dim, bf16), tiled(1, kv_heads * dim, bf16), tiled(1, heads, f32), tiled(1, kv_heads, f32),
        tiled(1, heads, f32),
    ]
    line_sems = [pltpu.SemaphoreType.DMA((2, n - 1, pieces))] * 2
    plane_sems = [pltpu.SemaphoreType.DMA((pieces, 2, places))] * 2
    made = pl.pallas_call(
        functools.partial(layer_front_kernel, n, bits, n_uly, heads, kv_heads, dim, scale),
        in_specs=[vm] * 10,
        out_specs=[vm] * len(shapes),
        out_shape=shapes,
        scratch_shapes=[*line_sems, *plane_sems],
        compiler_params=params(collective_id=collective_id, has_side_effects=True),
        cost_estimate=cost(2 * seqs * n * rows * width * 1024, 200_000_000),
        name="layer_front",
    )(x, attn_norm[None], w_query, w_key, w_value, w_headgate.T,
      *[t.reshape(n, cut_count, piece, dim) for t in tables], query_norm[None], key_norm[None])
    return [m.reshape(seqs, -1, m.shape[-1]) for m in made]


def finish_kernel(count, *refs):
    sources, mid_ref, adds, targets, out_ref = refs[:count], refs[count], refs[count + 1:-count - 1], refs[-count - 1:-1], refs[-1]
    for source, target in zip(sources, targets):
        target[...] = source[...]
    first = 0
    for add_ref in adds:
        last = first + add_ref.shape[0]
        out_ref[first:last] = (mid_ref[first:last] + add_ref[...].astype(f32)).astype(bf16)
        first = last


def finish(sources, middle, adds):
    vm = pl.BlockSpec(memory_space=pltpu.VMEM)
    count = len(sources)
    made = pl.pallas_call(
        functools.partial(finish_kernel, count),
        in_specs=[vm] * (count + 1 + len(adds)),
        out_specs=[vm] * (count + 1),
        out_shape=[jax.ShapeDtypeStruct(s.shape, s.dtype) for s in sources]
        + [jax.ShapeDtypeStruct(middle.shape, bf16)],
        compiler_params=params(),
        cost_estimate=cost(middle.size, 20 * middle.size),
        name="finish",
    )(*sources, middle, *adds)
    return made[:-1], made[-1]


def flatten(values):
    return values.reshape(-1, values.shape[-1])


def spread(values):
    return lax.all_gather(values.astype(bf16), "tp", axis=1, tiled=True)


def collect(values):
    return lax.psum_scatter(values.astype(bf16), "tp", scatter_dimension=1, tiled=True)


def per_device(sizes, inputs, doc_ids, attn_norm, w_query, w_key, w_value, w_headgate, query_norm, key_norm, w_output,
               mlp_norm, w_gate, w_up, w_down, cotangent):
    n_tensor = lax.axis_size("tp")
    n_uly = sizes[1]
    seqs, rows, width = inputs.shape
    group = rows * n_tensor
    dim = query_norm.shape[0]
    heads = w_query.shape[1] // dim
    kv_heads = w_key.shape[1] // dim
    scale = dim ** (-0.5)
    plane = ("ctx", "uly")
    place = lax.axis_index("ctx") * n_uly + lax.axis_index("uly")
    block_start = place * group
    positions = block_start + jnp.arange(group, dtype=jnp.int32)
    tables = lax.optimization_barrier(rope_tables(positions, dim))
    block = min(512, group)

    def wide(values):
        return values.reshape(seqs, group, -1)

    query_doc = lax.dynamic_slice_in_dim(doc_ids, block_start, group, 1)
    start = positions[None, :]
    for d in range(4):
        first_of = jnp.sum(((doc_ids >= 0) & (doc_ids < d)).astype(jnp.int32), axis=1)
        start = jnp.where(query_doc == d, first_of[:, None], start)
    lowest, highest = jnp.min(start, axis=1), jnp.max(start, axis=1)
    hi = jnp.full_like(lowest, (block_start + group + block - 1) // block)
    lo = lowest // block
    full_lo = jnp.clip((highest + block - 1) // block, lo, hi)
    full_hi = jnp.clip(jnp.full_like(lowest, (block_start + 1) // block), full_lo, hi)
    bounds = jnp.stack([lo, full_lo, full_hi, hi], axis=1)

    pad = 128 - heads
    w_first = jnp.concatenate([w_query, w_key, w_value, jnp.pad(w_headgate, ((0, 0), (0, pad)))], axis=1)
    q_cols, kv_cols = heads * dim, kv_heads * dim
    n_main = q_cols + 2 * kv_cols

    if fits_plane(sizes, width):
        first, q, kv, nq, nk, rq, rk, logits = layer_front(
            inputs, attn_norm, w_query, w_key, w_value, w_headgate, tables, query_norm, key_norm, n_tensor, sizes, scale,
            0)
    else:
        xs = inputs.astype(f32)
        inv_one = rms_inverse(xs)
        first = spread(xs * inv_one * attn_norm)
        q, kv, nq, nk, rq, rk, logits = (
            wide(m) for m in project(flatten(first), w_first, tables, query_norm, key_norm, heads, kv_heads, scale))
        kv = plane_gather(kv, sizes, 0)
    near = (seqs + 1) // 2
    early_cot, kv = lax.optimization_barrier((cotangent[:near], kv))
    cots = [spread(early_cot)]
    att, gated, lse = attend(q, kv, bounds, start[:, :, None], positions[:, None], logits, heads, kv_heads, dim, block)

    local = inputs.shape
    part, cots = lax.optimization_barrier((wide(mm(flatten(gated), w_output).astype(bf16)), cots))
    second, middle = line_call(
        norm_forward_kernel, n_tensor, local, part,
        (inputs, mlp_norm[None]), (), 1, "norm_forward")

    if near < seqs:
        late_cot, second = lax.optimization_barrier((cotangent[near:], second))
        cots.append(spread(late_cot))
    a2 = flatten(second)
    gate, up = mm(a2, w_gate), mm(a2, w_up)
    sig = jax.nn.sigmoid(gate)
    silu = gate * sig
    hidden = (silu * up).astype(bf16)
    made, cots = lax.optimization_barrier((wide(mm(hidden, w_down).astype(bf16)), cots))
    cots = [flatten(c) for c in cots]
    d_gate, d_up = hidden_back(cots, w_down, gate, up)
    d_second = second_back(d_gate, d_up, w_gate, w_up)
    d_branch, d_mid, grad_mlp_norm, grad_gate, grad_up, grad_down = norm_back(
        wide(d_second), cotangent, middle, mlp_norm, a2, cots, d_gate, d_up, hidden, n_tensor, sizes, 2)

    made, d_branch = lax.optimization_barrier((made, d_branch))
    outs = [collect(made)]
    d_gated = wide(mm(flatten(d_branch), w_output, NT).astype(bf16))
    d_q, d_logit, d_kv, d_qgain, grad_gate, grad_up, grad_down = attend_back(
        q, kv, d_gated, att, logits, logits.transpose(0, 2, 1), lse, bounds, start[:, None, :], positions[None, :], nq,
        rq, tables, query_norm, (grad_gate, grad_up, grad_down), heads, kv_heads, dim, block, scale)
    d_logit = jnp.pad(d_logit.astype(bf16).transpose(0, 2, 1), ((0, 0), (0, 0), (0, pad)))
    if fits_plane(sizes, width):
        grad_inputs, *grads = layer_back(
            d_kv, flatten(first), flatten(d_branch), d_q, d_logit, nk, rk, tables, key_norm,
            (w_query, w_key, w_value, w_headgate.T), flatten(gated), inputs, attn_norm, d_mid, d_qgain, grad_mlp_norm, n_tensor, sizes, heads, kv_heads, 3)
        (grad_inputs, grad_query, grad_key, grad_value, grad_headgate, grad_output), outputs = finish(
            (grad_inputs, *grads[:5]), middle, outs)
        grad_headgate = grad_headgate.T
        grad_attn_norm, grad_mlp_norm, grad_query_norm, grad_key_norm = (g[0] for g in grads[5:])
    else:
        outputs = (middle + jnp.concatenate(outs, axis=0).astype(f32)).astype(bf16)
        d_kv = blocks_sum(d_kv, sizes, 3)
        d_kv, d_kgain = key_back(d_kv, nk, rk, tables, key_norm, kv_heads, dim)
        d_all = flatten(jnp.concatenate([d_q, d_kv, d_logit], axis=-1))
        d_first = collect(wide(mm(d_all, w_first, NT))).astype(f32)

        grad_first, grad_output = outer_sums(
            (flatten(first), flatten(d_branch)), (0, 1), (d_all, flatten(gated)), sizes, 4)

        share = grad_first.shape[0]
        own_rows = lax.dynamic_slice_in_dim(w_first, place * share, share, 0).astype(f32)
        own_norm = jnp.sum(grad_first * own_rows, axis=1) / lax.dynamic_slice_in_dim(attn_norm, place * share, share, 0)
        grad_attn_norm = lax.dynamic_update_slice_in_dim(jnp.zeros((width,), f32), own_norm, place * share, 0)
        grad_attn_norm, grad_query_norm, grad_key_norm, grad_mlp_norm = lax.psum(
            (grad_attn_norm, d_qgain[0], d_kgain[0], grad_mlp_norm[0]), ("ctx", "uly", "tp"))

        unit = xs * inv_one
        inner = d_first * attn_norm
        grad_inputs = d_mid + inv_one * (inner - unit * jnp.mean(inner * unit, axis=-1, keepdims=True))
        grad_query, grad_key = grad_first[:, :q_cols], grad_first[:, q_cols:q_cols + kv_cols]
        grad_value, grad_headgate = grad_first[:, q_cols + kv_cols:n_main], grad_first[:, n_main:n_main + heads]
        grad_output = grad_output.T
    return (
        outputs,
        grad_inputs,
        grad_attn_norm,
        grad_query,
        grad_key,
        grad_value,
        grad_headgate,
        grad_query_norm,
        grad_key_norm,
        grad_output,
        grad_mlp_norm,
        grad_gate,
        grad_up,
        grad_down,
    )


def solution(mesh):
    tokens = P(None, ("ctx", "uly", "tp"), None)
    column, line, whole = P(None, "tp"), P("tp", None), P()
    rows_split, cols_split = P(("ctx", "uly"), "tp"), P("tp", ("ctx", "uly"))
    return jax.shard_map(
        functools.partial(per_device, (mesh.shape["ctx"], mesh.shape["uly"])),
        mesh=mesh,
        in_specs=(
            tokens, whole, whole, column, column, column, column, whole, whole, line, whole, column, column, line,
            tokens,
        ),
        out_specs=(
            tokens, tokens, whole, rows_split, rows_split, rows_split, rows_split, whole, whole, cols_split, whole,
            rows_split, rows_split, cols_split,
        ),
        check_vma=False,
    )
```

```python
import functools
import math

import jax
import jax.numpy as jnp
from jax import lax
from jax.experimental import pallas as pl
from jax.experimental.pallas import tpu as pltpu
from jax.sharding import PartitionSpec as P

epsilon = 1e-06
rope_base = 1000000.0
log2e = 1.0 / math.log(2.0)
bf16 = jnp.bfloat16
f32 = jnp.float32
back_quiet = (0, 2)
back_piece = 32
tail_piece = 64
tail_items = 3
vmem_bytes = 61 * 1024 * 1024

MESH = pl.DeviceIdType.MESH
NT = (((1,), (1,)), ((), ()))
NN = (((1,), (0,)), ((), ()))
TN = (((0,), (0,)), ((), ()))


def mm(left, right, dims=NN):
    return lax.dot_general(left, right, dims, preferred_element_type=f32)


def params(**more):
    return pltpu.CompilerParams(vmem_limit_bytes=vmem_bytes, **more)


def cost(flops, moved, trans=0):
    return pl.CostEstimate(flops=int(flops), bytes_accessed=int(moved), transcendentals=int(trans))


def full(shape):
    return pl.BlockSpec(shape, lambda *_: (0,) * len(shape))


def rms_inverse(values):
    return lax.rsqrt(jnp.mean(values * values, axis=-1, keepdims=True) + epsilon)


def rope_tables(positions, head_dim):
    half = head_dim // 2
    frequency = rope_base ** (-(jnp.arange(half, dtype=f32) * 2.0 / head_dim))
    angles = positions.astype(f32)[:, None] * frequency[None, :]
    cosine, sine = jnp.cos(angles), jnp.sin(angles)
    return jnp.concatenate([cosine, cosine], 1), jnp.concatenate([-sine, sine], 1)


def project_kernel(heads, kv_heads, dim, scale, x_ref, w_ref, cos_ref, sin_ref, qg_ref, kg_ref,
                   q_ref, kv_ref, nq_ref, nk_ref, rq_ref, rk_ref, logit_ref):
    cosine, sine = cos_ref[...], sin_ref[...]
    raw = mm(x_ref[...], w_ref[...])

    def rope(unit, gain):
        scaled = unit * gain
        return scaled * cosine + pltpu.roll(scaled, dim // 2, 1) * sine

    for h in range(heads + kv_heads):
        values = raw[:, h * dim:(h + 1) * dim]
        inverse = rms_inverse(values)
        unit = values * inverse
        if h < heads:
            at = slice(h * dim, (h + 1) * dim)
            q_ref[:, at] = (rope(unit, qg_ref[...]) * (scale * log2e)).astype(bf16)
            nq_ref[:, at] = unit.astype(bf16)
            rq_ref[:, h:h + 1] = inverse
        else:
            g = h - heads
            at = slice(g * dim, (g + 1) * dim)
            kv_ref[:, at] = rope(unit, kg_ref[...]).astype(bf16)
            nk_ref[:, at] = unit.astype(bf16)
            rk_ref[:, g:g + 1] = inverse
    first = (heads + kv_heads) * dim
    kv_ref[:, kv_heads * dim:] = raw[:, first:first + kv_heads * dim].astype(bf16)
    first += kv_heads * dim
    logit_ref[...] = raw[:, first:first + heads].astype(bf16).astype(f32)


def project(x, w, tables, query_norm, key_norm, heads, kv_heads, scale, block=256):
    rows, width = x.shape
    dim = query_norm.shape[0]
    cosine, sine = tables
    block = min(block, cosine.shape[0])
    around = cosine.shape[0] // block
    kernel = functools.partial(project_kernel, heads, kv_heads, dim, scale)

    def by_row(cols):
        return pl.BlockSpec((block, cols), lambda i: (i, 0))

    table = pl.BlockSpec((block, dim), lambda i: (i % around, 0))
    shapes = [
        (heads * dim, bf16), (2 * kv_heads * dim, bf16), (heads * dim, bf16), (kv_heads * dim, bf16),
        (heads, f32), (kv_heads, f32), (heads, f32),
    ]
    return pl.pallas_call(
        kernel,
        grid=(rows // block,),
        in_specs=[by_row(width), full(w.shape), table, table, full((1, dim)), full((1, dim))],
        out_specs=[by_row(c) for c, _ in shapes],
        out_shape=[jax.ShapeDtypeStruct((rows, c), t) for c, t in shapes],
        compiler_params=params(),
        cost_estimate=cost(2 * rows * width * w.shape[1], 2 * (rows * width + w.size) + rows * 4096),
        name="project",
    )(x, w, cosine, sine, query_norm[None], key_norm[None])


def bounds_loop(bounds_ref, row, body):
    lo, full_lo, full_hi, hi = (bounds_ref[row, i] for i in range(4))
    lax.fori_loop(lo, full_lo, lambda j, c: body(j, True), None)
    lax.fori_loop(full_lo, full_hi, lambda j, c: body(j, False), None)
    lax.fori_loop(full_hi, hi, lambda j, c: body(j, True), None)


def attend_kernel(heads, kv_heads, dim, block, bounds_ref, q_ref, kv_ref, start_ref, pos_ref, logit_ref,
                  att_ref, gated_ref, lse_ref, q2_ref, acc_ref, sum_ref):
    row = pl.program_id(0)
    group = q_ref.shape[1]
    repeat = heads // kv_heads
    for h in range(kv_heads):
        for g in range(repeat):
            at = slice((h * repeat + g) * dim, (h * repeat + g + 1) * dim)
            q2_ref[g * group:(g + 1) * group, :] = q_ref[0, :, at]
        acc_ref[...] = jnp.zeros_like(acc_ref)
        sum_ref[...] = jnp.zeros_like(sum_ref)

        def body(j, masked):
            at = pl.ds(pl.multiple_of(j * block, block), block)
            keys = kv_ref[0, at, h * dim:(h + 1) * dim]
            values = kv_ref[0, at, (kv_heads + h) * dim:(kv_heads + h + 1) * dim]
            if masked:
                spot = j * block + lax.broadcasted_iota(jnp.int32, (group, block), 1)
                allowed = (spot >= start_ref[0]) & (spot <= pos_ref[...])
            for g in range(repeat):
                part = slice(g * group, (g + 1) * group)
                weight = jnp.exp2(mm(q2_ref[part, :], keys, NT))
                if masked:
                    weight = jnp.where(allowed, weight, 0.0)
                total = weight[:, :dim]
                for i in range(1, block // dim):
                    total = total + weight[:, i * dim:(i + 1) * dim]
                sum_ref[part, :] += total
                acc_ref[part, :] += mm(weight.astype(bf16), values)

        bounds_loop(bounds_ref, row, body)
        for g in range(repeat):
            part = slice(g * group, (g + 1) * group)
            n = h * repeat + g
            at = slice(n * dim, (n + 1) * dim)
            total = jnp.sum(sum_ref[part, :], axis=1, keepdims=True)
            attended = acc_ref[part, :] / total
            att_ref[0, :, at] = attended.astype(bf16)
            gated_ref[0, :, at] = (attended * jax.nn.sigmoid(logit_ref[0, :, n:n + 1])).astype(bf16)
            lse_ref[0, n:n + 1, :] = jnp.log2(jnp.sum(sum_ref[part, :].T, axis=0, keepdims=True))


def attend(q, kv, bounds, start_col, pos_col, logits, heads, kv_heads, dim, block):
    rows, group, width = q.shape
    total = kv.shape[1]
    repeat = heads // kv_heads

    def by_row(*shape):
        return pl.BlockSpec((1, *shape), lambda r, *_: (r, 0, 0))

    return pl.pallas_call(
        functools.partial(attend_kernel, heads, kv_heads, dim, block),
        grid_spec=pltpu.PrefetchScalarGridSpec(
            num_scalar_prefetch=1,
            grid=(rows,),
            in_specs=[
                by_row(group, width), by_row(total, kv.shape[2]), by_row(group, 1), full((group, 1)),
                by_row(group, heads),
            ],
            out_specs=[by_row(group, width), by_row(group, width), by_row(heads, group)],
            scratch_shapes=[
                pltpu.VMEM((repeat * group, dim), bf16),
                pltpu.VMEM((repeat * group, dim), f32),
                pltpu.VMEM((repeat * group, dim), f32),
            ],
        ),
        out_shape=[
            jax.ShapeDtypeStruct((rows, group, width), bf16),
            jax.ShapeDtypeStruct((rows, group, width), bf16),
            jax.ShapeDtypeStruct((rows, heads, group), f32),
        ],
        compiler_params=params(),
        cost_estimate=cost(
            2 * rows * heads * group * total * dim, 2 * kv.size + 6 * q.size, rows * heads * group * total // 2
        ),
        name="attend",
    )(bounds, q, kv, start_col, pos_col, logits)


def attend_back_kernel(heads, kv_heads, dim, block, scale, bounds_ref, q_ref, kv_ref, dgated_ref, att_ref,
                       logit_ref, logit_row_ref, lse_ref, start_ref, pos_ref, nq_ref, rq_ref, cos_ref, sin_ref,
                       gain_ref, ggate_ref, gup_ref, gdown_ref, dq_ref, dlogit_ref, dkv_ref, dgain_ref, ggate_out,
                       gup_out, gdown_out, q2_ref, da2_ref, delta_ref, lse2_ref, dq2_ref, *moved):
    row = pl.program_id(0)
    slots, move_sems = moved[:3], moved[3]
    takes = [
        pltpu.make_async_copy(source, slot, move_sems.at[0, i])
        for i, (source, slot) in enumerate(zip((ggate_ref, gup_ref, gdown_ref), slots))
    ]
    gives = [
        pltpu.make_async_copy(slot, target, move_sems.at[1, i])
        for i, (slot, target) in enumerate(zip(slots, (ggate_out, gup_out, gdown_out)))
    ]

    @pl.when(row == 0)
    def _():
        for move in takes:
            move.start()

    group = q_ref.shape[1]
    repeat = heads // kv_heads
    cosine, sine, gain = cos_ref[...], sin_ref[...], gain_ref[...]

    @pl.when(row == 0)
    def _():
        dgain_ref[...] = jnp.zeros_like(dgain_ref)

    dkv_ref[...] = jnp.zeros_like(dkv_ref)
    for h in range(kv_heads):
        for g in range(repeat):
            n = h * repeat + g
            at = slice(n * dim, (n + 1) * dim)
            part = slice(g * group, (g + 1) * group)
            q2_ref[part, :] = q_ref[0, :, at]
            grad = dgated_ref[0, :, at].astype(f32)
            sigma = jax.nn.sigmoid(logit_ref[0, :, n:n + 1])
            da2_ref[part, :] = (grad * sigma).astype(bf16)
            dot = jnp.sum((grad * att_ref[0, :, at].astype(f32)).T, axis=0, keepdims=True)
            sigma_row = jax.nn.sigmoid(logit_row_ref[0, n:n + 1, :])
            dlogit_ref[0, n:n + 1, :] = dot * sigma_row * (1.0 - sigma_row)
            delta_ref[:, part] = dot * sigma_row
            lse2_ref[:, part] = lse_ref[0, n:n + 1, :]
        dq2_ref[...] = jnp.zeros_like(dq2_ref)

        def body(j, masked):
            at = pl.ds(pl.multiple_of(j * block, block), block)
            keys = kv_ref[0, at, h * dim:(h + 1) * dim]
            values = kv_ref[0, at, (kv_heads + h) * dim:(kv_heads + h + 1) * dim]
            if masked:
                spot = j * block + lax.broadcasted_iota(jnp.int32, (block, group), 0)
                allowed = (spot >= start_ref[0]) & (spot <= pos_ref[...])
            dk = jnp.zeros((block, dim), f32)
            dv = jnp.zeros((block, dim), f32)
            for g in range(repeat):
                part = slice(g * group, (g + 1) * group)
                weight = jnp.exp2(mm(keys, q2_ref[part, :], NT) - lse2_ref[:, part])
                if masked:
                    weight = jnp.where(allowed, weight, 0.0)
                dv += mm(weight.astype(bf16), da2_ref[part, :])
                dprob = mm(values, da2_ref[part, :], NT)
                dscore = (weight * (dprob - delta_ref[:, part])).astype(bf16)
                dk += mm(dscore, q2_ref[part, :])
                dq2_ref[part, :] += mm(dscore, keys, TN)
            dkv_ref[0, at, h * dim:(h + 1) * dim] = (dk * (1.0 / log2e)).astype(bf16)
            dkv_ref[0, at, (kv_heads + h) * dim:(kv_heads + h + 1) * dim] = dv.astype(bf16)

        bounds_loop(bounds_ref, row, body)
        for g in range(repeat):
            n = h * repeat + g
            at = slice(n * dim, (n + 1) * dim)
            part = slice(g * group, (g + 1) * group)
            turned = (dq2_ref[part, :] * scale).astype(bf16).astype(f32)
            back = turned * cosine - pltpu.roll(turned, dim // 2, 1) * sine
            unit = nq_ref[0, :, at].astype(f32)
            dgain_ref[...] += jnp.sum(back * unit, axis=0, keepdims=True)
            inner = back * gain
            mean = jnp.mean(inner * unit, axis=1, keepdims=True)
            dq_ref[0, :, at] = (rq_ref[0, :, n:n + 1] * (inner - unit * mean)).astype(bf16)

    @pl.when(row == 0)
    def _():
        for take, give in zip(takes, gives):
            take.wait()
            give.start()

    @pl.when(row == pl.num_programs(0) - 1)
    def _():
        for give in gives:
            give.wait()


def attend_back(q, kv, dgated, att, logits, logit_rows, lse, bounds, start_row, pos_row, nq, rq, tables, gain, moved,
                heads, kv_heads, dim, block, scale):
    rows, group, width = q.shape
    total = kv.shape[1]
    repeat = heads // kv_heads
    cosine, sine = tables

    def by_row(*shape):
        return pl.BlockSpec((1, *shape), lambda r, *_: (r, 0, 0))

    wide = by_row(group, width)
    return pl.pallas_call(
        functools.partial(attend_back_kernel, heads, kv_heads, dim, block, scale),
        grid_spec=pltpu.PrefetchScalarGridSpec(
            num_scalar_prefetch=1,
            grid=(rows,),
            in_specs=[
                wide, by_row(total, kv.shape[2]), wide, wide, by_row(group, heads), by_row(heads, group),
                by_row(heads, group), by_row(1, group), full((1, group)), wide, by_row(group, heads),
                full((group, dim)), full((group, dim)), full((1, dim)), *[pl.BlockSpec(memory_space=pl.ANY)] * 3,
            ],
            out_specs=[
                wide, by_row(heads, group), by_row(total, kv.shape[2]), full((1, dim)),
                *[pl.BlockSpec(memory_space=pl.ANY)] * 3,
            ],
            scratch_shapes=[
                pltpu.VMEM((repeat * group, dim), bf16),
                pltpu.VMEM((repeat * group, dim), bf16),
                pltpu.VMEM((1, repeat * group), f32),
                pltpu.VMEM((1, repeat * group), f32),
                pltpu.VMEM((repeat * group, dim), f32),
                *[pltpu.VMEM(m.shape, m.dtype) for m in moved],
                pltpu.SemaphoreType.DMA((2, 3)),
            ],
        ),
        out_shape=[
            jax.ShapeDtypeStruct((rows, group, width), bf16),
            jax.ShapeDtypeStruct((rows, heads, group), f32),
            jax.ShapeDtypeStruct(kv.shape, bf16),
            jax.ShapeDtypeStruct((1, dim), f32),
            *[jax.ShapeDtypeStruct(m.shape, m.dtype) for m in moved],
        ],
        compiler_params=params(),
        cost_estimate=cost(
            5 * rows * heads * group * total * dim, 4 * kv.size + 10 * q.size, rows * heads * group * total // 2
        ),
        name="attend_back",
    )(bounds, q, kv, dgated, att, logits, logit_rows, lse, start_row, pos_row, nq, rq, cosine, sine, gain[None], *moved)


def key_back_kernel(kv_heads, dim, dkv_ref, nk_ref, rk_ref, cos_ref, sin_ref, gain_ref, dk_ref, dgain_ref):
    @pl.when(pl.program_id(0) == 0)
    def _():
        dgain_ref[...] = jnp.zeros_like(dgain_ref)

    for h in range(kv_heads):
        at = slice(h * dim, (h + 1) * dim)
        turned = dkv_ref[0, :, at].astype(f32)
        back = turned * cos_ref[...] - pltpu.roll(turned, dim // 2, 1) * sin_ref[...]
        unit = nk_ref[0, :, at].astype(f32)
        dgain_ref[...] += jnp.sum(back * unit, axis=0, keepdims=True)
        inner = back * gain_ref[...]
        mean = jnp.mean(inner * unit, axis=1, keepdims=True)
        dk_ref[0, :, at] = (rk_ref[0, :, h:h + 1] * (inner - unit * mean)).astype(bf16)
    dk_ref[0, :, kv_heads * dim:] = dkv_ref[0, :, kv_heads * dim:]


def key_back(dkv, nk, rk, tables, gain, kv_heads, dim):
    rows, group, width = dkv.shape

    def by_row(*shape):
        return pl.BlockSpec((1, *shape), lambda r: (r, 0, 0))

    return pl.pallas_call(
        functools.partial(key_back_kernel, kv_heads, dim),
        grid=(rows,),
        in_specs=[
            by_row(group, width), by_row(group, kv_heads * dim), by_row(group, kv_heads), full((group, dim)),
            full((group, dim)), full((1, dim)),
        ],
        out_specs=[by_row(group, width), full((1, dim))],
        out_shape=[jax.ShapeDtypeStruct((rows, group, width), bf16), jax.ShapeDtypeStruct((1, dim), f32)],
        compiler_params=params(),
        cost_estimate=cost(20 * dkv.size, 6 * dkv.size),
        name="key_back",
    )(dkv, nk, rk, *tables, gain[None])


def hidden_back_kernel(parts, *refs):
    cots, (w_ref, gate_ref, up_ref, dgate_ref, dup_ref) = refs[:parts], refs[parts:]
    first = 0
    for cot_ref in cots:
        at = slice(first, first + cot_ref.shape[0])
        grad = mm(cot_ref[...], w_ref[...], NT)
        gate, up = gate_ref[at], up_ref[at]
        sigma = jax.nn.sigmoid(gate)
        dgate_ref[at] = (grad * up * sigma * (1.0 + gate * (1.0 - sigma))).astype(bf16)
        dup_ref[at] = (grad * gate * sigma).astype(bf16)
        first = at.stop


def hidden_back(cots, w_down, gate, up, block=256):
    units, width = w_down.shape
    tokens = gate.shape[0]
    column = pl.BlockSpec((tokens, block), lambda j: (0, j))
    return pl.pallas_call(
        functools.partial(hidden_back_kernel, len(cots)),
        grid=(units // block,),
        in_specs=[*[full(c.shape) for c in cots], pl.BlockSpec((block, width), lambda j: (j, 0)), column, column],
        out_specs=[column, column],
        out_shape=[jax.ShapeDtypeStruct((tokens, units), bf16)] * 2,
        compiler_params=params(),
        cost_estimate=cost(2 * tokens * units * width, 40_000_000),
        name="hidden_back",
    )(*cots, w_down, gate, up)


def second_back_kernel(dgate_ref, dup_ref, wgate_ref, wup_ref, out_ref):
    total = mm(dgate_ref[...], wgate_ref[...], NT) + mm(dup_ref[...], wup_ref[...], NT)
    out_ref[...] = total.astype(bf16)


def second_back(d_gate, d_up, w_gate, w_up, block=256):
    width, units = w_gate.shape
    tokens = d_gate.shape[0]
    rows = pl.BlockSpec((block, units), lambda j: (j, 0))
    return pl.pallas_call(
        second_back_kernel,
        grid=(width // block,),
        in_specs=[full(d_gate.shape), full(d_up.shape), rows, rows],
        out_specs=pl.BlockSpec((tokens, block), lambda j: (0, j)),
        out_shape=jax.ShapeDtypeStruct((tokens, width), bf16),
        compiler_params=params(),
        cost_estimate=cost(4 * tokens * units * width, 30_000_000),
        name="second_back",
    )(d_gate, d_up, w_gate, w_up)


def line_barrier(n, me):
    barrier = pltpu.get_barrier_semaphore()
    for way in (1, -1):
        @pl.when((me + way >= 0) & (me + way < n))
        def _():
            pl.semaphore_signal(barrier, inc=1, device_id={"tp": jnp.clip(me + way, 0, n - 1)}, device_id_type=MESH)
    edge = (me == 0) | (me == n - 1)

    @pl.when(edge)
    def _():
        pl.semaphore_wait(barrier, 1)

    @pl.when(jnp.logical_not(edge))
    def _():
        pl.semaphore_wait(barrier, 2)


def line_and_plane_barrier(n, me, bits, n_uly):
    barrier = pltpu.get_barrier_semaphore()
    place = plane_place(n_uly)
    for way in (1, -1):
        @pl.when((me + way >= 0) & (me + way < n))
        def _():
            pl.semaphore_signal(barrier, inc=1, device_id={"tp": jnp.clip(me + way, 0, n - 1)}, device_id_type=MESH)
    for b in range(bits):
        pl.semaphore_signal(barrier, inc=1, device_id=plane_device(place ^ (1 << b), n_uly), device_id_type=MESH)
    edge = (me == 0) | (me == n - 1)

    @pl.when(edge)
    def _():
        pl.semaphore_wait(barrier, bits + 1)

    @pl.when(jnp.logical_not(edge))
    def _():
        pl.semaphore_wait(barrier, bits + 2)


class LineSum:
    def __init__(self, n, pieces, part_at, own, land_ref, sems, out_at=None):
        self.n, self.pieces, self.part_at, self.own, self.land, self.out_at = n, pieces, part_at, own, land_ref, out_at
        self.rs_send, self.rs_recv = sems[:2]
        if out_at:
            self.ag_send, self.ag_recv = sems[2:]
        self.me = lax.axis_index("tp")
        self.stages = [functools.partial(self.reduce_step, k) for k in range(1, n)] + [self.own_step]
        if out_at:
            self.stages += [functools.partial(self.spread_step, k) for k in range(2, n + 1)]

    def inside(self, place):
        return (place >= 0) & (place < self.n)

    def near(self, way):
        return {"tp": jnp.clip(self.me + way, 0, self.n - 1)}

    def reduce_copy(self, way, k, s, source):
        d = 0 if way == 1 else 1
        return pltpu.make_async_remote_copy(
            src_ref=source, dst_ref=self.land.at[d, k - 1, s], send_sem=self.rs_send.at[d, k - 1, s],
            recv_sem=self.rs_recv.at[d, k - 1, s], device_id=self.near(way), device_id_type=MESH)

    def spread_copy(self, way, k, s, owner):
        d = 0 if way == 1 else 1
        rows = self.out_at(jnp.clip(owner, 0, self.n - 1), s)
        return pltpu.make_async_remote_copy(
            src_ref=rows, dst_ref=rows, send_sem=self.ag_send.at[d, k - 1, s], recv_sem=self.ag_recv.at[d, k - 1, s],
            device_id=self.near(way), device_id_type=MESH)

    def reduce_step(self, k, s):
        for way in (1, -1):
            d = 0 if way == 1 else 1
            first = jnp.logical_not(self.inside(self.me - way))
            dest = self.me + way * (self.n - k)
            part = self.part_at(jnp.clip(dest, 0, self.n - 1), s)

            @pl.when(first & self.inside(dest))
            def _():
                self.reduce_copy(way, k, s, part).start()

            if k > 1:
                @pl.when(self.inside(self.me - way) & self.inside(dest))
                def _():
                    landed = self.land.at[d, k - 2, s]
                    self.reduce_copy(way, k - 1, s, landed).wait_recv()
                    landed[...] = (part[...].astype(f32) + landed[...].astype(f32)).astype(bf16)
                    self.reduce_copy(way, k, s, landed).start()

    def own_step(self, s):
        for way in (1, -1):
            d = 0 if way == 1 else 1
            landed = self.land.at[d, self.n - 2, s]

            @pl.when(self.inside(self.me - way))
            def _():
                self.reduce_copy(way, self.n - 1, s, landed).wait_recv()

            @pl.when(jnp.logical_not(self.inside(self.me - way)))
            def _():
                landed[...] = jnp.zeros_like(landed)

        total = self.part_at(self.me, s)[...].astype(f32)
        for d in range(2):
            total = total + self.land[d, self.n - 2, s].astype(f32)
        rows = self.own(s, total)
        if self.out_at:
            self.out_at(self.me, s)[...] = rows
            self.spread_step(1, s)

    def spread_step(self, k, s):
        for way in (1, -1):
            owner = self.me - way * (k - 1)
            if k > 1:
                @pl.when(self.inside(owner))
                def _():
                    self.spread_copy(way, k - 1, s, owner).wait_recv()
            if k < self.n:
                @pl.when(self.inside(owner) & self.inside(self.me + way))
                def _():
                    self.spread_copy(way, k, s, owner).start()

    def drain_reduce(self):
        for s in range(self.pieces):
            for way in (1, -1):
                for k in range(1, self.n):
                    @pl.when(self.inside(self.me + way) & self.inside(self.me + way * (self.n - k)))
                    def _():
                        self.reduce_copy(way, k, s, self.land.at[0, 0, s]).wait_send()

    def drain_spread(self):
        for s in range(self.pieces):
            for way in (1, -1):
                for k in range(1, self.n):
                    owner = self.me - way * (k - 1)

                    @pl.when(self.inside(owner) & self.inside(self.me + way))
                    def _():
                        self.spread_copy(way, k, s, owner).wait_send()

    def run(self, beside=(), quiet=(0, 0), after=None):
        beside, done = list(beside), 0
        steps = self.pieces + len(self.stages) - 1
        turns = [(step, s) for step in range(steps) for s in range(self.pieces) if 0 <= step - s < len(self.stages)]
        slots = [i for i, (step, _) in enumerate(turns) if quiet[0] <= step < steps - quiet[1]]
        for i, (step, s) in enumerate(turns):
            self.stages[step - s](s)
            if after and step - s == len(self.stages) - 1:
                after(s)
            if i in slots:
                until = len(beside) * (slots.index(i) + 1) // len(slots)
                for item in beside[done:until]:
                    item()
                done = until
        self.drain_reduce()
        self.drain_spread()


def line_all_sum(n, seqs, rows, piece, finish, part_ref, out_ref, land_ref, sems, beside=(), quiet=(0, 0),
                 after=None):
    cuts = [(q, c) for q in range(seqs) for c in range(rows // piece)]

    def at(ref):
        return lambda owner, s: ref.at[
            cuts[s][0], pl.ds(pl.multiple_of(owner * rows + cuts[s][1] * piece, piece), piece)]

    LineSum(n, len(cuts), at(part_ref), lambda s, total: finish(*cuts[s], total), land_ref, sems, at(out_ref)).run(
        beside, quiet, after and (lambda s: after(*cuts[s])))


def line_scratch(n, seqs, rows, piece, width):
    count = seqs * (rows // piece)
    return [
        pltpu.VMEM((2, n - 1, count, piece, width), bf16),
        pltpu.SemaphoreType.DMA((2, n - 1, count)), pltpu.SemaphoreType.DMA((2, n - 1, count)),
        pltpu.SemaphoreType.DMA((2, n - 1, count)), pltpu.SemaphoreType.DMA((2, n - 1, count)),
    ]


def norm_forward_kernel(n, seqs, rows, piece, part_ref, x_ref, gain_ref, out_ref, mid_ref, land_ref, *sems):
    def finish(q, c, total):
        at = slice(c * piece, (c + 1) * piece)
        mid = x_ref[q, at].astype(f32) + total
        mid_ref[q, at] = mid
        return (mid * rms_inverse(mid) * gain_ref[...]).astype(bf16)

    line_barrier(n, lax.axis_index("tp"))
    line_all_sum(n, seqs, rows, piece, finish, part_ref, out_ref, land_ref, sems)


def line_call(kernel, n, local, part, others, extra, collective_id, name):
    seqs, rows, width = local
    piece = min(32, rows)
    vm = pl.BlockSpec(memory_space=pltpu.VMEM)
    shapes = [jax.ShapeDtypeStruct(part.shape, bf16), jax.ShapeDtypeStruct(local, f32), *extra]
    return pl.pallas_call(
        functools.partial(kernel, n, seqs, rows, piece),
        in_specs=[vm] * (1 + len(others)),
        out_specs=[vm] * len(shapes),
        out_shape=shapes,
        scratch_shapes=line_scratch(n, seqs, rows, piece, width),
        compiler_params=params(collective_id=collective_id, has_side_effects=True),
        cost_estimate=cost(20 * part.size, 100_000_000),
        name=name,
    )(part, *others)


def plane_place(n_uly):
    return lax.axis_index("ctx") * n_uly + lax.axis_index("uly")


def plane_device(place, n_uly):
    return {"ctx": place // n_uly, "uly": lax.rem(place, n_uly)}


def plane_barrier(bits, me, n_uly):
    barrier = pltpu.get_barrier_semaphore()
    for b in range(bits):
        pl.semaphore_signal(barrier, inc=1, device_id=plane_device(me ^ (1 << b), n_uly), device_id_type=MESH)
    pl.semaphore_wait(barrier, bits)


def ways(bits):
    upper = list(range(1, bits))
    return upper, upper[::-1]


def span(order):
    out = [0]
    for b in order:
        out += [e | (1 << b) for e in out]
    return out


def plane_gather_kernel(bits, n_uly, own_ref, out_ref, copy_sem, send_sem, recv_sem):
    me = plane_place(n_uly)
    rows, half = own_ref.shape[1], own_ref.shape[2] // 2
    plane_barrier(bits, me, n_uly)
    orders = [w + [0] for w in ways(bits)]

    def block(place, d):
        return out_ref.at[:, pl.ds(pl.multiple_of(place * rows, rows), rows), pl.ds(d * half, half)]

    def copy(d, level, e):
        bit = orders[d][level]
        source = own_ref.at[:, :, pl.ds(d * half, half)] if e == 0 else block(me ^ e, d)
        return pltpu.make_async_remote_copy(
            src_ref=source, dst_ref=block(me ^ e, d), send_sem=send_sem.at[d, e | (1 << bit)],
            recv_sem=recv_sem.at[d, e | (1 << bit)], device_id=plane_device(me ^ (1 << bit), n_uly),
            device_id_type=MESH)

    own = [pltpu.make_async_copy(own_ref.at[:, :, pl.ds(d * half, half)], block(me, d), copy_sem.at[d]) for d in range(2)]
    for c in own:
        c.start()
    for level in range(bits):
        for d in range(2):
            for e in span(orders[d][:level]):
                if level > 0 and e >> orders[d][level - 1] & 1:
                    continue
                copy(d, level, e).start()
        for d in range(2):
            for e in span(orders[d][:level]):
                copy(d, level, e).wait_recv()
                if level + 1 < bits:
                    copy(d, level + 1, e | (1 << orders[d][level])).start()
    for d in range(2):
        own[d].wait()
        for level in range(bits):
            for e in span(orders[d][:level]):
                copy(d, level, e).wait_send()


def plane_gather(own, sizes, collective_id):
    n_ctx, n_uly = sizes
    count = n_ctx * n_uly
    bits = count.bit_length() - 1
    seqs, rows, width = own.shape
    if own.size * count * 2 > 12 << 20 or count != 1 << bits or bits < 2:
        return lax.all_gather(own, ("ctx", "uly"), axis=1, tiled=True)
    vm = pl.BlockSpec(memory_space=pltpu.VMEM)
    return pl.pallas_call(
        functools.partial(plane_gather_kernel, bits, n_uly),
        in_specs=[vm], out_specs=vm,
        out_shape=jax.ShapeDtypeStruct((seqs, rows * count, width), own.dtype),
        scratch_shapes=[pltpu.SemaphoreType.DMA((2,)), pltpu.SemaphoreType.DMA((2, count)), pltpu.SemaphoreType.DMA((2, count))],
        compiler_params=params(collective_id=collective_id, has_side_effects=True),
        cost_estimate=cost(0, 100_000_000),
        name="plane_gather",
    )(own)


class PlaneSum:
    def __init__(self, bits, n_uly, make, store, buf_ref, land_ref, send, recv):
        self.bits, self.n_uly, self.make, self.store = bits, n_uly, make, store
        self.buf, self.land, self.send, self.recv = buf_ref, land_ref, send, recv
        self.me = plane_place(n_uly)
        width = buf_ref.shape[-1]
        half = max(width // 256, 1) * 128
        self.parts = [(0, half), (half, width - half)]
        self.orders = ways(bits)

    @staticmethod
    def scratch(bits, rows, width):
        n = 1 << bits
        return [
            pltpu.VMEM((n, rows, width), bf16), pltpu.VMEM((n - 1, rows, width), bf16),
            pltpu.SemaphoreType.DMA((3, n)), pltpu.SemaphoreType.DMA((3, n)),
        ]

    def slot(self, e):
        return e

    def view(self, ref, i, d):
        return ref.at[(i, *[slice(None)] * (len(ref.shape) - 2), pl.ds(*self.parts[d]))]

    def first_copy(self, e):
        return pltpu.make_async_remote_copy(
            src_ref=self.buf.at[e], dst_ref=self.land.at[e - 1], send_sem=self.send.at[2, e],
            recv_sem=self.recv.at[2, e], device_id=plane_device(self.me ^ 1, self.n_uly), device_id_type=MESH)

    def copy(self, d, level, e):
        return pltpu.make_async_remote_copy(
            src_ref=self.view(self.buf, self.slot(e), d), dst_ref=self.view(self.land, e - 1, d),
            send_sem=self.send.at[d, e],
            recv_sem=self.recv.at[d, e],
            device_id=plane_device(self.me ^ (1 << self.orders[d][level]), self.n_uly), device_id_type=MESH)

    def sent(self, d, level):
        return [(1 << self.orders[d][level]) | e for e in span(self.orders[d][level + 1:])]

    def compute(self):
        n = 1 << self.bits
        for e in range(1, n, 2):
            self.buf[e] = self.make(self.me ^ e).astype(bf16)
            self.first_copy(e).start()
        for e in range(0, n, 2):
            self.buf[e] = self.make(self.me ^ e).astype(bf16)

    def pair(self):
        for e in range(1, 1 << self.bits, 2):
            self.first_copy(e).wait_recv()
            kept = self.slot(e - 1)
            self.buf[kept] = (self.buf[kept].astype(f32) + self.land[e - 1].astype(f32)).astype(bf16)

    def push(self, level):
        for d in range(2):
            for e in self.sent(d, level):
                self.copy(d, level, e).start()

    def pull(self, level):
        for d in range(2):
            for e in self.sent(d, level):
                kept = self.view(self.buf, self.slot(e ^ (1 << self.orders[d][level])), d)
                self.copy(d, level, e).wait_recv()
                total = kept[...].astype(f32) + self.view(self.land, e - 1, d)[...].astype(f32)
                if level == self.bits - 2:
                    self.store(pl.ds(*self.parts[d]), total)
                else:
                    kept[...] = total.astype(bf16)

    def finish(self):
        for e in range(1, 1 << self.bits, 2):
            self.first_copy(e).wait_send()
        for d in range(2):
            for level in range(self.bits - 1):
                for e in self.sent(d, level):
                    self.copy(d, level, e).wait_send()


def blocks_sum_kernel(bits, n_uly, parts_ref, out_ref, *scratch):
    me = plane_place(n_uly)
    plane_barrier(bits, me, n_uly)
    seqs, rows = out_ref.shape[0], out_ref.shape[1]

    def make(place):
        return parts_ref[:, pl.ds(pl.multiple_of(place * rows, rows), rows)].reshape(seqs * rows, -1)

    def store(at, total):
        out_ref[:, :, at] = total.reshape(seqs, rows, -1).astype(out_ref.dtype)

    job = PlaneSum(bits, n_uly, make, store, *scratch)
    job.compute()
    job.pair()
    for level in range(bits - 1):
        job.push(level)
        job.pull(level)
    job.finish()


def blocks_sum(parts, sizes, collective_id):
    n_ctx, n_uly = sizes
    count = n_ctx * n_uly
    bits = count.bit_length() - 1
    seqs, total, width = parts.shape
    rows = total // count
    if parts.size * 2 > 12 << 20 or count != 1 << bits or bits < 2:
        return lax.psum_scatter(parts, ("ctx", "uly"), scatter_dimension=1, tiled=True)
    vm = pl.BlockSpec(memory_space=pltpu.VMEM)
    return pl.pallas_call(
        functools.partial(blocks_sum_kernel, bits, n_uly),
        in_specs=[vm],
        out_specs=vm,
        out_shape=jax.ShapeDtypeStruct((seqs, rows, width), bf16),
        scratch_shapes=PlaneSum.scratch(bits, seqs * rows, width),
        compiler_params=params(collective_id=collective_id, has_side_effects=True),
        cost_estimate=cost(10 * parts.size, 100_000_000),
        name="blocks_sum",
    )(parts)


def outer_sums_kernel(bits, n_uly, use, *refs):
    count, kinds = len(use), max(use) + 1
    lefts, refs = [refs[k] for k in use], refs[kinds:]
    rights, outs, scratch = refs[:count], refs[count:2 * count], refs[2 * count:]
    plane_barrier(bits, plane_place(n_uly), n_uly)
    jobs = []
    for i in range(count):
        each = outs[i].shape[0]

        def make(place, i=i, each=each):
            left = lefts[i][:, pl.ds(pl.multiple_of(place * each, each), each)]
            return mm(left, rights[i][...], TN)

        def store(at, total, i=i):
            outs[i][:, at] = total

        jobs.append(PlaneSum(bits, n_uly, make, store, *scratch[4 * i:4 * i + 4]))
    last = bits - 2
    for i in range(count + last + 1):
        if i < count:
            jobs[i].compute()
            jobs[i].pair()
            jobs[i].push(0)
        for level in range(last + 1):
            j = i - 1 - level
            if 0 <= j < count:
                jobs[j].pull(level)
                if level < last:
                    jobs[j].push(level + 1)
                else:
                    jobs[j].finish()


def fits_plane(sizes, width):
    places = sizes[0] * sizes[1]
    return places & (places - 1) == 0 and places >= 4 and width // places % 128 == 0


def outer_sums(kinds, use, rights, sizes, collective_id):
    lefts = [kinds[k] for k in use]
    n_ctx, n_uly = sizes
    places = n_ctx * n_uly
    bits = places.bit_length() - 1
    count = len(lefts)
    if not fits_plane(sizes, lefts[0].shape[1]):
        return [
            lax.psum_scatter(mm(l, r, TN).astype(bf16), ("ctx", "uly"), scatter_dimension=0, tiled=True).astype(f32)
            for l, r in zip(lefts, rights)
        ]
    vm = pl.BlockSpec(memory_space=pltpu.VMEM)
    shapes = [(l.shape[1] // places, r.shape[1]) for l, r in zip(lefts, rights)]
    scratch = []
    for shape in shapes:
        scratch += PlaneSum.scratch(bits, *shape)
    work = sum(l.size * r.shape[1] for l, r in zip(lefts, rights))
    return pl.pallas_call(
        functools.partial(outer_sums_kernel, bits, n_uly, use),
        in_specs=[vm] * (len(kinds) + count),
        out_specs=[vm] * count,
        out_shape=[jax.ShapeDtypeStruct(s, f32) for s in shapes],
        scratch_shapes=scratch,
        compiler_params=pltpu.CompilerParams(
            collective_id=collective_id, has_side_effects=True, vmem_limit_bytes=vmem_bytes),
        cost_estimate=cost(2 * work, 200_000_000),
        name="outer_sums",
    )(*kinds, *rights)


def back_finish(piece, cot_ref, mid_ref, gain_ref, dmid_ref, dgain_ref):
    def finish(q, c, total):
        at = slice(c * piece, (c + 1) * piece)
        mid = mid_ref[q, at]
        inverse = rms_inverse(mid)
        unit = mid * inverse
        dgain_ref[...] += jnp.sum(total * unit, axis=0, keepdims=True)
        inner = total * gain_ref[...]
        mean = jnp.mean(inner * unit, axis=-1, keepdims=True)
        d_mid = cot_ref[q, at].astype(f32) + inverse * (inner - unit * mean)
        dmid_ref[q, at] = d_mid
        return d_mid.astype(bf16)

    return finish


def plain_back_kernel(n, seqs, rows, piece, part_ref, cot_ref, mid_ref, gain_ref, out_ref, dmid_ref, dgain_ref,
                      land_ref, *sems):
    dgain_ref[...] = jnp.zeros_like(dgain_ref)
    line_barrier(n, lax.axis_index("tp"))
    line_all_sum(n, seqs, rows, piece, back_finish(piece, cot_ref, mid_ref, gain_ref, dmid_ref, dgain_ref), part_ref,
                 out_ref, land_ref, sems)


class StreamedOuter:
    def __init__(self, jobs, each, left_slots, right_slots, left_sems, right_sems):
        self.jobs, self.each = jobs, each
        self.left, self.right, self.left_sems, self.right_sems = left_slots, right_slots, left_sems, right_sems

    def right_copy(self, i):
        _, right, half, _ = self.jobs[i]
        wide = self.right.shape[-1]
        return pltpu.make_async_copy(
            right.at[:, pl.ds(half * wide, wide)], self.right.at[i % 2], self.right_sems.at[i % 2])

    def left_copies(self, i, turn, place):
        at = pl.ds(pl.multiple_of(place * self.each, self.each), self.each)
        copies, first = [], 0
        for k, source in enumerate(self.jobs[i][0]):
            rows = pl.ds(first, source.shape[0])
            copies.append(pltpu.make_async_copy(
                source.at[:, at], self.left.at[turn % 2, rows], self.left_sems.at[turn % 2, k]))
            first += source.shape[0]
        return copies

    def product(self, i, turn, places, take):
        if turn == 0:
            if i == 0:
                self.right_copy(0).start()
                for copy in self.left_copies(0, 0, places[0]):
                    copy.start()
            self.right_copy(i).wait()
            if i + 1 < len(self.jobs):
                self.right_copy(i + 1).start()
        if turn + 1 < len(places):
            for copy in self.left_copies(i, turn + 1, places[turn + 1]):
                copy.start()
        for copy in self.left_copies(i, turn, places[turn]):
            copy.wait()
        value = mm(self.left[turn % 2], self.right[i % 2], TN)
        if turn + 1 == len(places) and i + 1 < len(self.jobs):
            for copy in self.left_copies(i + 1, 0, places[0]):
                copy.start()
        take(value)


def norm_back_kernel(n, seqs, rows, piece, bits, n_uly, parts, part_ref, cot_ref, mid_ref, gain_ref, wo_ref, a2_ref, *refs):
    cot_refs, refs = refs[:parts], refs[parts:]
    norm_back_body(n, seqs, rows, piece, bits, n_uly, part_ref, cot_ref, mid_ref, gain_ref, wo_ref, a2_ref, cot_refs,
                   *refs)


def norm_back_body(n, seqs, rows, piece, bits, n_uly, part_ref, cot_ref, mid_ref, gain_ref, wo_ref, a2_ref, cot_refs,
                   dgate_ref, dup_ref, hidden_ref, out_ref, dmid_ref, dgain_ref, ggate_ref, gup_ref, gdown_ref, dgated_ref,
                     land_ref, rs_send, rs_recv, ag_send, ag_recv, left_slots, right_slots, left_sems, right_sems,
                     *plane_scratch):
    dgain_ref[...] = jnp.zeros_like(dgain_ref)

    finish = back_finish(piece, cot_ref, mid_ref, gain_ref, dmid_ref, dgain_ref)
    wide = right_slots.shape[-1]
    halves = ggate_ref.shape[1] // wide
    jobs = [
        (left, right, half, out)
        for left, right, out in (
            ((a2_ref,), dgate_ref, ggate_ref), ((a2_ref,), dup_ref, gup_ref), (cot_refs, hidden_ref, gdown_ref))
        for half in range(halves)
    ]
    streamed = StreamedOuter(jobs, ggate_ref.shape[0], left_slots, right_slots, left_sems, right_sems)
    sums = []
    for i, (_, _, half, out) in enumerate(jobs):
        def store(at, total, half=half, out=out):
            to = pl.ds(half * wide + at.start, at.size)
            if out is gdown_ref:
                out[to] = total.T
            else:
                out[:, to] = total

        buf = plane_scratch[i % 3]
        land, send, recv = plane_scratch[3 + 3 * i:6 + 3 * i]
        sums.append(PlaneSum(bits, n_uly, None, store, buf, land, send, recv))
    last = bits - 2

    order = list(range(1, 1 << bits, 2)) + list(range(0, 1 << bits, 2))
    quiet = back_quiet

    def branch(q, c):
        spots = [slice(t * rows + c * piece, t * rows + (c + 1) * piece) for t in range(n)]
        value = mm(jnp.concatenate([out_ref[q, at] for at in spots], axis=0), wo_ref[...], NT).astype(bf16)
        for t, at in enumerate(spots):
            dgated_ref[q, at] = value[t * piece:(t + 1) * piece]

    beside = []

    def product(i, turn):
        def take(value):
            sums[i].buf[order[turn]] = value.astype(bf16)
            if order[turn] % 2:
                sums[i].first_copy(order[turn]).start()

        streamed.product(i, turn, [sums[i].me ^ e for e in order], take)

    for i in range(len(jobs) + last + 1):
        if i < len(jobs):
            beside += [functools.partial(product, i, turn) for turn in range(len(order))]
        for level in range(last):
            j = i - 1 - level
            if 0 <= j < len(jobs):
                beside += [functools.partial(sums[j].pull, level), functools.partial(sums[j].push, level + 1)]
        if i < len(jobs):
            beside += [sums[i].pair, functools.partial(sums[i].push, 0)]
        if 0 <= i - 1 - last < len(jobs):
            beside += [functools.partial(sums[i - 1 - last].pull, last), sums[i - 1 - last].finish]

    line_and_plane_barrier(n, lax.axis_index("tp"), bits, n_uly)
    line_all_sum(n, seqs, rows, piece, finish, part_ref, out_ref, land_ref, (rs_send, rs_recv, ag_send, ag_recv),
                 beside, quiet, branch)


def norm_back(part, cotangent, middle, gain, w_output, a2, cots, d_gate, d_up, hidden, n, sizes, collective_id):
    n_ctx, n_uly = sizes
    places = n_ctx * n_uly
    bits = places.bit_length() - 1
    seqs, rows, width = cotangent.shape
    tokens, units = d_gate.shape
    each = width // places
    if not fits_plane(sizes, width) or units % 512:
        out, d_mid, dgain = line_call(
            plain_back_kernel, n, cotangent.shape, part, (cotangent, middle, gain[None]),
            (jax.ShapeDtypeStruct((1, width), f32),), collective_id, "norm_back")
        grads = outer_sums((a2, jnp.concatenate(cots)), (0, 0, 1), (d_gate, d_up, hidden), sizes, 0)
        d_gated = mm(flatten(out), w_output, NT).astype(bf16).reshape(*part.shape[:2], -1)
        return (out, d_mid, dgain, *grads[:2], grads[2].T, d_gated)
    piece = min(back_piece, rows)
    half = units // 2
    vm, anywhere = pl.BlockSpec(memory_space=pltpu.VMEM), pl.BlockSpec(memory_space=pl.ANY)
    shapes = [
        jax.ShapeDtypeStruct(part.shape, bf16), jax.ShapeDtypeStruct(cotangent.shape, f32),
        jax.ShapeDtypeStruct((1, width), f32), *[jax.ShapeDtypeStruct((each, units), f32)] * 2,
        jax.ShapeDtypeStruct((units, each), f32), jax.ShapeDtypeStruct((*part.shape[:2], w_output.shape[0]), bf16),
    ]
    plane_scratch = [PlaneSum.scratch(bits, each, half) for _ in range(6)]
    return pl.pallas_call(
        functools.partial(norm_back_kernel, n, seqs, rows, piece, bits, n_uly, len(cots)),
        in_specs=[vm] * 5 + [anywhere] * (4 + len(cots)),
        out_specs=[vm] * len(shapes),
        out_shape=shapes,
        scratch_shapes=[
            *line_scratch(n, seqs, rows, piece, width),
            pltpu.VMEM((2, tokens, each), bf16), pltpu.VMEM((2, tokens, half), bf16),
            pltpu.SemaphoreType.DMA((2, len(cots))), pltpu.SemaphoreType.DMA((2,)),
            plane_scratch[0][0], plane_scratch[0][0], plane_scratch[0][0],
            *[item for scratch in plane_scratch for item in scratch[1:]],
        ],
        compiler_params=pltpu.CompilerParams(
            collective_id=collective_id, has_side_effects=True, vmem_limit_bytes=vmem_bytes),
        cost_estimate=cost(6 * tokens * units * width, 250_000_000),
        name="norm_back",
    )(part, cotangent, middle, gain[None], w_output, a2, *cots, d_gate, d_up, hidden)


class StoredSum(PlaneSum):
    def __init__(self, bits, n_uly, source, store, buf_ref, land_ref, send, recv, load):
        super().__init__(bits, n_uly, None, store, buf_ref, land_ref, send, recv)
        self.source, self.load = source, load

    @staticmethod
    def scratch(bits, *shape):
        n = 1 << bits
        return [
            pltpu.VMEM((n // 2, *shape), bf16), pltpu.VMEM((n - 1, *shape), bf16),
            pltpu.SemaphoreType.DMA((3, n)), pltpu.SemaphoreType.DMA((3, n)), pltpu.SemaphoreType.DMA((n // 2,)),
        ]

    def slot(self, e):
        return e // 2

    def first_copy(self, e):
        return pltpu.make_async_remote_copy(
            src_ref=self.source(self.me ^ e), dst_ref=self.land.at[e - 1], send_sem=self.send.at[2, e],
            recv_sem=self.recv.at[2, e], device_id=plane_device(self.me ^ 1, self.n_uly), device_id_type=MESH)

    def load_copy(self, e):
        return pltpu.make_async_copy(self.source(self.me ^ e), self.buf.at[e // 2], self.load.at[e // 2])

    def compute(self):
        for e in range(1, 1 << self.bits, 2):
            self.first_copy(e).start()
            self.load_copy(e - 1).start()

    def pair(self):
        for e in range(0, 1 << self.bits, 2):
            self.load_copy(e).wait()
        super().pair()


def all_barrier(n, bits, n_uly):
    barrier = pltpu.get_barrier_semaphore()
    me, place = lax.axis_index("tp"), plane_place(n_uly)
    for d in range(1, n):
        pl.semaphore_signal(barrier, inc=1, device_id={"tp": lax.rem(me + d, n)}, device_id_type=MESH)
    for b in range(bits):
        pl.semaphore_signal(barrier, inc=1, device_id=plane_device(place ^ (1 << b), n_uly), device_id_type=MESH)
    pl.semaphore_wait(barrier, n - 1 + bits)


def layer_back_kernel(
    n, bits, n_uly, heads, kv_heads, dim, dkv_ref, first_ref, dbranch_ref, dq_ref, dlogit_ref, nk_ref, rk_ref, cos_ref,
    sin_ref, kgain_ref, wq_ref, wk_ref, wv_ref, wg_ref, gated_ref, x_ref, gain_ref, dmid_ref, dqgain_ref, dmlp_ref, gin_ref, gq_ref, gk_ref,
    gv_ref, gh_ref, gout_ref, gattn_ref, gmlp_ref, gqn_ref, gkn_ref, all_ref, cut_ref, part_ref, sum_ref, line_land, rs_send, rs_recv, left_slots, left_sems,
    vec_ref, vec_land, vec_send, vec_recv, *plane_scratch,
):
    seqs, _, cut_count, piece, _ = dq_ref.shape
    rows, width = cut_count * piece, x_ref.shape[-1]
    group = n * rows
    cuts = [(q, c) for q in range(seqs) for c in range(cut_count)]
    q_cols, kv_cols = heads * dim, kv_heads * dim
    n_main = q_cols + 2 * kv_cols
    each = gq_ref.shape[0]
    place, line_me = plane_place(n_uly), lax.axis_index("tp")

    vec_ref[0] = jnp.zeros_like(vec_ref[0])
    vec_ref[0, :, width:2 * width] = dmlp_ref[...]
    vec_ref[0, :, 2 * width:2 * width + dim] = dqgain_ref[...]

    def row_at(q, t, c):
        return q * group + t * rows + c * piece

    def key_values(s):
        q, c = cuts[s]

        def store(at, total):
            sum_ref[:, :, at] = total.astype(bf16)

        return StoredSum(
            bits, n_uly, lambda at: dkv_ref.at[q, pl.ds(pl.multiple_of(at * n, n), n), c], store,
            *plane_scratch[5 * s:5 * s + 5])

    sums = [key_values(s) for s in range(len(cuts))]

    def turn(s):
        q, c = cuts[s]
        for t in range(n):
            at = slice(t * piece, (t + 1) * piece)
            cut_ref[at, :q_cols] = dq_ref[q, t, c]
            for h in range(kv_heads):
                turned = sum_ref[t, :, h * dim:(h + 1) * dim].astype(f32)
                back = turned * cos_ref[t, c] - pltpu.roll(turned, dim // 2, 1) * sin_ref[t, c]
                unit = nk_ref[q, t, c, :, h * dim:(h + 1) * dim].astype(f32)
                vec_ref[0, :, 2 * width + dim:] += jnp.sum(back * unit, axis=0, keepdims=True)
                inner = back * kgain_ref[...]
                mean = jnp.mean(inner * unit, axis=1, keepdims=True)
                cut_ref[at, q_cols + h * dim:q_cols + (h + 1) * dim] = (
                    rk_ref[q, t, c, :, h:h + 1] * (inner - unit * mean)).astype(bf16)
            cut_ref[at, q_cols + kv_cols:n_main] = sum_ref[t, :, kv_cols:]
            cut_ref[at, n_main:] = dlogit_ref[q, t, c]
        partial = mm(cut_ref[:, :q_cols], wq_ref[...], NT)
        partial += mm(cut_ref[:, q_cols:q_cols + kv_cols], wk_ref[...], NT)
        partial += mm(cut_ref[:, q_cols + kv_cols:n_main], wv_ref[...], NT)
        partial += mm(cut_ref[:, n_main:n_main + heads], wg_ref[...])
        partial = partial.astype(bf16)
        for t in range(n):
            at = slice(t * piece, (t + 1) * piece)
            to = slice(row_at(q, t, c), row_at(q, t, c) + piece)
            part_ref[to] = partial[at]
            all_ref[to] = cut_ref[at]

    split = line_land.shape[2] // len(cuts)
    short = piece // split

    def part_at(owner, p):
        q, c = cuts[p // split]
        return part_ref.at[pl.ds(pl.multiple_of(row_at(q, owner, c) + p % split * short, short), short)]

    def own(p, total):
        q, c = cuts[p // split]
        at = slice(c * piece + p % split * short, c * piece + (p % split + 1) * short)
        x = x_ref[q, at].astype(f32)
        inverse = rms_inverse(x)
        unit = x * inverse
        inner = total * gain_ref[...]
        mean = jnp.mean(inner * unit, axis=-1, keepdims=True)
        gin_ref[q, at] = dmid_ref[q, at] + inverse * (inner - unit * mean)

    line = LineSum(n, len(cuts) * split, part_at, own, line_land, (rs_send, rs_recv))

    order = list(range(1, 1 << bits, 2)) + list(range(0, 1 << bits, 2))
    turns = [(dbranch_ref, e) for e in order] + [(first_ref, e) for e in order]

    def left_copy(i):
        source, e = turns[i]
        at = pl.ds(pl.multiple_of((place ^ e) * each, each), each)
        return pltpu.make_async_copy(source.at[:, at], left_slots.at[i % 2], left_sems.at[i % 2])

    def store_out(at, total):
        gout_ref[at] = total.T

    def store_first(at, total):
        if at.start + at.size > n_main:
            gh_ref[...] = total[:, n_main - at.start:].T[:heads]
        first = 0
        for out in (gq_ref, gk_ref, gv_ref):
            lo, hi = max(first, at.start), min(first + out.shape[1], at.start + at.size)
            if lo < hi:
                out[:, lo - first:hi - first] = total[:, lo - at.start:hi - at.start]
            first += out.shape[1]

    scratch = plane_scratch[5 * len(cuts):]
    out_sum = PlaneSum(bits, n_uly, None, store_out, *scratch[:4])
    first_sum = PlaneSum(bits, n_uly, None, store_first, *scratch[4:])

    def product(i):
        e = turns[i][1]
        if i + 1 < len(turns):
            left_copy(i + 1).start()
        left_copy(i).wait()
        job = out_sum if i < len(order) else first_sum
        value = mm(left_slots[i % 2], gated_ref[...] if i < len(order) else all_ref[...], TN)
        job.buf[e] = value.astype(bf16)
        if e % 2:
            job.first_copy(e).start()
        if job is first_sum:
            at = pl.ds(pl.multiple_of((place ^ e) * each, each), each)
            lanes, first = jnp.zeros((each, 128), f32), 0
            for w_ref in (wq_ref, wk_ref, wv_ref):
                for k in range(0, w_ref.shape[1], 128):
                    lanes += value[:, first + k:first + k + 128] * w_ref[at, k:k + 128].astype(f32)
                first += w_ref.shape[1]
            total = jnp.sum(lanes.T, axis=0, keepdims=True)
            last = value[:, n_main:].T[:heads] * wg_ref[:, at].astype(f32)
            total += jnp.sum(last, axis=0, keepdims=True)
            vec_ref[0, :, at] = total / gain_ref[:, at]

    line_bits = n.bit_length() - 1
    steps = bits + line_bits

    def vec_copy(k):
        partner = plane_device(place ^ (1 << k), n_uly) if k < bits else {"tp": line_me ^ (1 << (k - bits))}
        return pltpu.make_async_remote_copy(
            src_ref=vec_ref.at[k], dst_ref=vec_land.at[k], send_sem=vec_send.at[k], recv_sem=vec_recv.at[k],
            device_id=partner, device_id_type=MESH)

    def vec_step(k):
        if k > 0:
            vec_copy(k - 1).wait_recv()
            vec_ref[k] = vec_ref[k - 1] + vec_land[k - 1]
        if k < steps:
            vec_copy(k).start()

    def levels(job):
        items = []
        for level in range(bits - 1):
            items.append(functools.partial(job.pull, level))
            if level + 1 < bits - 1:
                items.append(functools.partial(job.push, level + 1))
        return items

    early = [functools.partial(product, i) for i in range(len(order))]
    early += [out_sum.pair, functools.partial(out_sum.push, 0)]
    late = [functools.partial(product, i) for i in range(len(order), len(turns))]
    late.append(functools.partial(vec_step, 0))
    late += levels(out_sum)[:2]
    late += [first_sum.pair, functools.partial(first_sum.push, 0)]
    rest = levels(out_sum)[2:] + levels(first_sum)
    for k in range(1, steps + 1):
        late.append(functools.partial(vec_step, k))
        if k % 2 == 0 and rest:
            late.append(rest.pop(0))
    late += rest

    all_barrier(n, bits, n_uly)
    for job in sums:
        job.compute()
    left_copy(0).start()
    ready = 0
    line_steps = split * (len(cuts) + bits - 1) + n - 1
    for step in range(-(-line_steps // split)):
        if step < len(cuts):
            sums[step].pair()
            sums[step].push(0)
        for level in range(bits - 1):
            j = step - 1 - level
            if 0 <= j < len(cuts):
                sums[j].pull(level)
                if level + 1 < bits - 1:
                    sums[j].push(level + 1)
                else:
                    turn(j)
                    ready += 1
        for turn_of in range(split * step, split * (step + 1)):
            for p in range(line.pieces):
                stage = turn_of - p - split * (bits - 1)
                if 0 <= stage < n:
                    line.stages[stage](p)
                    queue = early or (late if ready == len(cuts) else [])
                    for item in queue[:tail_items]:
                        item()
                    del queue[:tail_items]
    for item in early + late:
        item()
    line.drain_reduce()
    first = 0
    for out in (gattn_ref, gmlp_ref, gqn_ref, gkn_ref):
        out[...] = vec_ref[steps, :, first:first + out.shape[1]]
        first += out.shape[1]
    for k in range(steps):
        vec_copy(k).wait_send()
    for job in (*sums, out_sum, first_sum):
        job.finish()


def layer_back(d_kv, first, d_branch, d_q, d_logit, nk, rk, tables, key_norm, weights, gated, x, attn_norm, d_mid, d_qgain,
               d_mlp, n, sizes, heads, kv_heads, collective_id):
    n_ctx, n_uly = sizes
    places = n_ctx * n_uly
    bits = places.bit_length() - 1
    seqs, rows, width = x.shape
    group, dim = n * rows, key_norm.shape[0]
    piece = min(64, rows)
    cut_count = rows // piece
    each = width // places
    tokens = seqs * group
    wide = (heads + 2 * kv_heads) * dim + d_logit.shape[-1]
    small = 2 * width + 2 * dim
    kv_wide = d_kv.shape[-1]
    pieces = seqs * cut_count
    steps = bits + n.bit_length() - 1

    def tiles(values):
        return values.reshape(seqs, n, cut_count, piece, values.shape[-1])

    vm, anywhere = pl.BlockSpec(memory_space=pltpu.VMEM), pl.BlockSpec(memory_space=pl.ANY)
    plane_scratch = []
    for _ in range(pieces):
        plane_scratch += StoredSum.scratch(bits, n, piece, kv_wide)
    plane_scratch += PlaneSum.scratch(bits, each, heads * dim) + PlaneSum.scratch(bits, each, wide)
    shapes = [
        jax.ShapeDtypeStruct(shape, f32) for shape in (
            x.shape, (each, heads * dim), (each, kv_heads * dim), (each, kv_heads * dim), (heads, each),
            (heads * dim, each), (1, width), (1, width), (1, dim), (1, dim))
    ]
    line = line_scratch(n, seqs, rows, min(tail_piece, piece), width)
    return pl.pallas_call(
        functools.partial(layer_back_kernel, n, bits, n_uly, heads, kv_heads, dim),
        in_specs=[anywhere] * 3 + [vm] * 17,
        out_specs=[vm] * len(shapes),
        out_shape=shapes,
        scratch_shapes=[
            pltpu.VMEM((tokens, wide), bf16), pltpu.VMEM((n * piece, wide), bf16), pltpu.VMEM((tokens, width), bf16),
            pltpu.VMEM((n, piece, kv_wide), bf16), *line[:3],
            pltpu.VMEM((2, tokens, each), bf16), pltpu.SemaphoreType.DMA((2,)),
            pltpu.VMEM((steps + 1, 1, small), f32), pltpu.VMEM((steps, 1, small), f32),
            pltpu.SemaphoreType.DMA((steps,)), pltpu.SemaphoreType.DMA((steps,)),
            *plane_scratch,
        ],
        compiler_params=pltpu.CompilerParams(
            collective_id=collective_id, has_side_effects=True, vmem_limit_bytes=vmem_bytes),
        cost_estimate=cost(4 * tokens * width * wide, 250_000_000),
        name="layer_back",
    )(d_kv.reshape(seqs, places * n, cut_count, piece, kv_wide), first, d_branch, tiles(d_q), tiles(d_logit), tiles(nk),
      tiles(rk), *[t.reshape(n, cut_count, piece, dim) for t in tables], key_norm[None], *weights, gated, x,
      attn_norm[None], d_mid, d_qgain, d_mlp)


class LineSpread(LineSum):
    def __init__(self, n, pieces, own, out_at, sems):
        super().__init__(n, pieces, None, own, None, (None, None, *sems), out_at)
        self.stages = [self.own_step] + [functools.partial(self.spread_step, k) for k in range(2, n + 1)]

    def own_step(self, s):
        self.out_at(self.me, s)[...] = self.own(s)
        self.spread_step(1, s)


class PlaneSpread:
    def __init__(self, bits, n_uly, block, send, recv):
        self.bits, self.n_uly, self.block, self.send, self.recv = bits, n_uly, block, send, recv
        self.me = plane_place(n_uly)
        self.orders = [w + [0] for w in ways(bits)]

    def copy(self, d, level, e):
        bit = 1 << self.orders[d][level]
        block = self.block(self.me ^ e, d)
        return pltpu.make_async_remote_copy(
            src_ref=block, dst_ref=block, send_sem=self.send.at[d, e | bit], recv_sem=self.recv.at[d, e | bit],
            device_id=plane_device(self.me ^ bit, self.n_uly), device_id_type=MESH)

    def pass_on(self, d, first, e):
        for level in range(first, self.bits):
            self.copy(d, level, e).start()

    def begin(self):
        for d in range(2):
            self.pass_on(d, 0, 0)

    def take(self, level):
        for d in range(2):
            for e in span(self.orders[d][:level]):
                self.copy(d, level, e).wait_recv()
                self.pass_on(d, level + 1, e | (1 << self.orders[d][level]))

    def finish(self):
        for d in range(2):
            for level in range(self.bits):
                for e in span(self.orders[d][:level]):
                    self.copy(d, level, e).wait_send()


def layer_front_kernel(
    n, bits, n_uly, heads, kv_heads, dim, scale, x_ref, gain_ref, wq_ref, wk_ref, wv_ref, wg_ref, cos_ref, sin_ref,
    qg_ref, kg_ref, a1_ref, q_ref, kv_ref, nq_ref, nk_ref, rq_ref, rk_ref, logit_ref, ag_send, ag_recv, kv_send,
    kv_recv,
):
    seqs, _, cut_count, piece, width = a1_ref.shape
    cuts = [(q, c) for q in range(seqs) for c in range(cut_count)]
    place = plane_place(n_uly)
    tokens = n * piece
    half = kv_heads * dim

    def own(s):
        q, c = cuts[s]
        x = x_ref[q, c * piece:(c + 1) * piece].astype(f32)
        return (x * rms_inverse(x) * gain_ref[...]).astype(bf16)

    line = LineSpread(
        n, len(cuts), own, lambda owner, s: a1_ref.at[cuts[s][0], owner, cuts[s][1]], (ag_send, ag_recv))

    def keys(s):
        q, c = cuts[s]
        return PlaneSpread(
            bits, n_uly,
            lambda at, d: kv_ref.at[q, pl.ds(pl.multiple_of(at * n, n), n), c, :, pl.ds(d * half, half)],
            kv_send.at[s], kv_recv.at[s])

    spreads = [keys(s) for s in range(len(cuts))]

    def turn(s):
        q, c = cuts[s]
        a1 = a1_ref[q, :, c].reshape(tokens, width)
        cosine, sine = cos_ref[:, c].reshape(tokens, dim), sin_ref[:, c].reshape(tokens, dim)

        def tiles(values):
            return values.reshape(n, piece, values.shape[-1])

        def rope(unit, gain):
            scaled = unit * gain
            return scaled * cosine + pltpu.roll(scaled, dim // 2, 1) * sine

        mine = pl.ds(pl.multiple_of(place * n, n), n)
        raw = mm(a1, wk_ref[...])
        for h in range(kv_heads):
            at = slice(h * dim, (h + 1) * dim)
            values = raw[:, at]
            inverse = rms_inverse(values)
            unit = values * inverse
            kv_ref[q, mine, c, :, at] = tiles(rope(unit, kg_ref[...]).astype(bf16))
            nk_ref[q, :, c, :, at] = tiles(unit.astype(bf16))
            rk_ref[q, :, c, :, h:h + 1] = tiles(inverse)
        kv_ref[q, mine, c, :, half:] = tiles(mm(a1, wv_ref[...]).astype(bf16))
        spreads[s].begin()
        raw = mm(a1, wq_ref[...])
        for h in range(heads):
            at = slice(h * dim, (h + 1) * dim)
            values = raw[:, at]
            inverse = rms_inverse(values)
            unit = values * inverse
            q_ref[q, :, c, :, at] = tiles((rope(unit, qg_ref[...]) * (scale * log2e)).astype(bf16))
            nq_ref[q, :, c, :, at] = tiles(unit.astype(bf16))
            rq_ref[q, :, c, :, h:h + 1] = tiles(inverse)
        logit_ref[q, :, c] = tiles(mm(a1, wg_ref[...], NT).astype(bf16).astype(f32))

    line_and_plane_barrier(n, lax.axis_index("tp"), bits, n_uly)
    for step in range(len(cuts) + n - 1 + bits):
        for s in range(len(cuts)):
            stage = step - s
            if 0 <= stage < n:
                line.stages[stage](s)
                if stage == n - 1:
                    turn(s)
        for s in range(len(cuts)):
            level = step - s - n
            if 0 <= level < bits:
                spreads[s].take(level)
    line.drain_spread()
    for spread in spreads:
        spread.finish()


def layer_front(x, attn_norm, w_query, w_key, w_value, w_headgate, tables, query_norm, key_norm, n, sizes, scale,
                collective_id):
    n_ctx, n_uly = sizes
    places = n_ctx * n_uly
    bits = places.bit_length() - 1
    seqs, rows, width = x.shape
    dim = query_norm.shape[0]
    heads, kv_heads = w_query.shape[1] // dim, w_key.shape[1] // dim
    piece = min(32, rows)
    cut_count = rows // piece
    pieces = seqs * cut_count
    vm = pl.BlockSpec(memory_space=pltpu.VMEM)

    def tiled(devices, cols, kind):
        return jax.ShapeDtypeStruct((seqs, devices * n, cut_count, piece, cols), kind)

    shapes = [
        tiled(1, width, bf16), tiled(1, heads * dim, bf16), tiled(places, 2 * kv_heads * dim, bf16),
        tiled(1, heads * dim, bf16), tiled(1, kv_heads * dim, bf16), tiled(1, heads, f32), tiled(1, kv_heads, f32),
        tiled(1, heads, f32),
    ]
    line_sems = [pltpu.SemaphoreType.DMA((2, n - 1, pieces))] * 2
    plane_sems = [pltpu.SemaphoreType.DMA((pieces, 2, places))] * 2
    made = pl.pallas_call(
        functools.partial(layer_front_kernel, n, bits, n_uly, heads, kv_heads, dim, scale),
        in_specs=[vm] * 10,
        out_specs=[vm] * len(shapes),
        out_shape=shapes,
        scratch_shapes=[*line_sems, *plane_sems],
        compiler_params=params(collective_id=collective_id, has_side_effects=True),
        cost_estimate=cost(2 * seqs * n * rows * width * 1024, 200_000_000),
        name="layer_front",
    )(x, attn_norm[None], w_query, w_key, w_value, w_headgate.T,
      *[t.reshape(n, cut_count, piece, dim) for t in tables], query_norm[None], key_norm[None])
    return [m.reshape(seqs, -1, m.shape[-1]) for m in made]


def finish_kernel(count, *refs):
    sources, mid_ref, adds, targets, out_ref = refs[:count], refs[count], refs[count + 1:-count - 1], refs[-count - 1:-1], refs[-1]
    for source, target in zip(sources, targets):
        target[...] = source[...]
    first = 0
    for add_ref in adds:
        last = first + add_ref.shape[0]
        out_ref[first:last] = (mid_ref[first:last] + add_ref[...].astype(f32)).astype(bf16)
        first = last


def finish(sources, middle, adds):
    vm = pl.BlockSpec(memory_space=pltpu.VMEM)
    count = len(sources)
    made = pl.pallas_call(
        functools.partial(finish_kernel, count),
        in_specs=[vm] * (count + 1 + len(adds)),
        out_specs=[vm] * (count + 1),
        out_shape=[jax.ShapeDtypeStruct(s.shape, s.dtype) for s in sources]
        + [jax.ShapeDtypeStruct(middle.shape, bf16)],
        compiler_params=params(),
        cost_estimate=cost(middle.size, 20 * middle.size),
        name="finish",
    )(*sources, middle, *adds)
    return made[:-1], made[-1]


def flatten(values):
    return values.reshape(-1, values.shape[-1])


def spread(values):
    return lax.all_gather(values.astype(bf16), "tp", axis=1, tiled=True)


def collect(values):
    return lax.psum_scatter(values.astype(bf16), "tp", scatter_dimension=1, tiled=True)


def per_device(sizes, inputs, doc_ids, attn_norm, w_query, w_key, w_value, w_headgate, query_norm, key_norm, w_output,
               mlp_norm, w_gate, w_up, w_down, cotangent):
    n_tensor = lax.axis_size("tp")
    n_uly = sizes[1]
    seqs, rows, width = inputs.shape
    group = rows * n_tensor
    dim = query_norm.shape[0]
    heads = w_query.shape[1] // dim
    kv_heads = w_key.shape[1] // dim
    scale = dim ** (-0.5)
    plane = ("ctx", "uly")
    place = lax.axis_index("ctx") * n_uly + lax.axis_index("uly")
    block_start = place * group
    positions = block_start + jnp.arange(group, dtype=jnp.int32)
    tables = lax.optimization_barrier(rope_tables(positions, dim))
    block = min(512, group)

    def wide(values):
        return values.reshape(seqs, group, -1)

    query_doc = lax.dynamic_slice_in_dim(doc_ids, block_start, group, 1)
    start = positions[None, :]
    for d in range(4):
        first_of = jnp.sum(((doc_ids >= 0) & (doc_ids < d)).astype(jnp.int32), axis=1)
        start = jnp.where(query_doc == d, first_of[:, None], start)
    lowest, highest = jnp.min(start, axis=1), jnp.max(start, axis=1)
    hi = jnp.full_like(lowest, (block_start + group + block - 1) // block)
    lo = lowest // block
    full_lo = jnp.clip((highest + block - 1) // block, lo, hi)
    full_hi = jnp.clip(jnp.full_like(lowest, (block_start + 1) // block), full_lo, hi)
    bounds = jnp.stack([lo, full_lo, full_hi, hi], axis=1)

    pad = 128 - heads
    w_first = jnp.concatenate([w_query, w_key, w_value, jnp.pad(w_headgate, ((0, 0), (0, pad)))], axis=1)
    q_cols, kv_cols = heads * dim, kv_heads * dim
    n_main = q_cols + 2 * kv_cols

    if fits_plane(sizes, width):
        first, q, kv, nq, nk, rq, rk, logits = layer_front(
            inputs, attn_norm, w_query, w_key, w_value, w_headgate, tables, query_norm, key_norm, n_tensor, sizes, scale,
            0)
    else:
        xs = inputs.astype(f32)
        inv_one = rms_inverse(xs)
        first = spread(xs * inv_one * attn_norm)
        q, kv, nq, nk, rq, rk, logits = (
            wide(m) for m in project(flatten(first), w_first, tables, query_norm, key_norm, heads, kv_heads, scale))
        kv = plane_gather(kv, sizes, 0)
    near = (seqs + 1) // 2
    early_cot, kv = lax.optimization_barrier((cotangent[:near], kv))
    cots = [spread(early_cot)]
    att, gated, lse = attend(q, kv, bounds, start[:, :, None], positions[:, None], logits, heads, kv_heads, dim, block)

    local = inputs.shape
    part, cots = lax.optimization_barrier((wide(mm(flatten(gated), w_output).astype(bf16)), cots))
    second, middle = line_call(
        norm_forward_kernel, n_tensor, local, part,
        (inputs, mlp_norm[None]), (), 1, "norm_forward")

    if near < seqs:
        late_cot, second = lax.optimization_barrier((cotangent[near:], second))
        cots.append(spread(late_cot))
    a2 = flatten(second)
    gate, up = mm(a2, w_gate), mm(a2, w_up)
    sig = jax.nn.sigmoid(gate)
    silu = gate * sig
    hidden = (silu * up).astype(bf16)
    made, cots = lax.optimization_barrier((wide(mm(hidden, w_down).astype(bf16)), cots))
    cots = [flatten(c) for c in cots]
    d_gate, d_up = hidden_back(cots, w_down, gate, up)
    d_second = second_back(d_gate, d_up, w_gate, w_up)
    d_branch, d_mid, grad_mlp_norm, grad_gate, grad_up, grad_down, d_gated = norm_back(
        wide(d_second), cotangent, middle, mlp_norm, w_output, a2, cots, d_gate, d_up, hidden, n_tensor, sizes, 2)

    made, d_branch = lax.optimization_barrier((made, d_branch))
    outs = [collect(made)]
    d_q, d_logit, d_kv, d_qgain, grad_gate, grad_up, grad_down = attend_back(
        q, kv, d_gated, att, logits, logits.transpose(0, 2, 1), lse, bounds, start[:, None, :], positions[None, :], nq,
        rq, tables, query_norm, (grad_gate, grad_up, grad_down), heads, kv_heads, dim, block, scale)
    d_logit = jnp.pad(d_logit.astype(bf16).transpose(0, 2, 1), ((0, 0), (0, 0), (0, pad)))
    if fits_plane(sizes, width):
        grad_inputs, *grads = layer_back(
            d_kv, flatten(first), flatten(d_branch), d_q, d_logit, nk, rk, tables, key_norm,
            (w_query, w_key, w_value, w_headgate.T), flatten(gated), inputs, attn_norm, d_mid, d_qgain, grad_mlp_norm, n_tensor, sizes, heads, kv_heads, 3)
        (grad_inputs, grad_query, grad_key, grad_value, grad_headgate, grad_output, *gains), outputs = finish(
            (grad_inputs, *grads), middle, outs)
        grad_headgate = grad_headgate.T
        grad_attn_norm, grad_mlp_norm, grad_query_norm, grad_key_norm = (g[0] for g in gains)
    else:
        outputs = (middle + jnp.concatenate(outs, axis=0).astype(f32)).astype(bf16)
        d_kv = blocks_sum(d_kv, sizes, 3)
        d_kv, d_kgain = key_back(d_kv, nk, rk, tables, key_norm, kv_heads, dim)
        d_all = flatten(jnp.concatenate([d_q, d_kv, d_logit], axis=-1))
        d_first = collect(wide(mm(d_all, w_first, NT))).astype(f32)

        grad_first, grad_output = outer_sums(
            (flatten(first), flatten(d_branch)), (0, 1), (d_all, flatten(gated)), sizes, 4)

        share = grad_first.shape[0]
        own_rows = lax.dynamic_slice_in_dim(w_first, place * share, share, 0).astype(f32)
        own_norm = jnp.sum(grad_first * own_rows, axis=1) / lax.dynamic_slice_in_dim(attn_norm, place * share, share, 0)
        grad_attn_norm = lax.dynamic_update_slice_in_dim(jnp.zeros((width,), f32), own_norm, place * share, 0)
        grad_attn_norm, grad_query_norm, grad_key_norm, grad_mlp_norm = lax.psum(
            (grad_attn_norm, d_qgain[0], d_kgain[0], grad_mlp_norm[0]), ("ctx", "uly", "tp"))

        unit = xs * inv_one
        inner = d_first * attn_norm
        grad_inputs = d_mid + inv_one * (inner - unit * jnp.mean(inner * unit, axis=-1, keepdims=True))
        grad_query, grad_key = grad_first[:, :q_cols], grad_first[:, q_cols:q_cols + kv_cols]
        grad_value, grad_headgate = grad_first[:, q_cols + kv_cols:n_main], grad_first[:, n_main:n_main + heads]
        grad_output = grad_output.T
    return (
        outputs,
        grad_inputs,
        grad_attn_norm,
        grad_query,
        grad_key,
        grad_value,
        grad_headgate,
        grad_query_norm,
        grad_key_norm,
        grad_output,
        grad_mlp_norm,
        grad_gate,
        grad_up,
        grad_down,
    )


def solution(mesh):
    tokens = P(None, ("ctx", "uly", "tp"), None)
    column, line, whole = P(None, "tp"), P("tp", None), P()
    rows_split, cols_split = P(("ctx", "uly"), "tp"), P("tp", ("ctx", "uly"))
    return jax.shard_map(
        functools.partial(per_device, (mesh.shape["ctx"], mesh.shape["uly"])),
        mesh=mesh,
        in_specs=(
            tokens, whole, whole, column, column, column, column, whole, whole, line, whole, column, column, line,
            tokens,
        ),
        out_specs=(
            tokens, tokens, whole, rows_split, rows_split, rows_split, rows_split, whole, whole, cols_split, whole,
            rows_split, rows_split, cols_split,
        ),
        check_vma=False,
    )
```
